32 devices in a mesh: row: 8 (over z, x), col: 4 (over y, core).
Axes of the slice: x: 2, y: 2, z: 4, core: 2. Of those that a mesh axis runs over, the one named last changes fastest.
Arguments:
- features: bfloat16 [14336, 2048], P('row', 'col'), may hold values from -6 to 6
- neighbours: int32 [14336, 32], P('row'), may hold values from -1 to 127, as said below
- node_valid: int32 [14336], P('row'), may hold values from 0 to 1, as said below
- weight_one: bfloat16 [2048, 2048], P(None, 'col'), may hold values from -0.125 to 0.125
- gamma_one: float32 [2048], P('col'), may hold values from 0.25 to 1.75
- beta_one: float32 [2048], P('col'), may hold values from -0.5 to 0.5
- weight_two: bfloat16 [2048, 2048], P(None, 'col'), may hold values from -0.125 to 0.125
- gamma_two: float32 [2048], P('col'), may hold values from 0.25 to 1.75
- beta_two: float32 [2048], P('col'), may hold values from -0.5 to 0.5
- cotangent: bfloat16 [14336, 2048], P('row', 'col'), may hold values from -6 to 6
Outputs:
- output: float32 [14336, 2048], P('row', 'col')
- grad_features: float32 [14336, 2048], P('row', 'col')
- grad_weight_one: float32 [2048, 2048], P(None, 'col')
- grad_gamma_one: float32 [2048], P('col')
- grad_beta_one: float32 [2048], P('col')
- grad_weight_two: float32 [2048, 2048], P(None, 'col')
- grad_gamma_two: float32 [2048], P('col')
- grad_beta_two: float32 [2048], P('col')
The draws below stay inside these ranges and needn't reach their ends.
Inputs may be any that keep to these rules, and one draw needn't show every extreme that they name: `neighbours`: entries >= 0 name valid nodes of the same slot; every valid node has 1 to 32 such entries, first in its list, the rest are -1; a padding row has only -1; some slot is full. `node_valid`: in each slot the valid nodes come first and number at least 40.
All inputs are finite; a program needn't handle non-finite values.
Results may differ from the reference program's by a relative error of at most 0.012.
Values may be sent and summed in bfloat16 or wider, within the bound.
No kernel may reach another device: no remote copies, remote signals or barrier semaphores. Data moves between devices by JAX's collectives and lax.ppermute only.
A program may use at most 128 MiB of HBM per device.

```python
import jax
import jax.numpy as jnp
from jax import lax

D = 2048
SLOT = 128
NBR = 32
NODES = 14336


def slot_layout(key):
    slot_total = NODES // SLOT
    base = 40 + 88 * jnp.arange(slot_total, dtype=jnp.int32) // slot_total
    extra = jax.random.randint(jax.random.fold_in(key, 11), (slot_total,), 0, 17)
    filled = jnp.minimum(base + extra, SLOT)
    local = jnp.arange(SLOT, dtype=jnp.int32)
    valid = local[None, :] < filled[:, None]
    degree = jax.random.randint(jax.random.fold_in(key, 12), (slot_total, SLOT), 1, NBR + 1)
    picked = jax.random.randint(jax.random.fold_in(key, 13), (slot_total, SLOT, NBR), 0, filled[:, None, None])
    used = valid[:, :, None] & (jnp.arange(NBR, dtype=jnp.int32)[None, None, :] < degree[:, :, None])
    entries = jnp.where(used, picked, -1).astype(jnp.int32)
    return (entries.reshape(NODES, NBR), valid.astype(jnp.int32).reshape(NODES))


def draw_neighbours(key, part):
    return slot_layout(key)[0]


def draw_node_valid(key, part):
    return slot_layout(key)[1]


def level_of(stream_key, shape, split, least, high):
    def one(dim, parts):
        steps = jax.random.uniform(jax.random.fold_in(jax.random.fold_in(stream_key, 6), dim), (parts,), jnp.float32, least / len(split), high / len(split))
        return jnp.repeat(jnp.exp(steps), shape[dim] // parts).reshape((-1,) + (1,) * (len(shape) - dim - 1))

    loudness = one(*split[0])
    for cut in split[1:]:
        loudness = loudness * one(*cut)
    return loudness


def bell_draw(stream_key, extent, spread, most, cuts=(), kind=jnp.bfloat16):
    loudness = level_of(stream_key, extent, cuts, -0.22, 0.18) if cuts else 1.0
    drawn = jax.random.normal(stream_key, extent, jnp.float32) * spread * loudness
    return jnp.minimum(jnp.maximum(drawn, -most), most).astype(kind)


def setup_inputs(seed: int = 0) -> dict:
    key_of = jax.random.split(jax.random.key(seed), 11)
    features = bell_draw(key_of[0], (NODES, D), 1.0, 6.0, ((0, 8), (1, 4)))
    neighbours = draw_neighbours(jax.random.fold_in(key_of[10], 71), 0)
    node_valid = draw_node_valid(jax.random.fold_in(key_of[10], 71), 0)
    weight_one = bell_draw(key_of[3], (D, D), D ** -0.5, 0.125, ((1, 4),))
    gamma_one = jnp.clip(1.0 + 0.15 * jax.random.normal(key_of[4], (D,), jnp.float32), 0.25, 1.75)
    beta_one = jnp.clip(jax.random.uniform(key_of[5], (D,), jnp.float32, -0.5, 0.5) * level_of(key_of[5], (D,), ((0, 4),), -0.4, 0.0), -0.5, 0.5)
    weight_two = bell_draw(key_of[6], (D, D), D ** -0.5, 0.125, ((1, 4),))
    gamma_two = jnp.clip(1.0 + 0.15 * jax.random.normal(key_of[7], (D,), jnp.float32), 0.25, 1.75)
    beta_two = jnp.clip(jax.random.uniform(key_of[8], (D,), jnp.float32, -0.5, 0.5) * level_of(key_of[8], (D,), ((0, 4),), -0.4, 0.0), -0.5, 0.5)
    cotangent = bell_draw(key_of[9], (NODES, D), 1.0, 6.0, ((0, 8), (1, 4)))
    return dict(features=features, neighbours=neighbours, node_valid=node_valid, weight_one=weight_one, gamma_one=gamma_one, beta_one=beta_one, weight_two=weight_two, gamma_two=gamma_two, beta_two=beta_two, cotangent=cotangent)


@jax.custom_vjp
def low(v):
    return lax.optimization_barrier(v.astype(jnp.bfloat16)).astype(jnp.float32)

@jax.custom_vjp
def low_back(v):
    return v

def low_keep(v):
    return (low(v), None)

def low_pass(kept, grad):
    return (grad,)

def back_keep(v):
    return (v, None)

def back_low(kept, grad):
    return (low(grad),)
low.defvjp(low_keep, low_pass)
low_back.defvjp(back_keep, back_low)
EPSILON = 1e-05

def slot_tiles(neighbours):
    entries_all = neighbours.reshape(-1, SLOT, NBR)

    def build(entries):
        columns = jnp.arange(SLOT, dtype=jnp.int32)
        hits = lax.optimization_barrier(jnp.sum((entries[:, :, None] == columns[None, None, :]).astype(jnp.float32), axis=1))
        degree = lax.optimization_barrier(jnp.sum((entries >= 0).astype(jnp.float32), axis=1))
        joined = hits + jnp.eye(SLOT, dtype=jnp.float32)
        return joined / (degree[:, None] + 1.0)
    return lax.map(build, entries_all)

def aggregate(values, tiles):
    shaped = values.reshape(tiles.shape[0], SLOT, values.shape[1])
    summed = jnp.einsum('sij,sjd->sid', tiles, shaped, precision=lax.Precision.HIGHEST)
    self_weight = jnp.diagonal(tiles, axis1=1, axis2=2)
    return (summed + self_weight[:, :, None] * shaped).reshape(values.shape)

def layer(values, weight, gamma, beta, tiles, valid):
    mixed = low(aggregate(values, tiles))
    linear = low_back(jnp.dot(mixed, weight, precision=lax.Precision.HIGHEST))
    total_valid = jnp.sum(valid)
    mean = lax.optimization_barrier(jnp.sum(valid[:, None] * linear, axis=0)) / total_valid
    centred = linear - mean
    variance = lax.optimization_barrier(jnp.sum(valid[:, None] * centred * centred, axis=0)) / total_valid
    normed = centred * lax.rsqrt(variance + EPSILON)
    return valid[:, None] * jax.nn.silu(gamma * normed + beta)

def reference(features, neighbours, node_valid, weight_one, gamma_one, beta_one, weight_two, gamma_two, beta_two, cotangent):
    tiles = slot_tiles(neighbours)
    valid = node_valid.astype(jnp.float32)
    saved_layer = jax.checkpoint(layer)

    def forward(feat, w_one, g_one, b_one, w_two, g_two, b_two):
        hidden = saved_layer(feat, w_one, g_one, b_one, tiles, valid)
        return saved_layer(hidden, w_two, g_two, b_two, tiles, valid)
    output, pullback = jax.vjp(forward, features.astype(jnp.float32), weight_one.astype(jnp.float32), gamma_one, beta_one, weight_two.astype(jnp.float32), gamma_two, beta_two)
    grads = pullback(cotangent.astype(jnp.float32))
    return (output, grads[0], grads[1], grads[2], grads[3], grads[4], grads[5], grads[6])
```

```python
import functools

import jax
import jax.numpy as jnp
from jax import lax
from jax.experimental import pallas as pl
from jax.experimental.pallas import tpu as pltpu
from jax.sharding import PartitionSpec as P

SLOT = 128
NBR = 32
LANES = 128
EPSILON = 1e-05
BF = jnp.bfloat16
F32 = jnp.float32
ANY = pl.BlockSpec(memory_space=pl.ANY)


def params(limit=48 << 20):
    return pltpu.CompilerParams(dimension_semantics=("arbitrary",), vmem_limit_bytes=limit)


def cost(flops, moved):
    return pl.CostEstimate(flops=int(flops), bytes_accessed=int(moved), transcendentals=0)


def dot(a, b):
    return jnp.dot(a, b, preferred_element_type=F32)


def dot_t(a, b):
    return lax.dot_general(a, b, (((1,), (1,)), ((), ())), preferred_element_type=F32)


def wide(v, columns):
    return jnp.concatenate([v] * (columns // LANES), axis=1)


def sigmoid(v):
    return 0.5 * jnp.tanh(0.5 * v) + 0.5


def tiles_kernel(nbr_ref, valid_ref, h_ref, ht_ref, inv_ref, val_ref):
    entries = nbr_ref[0]
    rows = lax.broadcasted_iota(jnp.int32, (SLOT, SLOT), 0)
    cols = lax.broadcasted_iota(jnp.int32, (SLOT, SLOT), 1)
    hits = jnp.zeros((SLOT, SLOT), F32)
    degree = jnp.zeros((1, SLOT), F32)
    for k in range(entries.shape[0]):
        one = entries[k : k + 1, :]
        hits += (one == rows).astype(F32)
        degree += (one >= 0).astype(F32)
    eye = (rows == cols).astype(F32)
    joined = hits + eye
    counts = joined + joined * eye
    ht_ref[0] = counts.astype(BF)
    h_ref[0] = counts.T.astype(BF)
    inv_ref[0] = jnp.broadcast_to(1.0 / (degree + 1.0), (SLOT, SLOT)).T
    val_ref[0] = jnp.broadcast_to(valid_ref[0].astype(F32), (SLOT, SLOT)).T


def build_tiles(neighbours, node_valid):
    slots = neighbours.shape[0] // SLOT
    turned = neighbours.reshape(slots, SLOT, NBR).transpose(0, 2, 1)
    square = pl.BlockSpec((1, SLOT, SLOT), lambda i: (i, 0, 0))
    return pl.pallas_call(
        tiles_kernel,
        grid=(slots,),
        in_specs=[
            pl.BlockSpec((1, NBR, SLOT), lambda i: (i, 0, 0)),
            pl.BlockSpec((1, 1, SLOT), lambda i: (i, 0, 0)),
        ],
        out_specs=[square] * 4,
        out_shape=[jax.ShapeDtypeStruct((slots, SLOT, SLOT), t) for t in (BF, BF, F32, F32)],
        compiler_params=params(),
        cost_estimate=cost(slots * SLOT * SLOT * NBR * 3, slots * SLOT * SLOT * 12),
        name="tiles",
    )(turned, node_valid.reshape(slots, 1, SLOT))


def combine(gathered):
    mref, first, second, count = (gathered[:, k, :] for k in range(4))
    shift = first / count
    mean_each = mref + shift
    spread_each = second - first * shift
    total = jnp.sum(count, axis=0, keepdims=True)
    mean = jnp.sum(count * mean_each, axis=0, keepdims=True) / total
    away = mean_each - mean
    variance = jnp.sum(spread_each + count * away * away, axis=0, keepdims=True) / total
    return total, mean, lax.rsqrt(variance + EPSILON)


def small_gather(block, axis):
    parts = lax.axis_size(axis)
    copies = jnp.broadcast_to(block[None], (parts,) + block.shape)
    return lax.all_to_all(copies, axis, split_axis=0, concat_axis=0, tiled=True)


def mix(tile_ref, value, step):
    out = []
    for s in range(step):
        part = value[s * SLOT : (s + 1) * SLOT]
        high = part.astype(BF)
        low = (part - high.astype(F32)).astype(BF)
        out.append(dot(tile_ref[s], high) + dot(tile_ref[s], low))
    return out[0] if step == 1 else jnp.concatenate(out, axis=0)


def flat(ref, columns):
    v = ref[...]
    return wide(v.reshape(v.shape[0] * v.shape[1], v.shape[2]), columns)


def forward_kernel(step, first, *refs):
    refs = refs[1:]
    xs, ws = refs[:4], refs[4:8]
    h_ref, inv_ref, val_ref = refs[8:11]
    if first:
        lin_ref, all_ref, st_ref = refs[11:]
    else:
        stin_ref, lin_ref, all_ref, st_ref = refs[11], *refs[14:]
    i = pl.program_id(0)
    columns = lin_ref.shape[1]
    total = None
    for b in range(4):
        x = xs[b][...]
        all_ref[b] = x
        term = dot(x, ws[b][...])
        total = term if total is None else total + term
    lin = mix(h_ref, total, step) * flat(inv_ref, columns)
    lin_ref[...] = lin
    v = flat(val_ref, columns)

    @pl.when(i == 0)
    def _():
        if first:
            st_ref[...] = jnp.zeros_like(st_ref)
            st_ref[0:1, :] = jnp.sum(v * lin, axis=0, keepdims=True) / jnp.sum(v, axis=0, keepdims=True)
        else:
            st_ref[...] = stin_ref[...]

    away = (lin - st_ref[0:1, :]) * v
    st_ref[1:2, :] += jnp.sum(away, axis=0, keepdims=True)
    st_ref[2:3, :] += jnp.sum(away * away, axis=0, keepdims=True)
    st_ref[3:4, :] += jnp.sum(v, axis=0, keepdims=True)


def forward_chunk(ids, plan, k, blocks, weight, tiles, carried):
    step, starts, sizes = plan
    base, steps = starts[k], sizes[k]
    rows = step * SLOT
    h, _, inv, val = tiles
    nodes, columns = h.shape[0] * SLOT, weight.shape[1]
    depth = weight.shape[0] // 4
    first = carried is None

    def block_spec(x):
        off = base if x.shape[0] == nodes else 0
        return pl.BlockSpec((rows, depth), lambda i, ids: (i + off, 0))

    tile = pl.BlockSpec((step, SLOT, SLOT), lambda i, ids: (i + base, 0, 0))
    ins = [block_spec(x) for x in blocks]
    ins += [pl.BlockSpec((depth, columns), lambda i, ids, b=b: (ids[b], 0)) for b in range(4)]
    ins += [tile] * 3
    args = [*blocks, *[weight] * 4, h, inv, val]
    aliases = {}
    small = pl.BlockSpec((8, columns), lambda i, ids: (0, 0))
    if not first:
        lin, everything, stats = carried
        ins += [small, ANY, ANY]
        args += [stats, lin, everything]
        aliases = {13: 0, 14: 1}
    return pl.pallas_call(
        functools.partial(forward_kernel, step, first),
        grid_spec=pltpu.PrefetchScalarGridSpec(
            num_scalar_prefetch=1,
            grid=(steps,),
            in_specs=ins,
            out_specs=[
                pl.BlockSpec((rows, columns), lambda i, ids: (i + base, 0)),
                pl.BlockSpec((4, rows, depth), lambda i, ids: (0, i + base, 0)),
                small,
            ],
        ),
        out_shape=[
            jax.ShapeDtypeStruct((nodes, columns), F32),
            jax.ShapeDtypeStruct((4, nodes, depth), BF),
            jax.ShapeDtypeStruct((8, columns), F32),
        ],
        input_output_aliases=aliases,
        compiler_params=params(),
        cost_estimate=cost(2 * steps * rows * 4 * depth * columns, steps * rows * (8 * depth + 4 * columns) + 8 * depth * columns),
        name=f"forward_{k}",
    )(ids, *args)


def coefficients(g_ref, gamma_ref, beta_ref):
    total, mean, inv_std = combine(g_ref[...])
    return total, mean, inv_std, gamma_ref[...], beta_ref[...]


def hidden_kernel(lin_ref, val_ref, g_ref, gamma_ref, beta_ref, out_ref):
    _, mean, inv_std, gamma, beta = coefficients(g_ref, gamma_ref, beta_ref)
    before = gamma * ((lin_ref[...] - mean) * inv_std) + beta
    out_ref[...] = (flat(val_ref, lin_ref.shape[1]) * (before * sigmoid(before))).astype(out_ref.dtype)


def slope_of(lin, mean, inv_std, gamma, beta):
    normed = (lin - mean) * inv_std
    before = gamma * normed + beta
    sig = sigmoid(before)
    return normed, sig * (1.0 + before * (1.0 - sig))


def sums_kernel(lin_ref, cot_ref, val_ref, g_ref, gamma_ref, beta_ref, st_ref):
    _, mean, inv_std, gamma, beta = coefficients(g_ref, gamma_ref, beta_ref)
    normed, slope = slope_of(lin_ref[...], mean, inv_std, gamma, beta)
    grad = cot_ref[...].astype(F32) * flat(val_ref, lin_ref.shape[1]) * slope

    @pl.when(pl.program_id(0) == 0)
    def _():
        st_ref[...] = jnp.zeros_like(st_ref)

    st_ref[0:1, :] += jnp.sum(grad, axis=0, keepdims=True)
    st_ref[1:2, :] += jnp.sum(grad * normed, axis=0, keepdims=True)


def turn_kernel(step, from_cot, lin_ref, grad_ref, val_ref, inv_ref, ht_ref, g_ref, sg_ref, gamma_ref, beta_ref, out_ref):
    total, mean, inv_std, gamma, beta = coefficients(g_ref, gamma_ref, beta_ref)
    sg = sg_ref[...]
    grad_beta = jnp.sum(sg[:, 0, :], axis=0, keepdims=True)
    grad_gamma = jnp.sum(sg[:, 1, :], axis=0, keepdims=True)
    columns = lin_ref.shape[1]
    v = flat(val_ref, columns)
    if from_cot:
        normed, slope = slope_of(lin_ref[...], mean, inv_std, gamma, beta)
        grad = grad_ref[...].astype(F32) * v * slope
    else:
        normed = (lin_ref[...] - mean) * inv_std
        grad = grad_ref[...]
    scale = inv_std * gamma
    lin_grad = scale * (grad - v * ((grad_beta + normed * grad_gamma) / total))
    out_ref[...] = mix(ht_ref, lin_grad * flat(inv_ref, columns), step).astype(BF)


def rows_call(kernel, plan, k, big, tiles, smalls, out_dtype, out_full, name, ops, extra=()):
    step, starts, sizes = plan
    base, steps = (0, sum(sizes)) if k is None else (starts[k], sizes[k])
    rows = step * SLOT
    nodes, columns = big[0].shape
    ins = [pl.BlockSpec((rows, columns), lambda i: (i + base, 0)) for _ in big]
    ins += [pl.BlockSpec((step, SLOT, SLOT), lambda i: (i + base, 0, 0)) for _ in tiles]
    ins += [pl.BlockSpec(s.shape, lambda i, n=s.ndim: (0,) * n) for s in smalls]
    if out_dtype is None:
        out_spec = pl.BlockSpec((8, columns), lambda i: (0, 0))
        out_shape = jax.ShapeDtypeStruct((8, columns), F32)
    else:
        out_spec = pl.BlockSpec((rows, columns), lambda i: (i, 0))
        out_shape = jax.ShapeDtypeStruct((steps * rows, columns), out_dtype)
    return pl.pallas_call(
        kernel,
        grid=(steps,),
        in_specs=ins,
        out_specs=out_spec,
        out_shape=out_shape,
        compiler_params=params(),
        cost_estimate=cost(ops * steps * rows * columns, 8 * steps * rows * columns),
        name=name,
    )(*big, *tiles, *smalls)


def backward_kernel(layer_one, first, *refs):
    refs = refs[1:]
    xs, ws = refs[:4], refs[4:8]
    total = None
    for b in range(4):
        term = dot_t(xs[b][...], ws[b][...])
        total = term if total is None else total + term
    if layer_one:
        refs[-1][...] = total
        return
    lin_ref, val_ref, g_ref, gamma_ref, beta_ref = refs[8:13]
    out_ref, st_ref = refs[-2:]
    _, mean, inv_std, gamma, beta = coefficients(g_ref, gamma_ref, beta_ref)
    normed, slope = slope_of(lin_ref[...], mean, inv_std, gamma, beta)
    grad = total * flat(val_ref, lin_ref.shape[1]) * slope
    out_ref[...] = grad

    @pl.when(pl.program_id(0) == 0)
    def _():
        st_ref[...] = jnp.zeros_like(st_ref) if first else refs[13][...]

    st_ref[0:1, :] += jnp.sum(grad, axis=0, keepdims=True)
    st_ref[1:2, :] += jnp.sum(grad * normed, axis=0, keepdims=True)


def backward_chunk(ids, plan, k, blocks, pieces, norm, carried):
    step, starts, sizes = plan
    base, steps = starts[k], sizes[k]
    rows = step * SLOT
    nodes = sum(sizes) * rows
    depth = blocks[0].shape[1]
    columns = depth
    layer_one = norm is None
    first = carried is None
    ins = [pl.BlockSpec((rows, depth), lambda i, ids: (i, 0)) for _ in blocks]
    where = (lambda i, ids: (ids[0], 0), lambda i, ids: (0, 0), lambda i, ids: (ids[4], 0), lambda i, ids: (0, 0))
    ins += [pl.BlockSpec((depth, columns), w) for w in where]
    args = [*blocks, *pieces]
    out_specs = [pl.BlockSpec((rows, columns), lambda i, ids: (i + base, 0))]
    out_shape = [jax.ShapeDtypeStruct((nodes, columns), F32)]
    small = pl.BlockSpec((8, columns), lambda i, ids: (0, 0))
    if not layer_one:
        lin, val, g, gamma, beta = norm
        ins += [
            pl.BlockSpec((rows, columns), lambda i, ids: (i + base, 0)),
            pl.BlockSpec((step, SLOT, SLOT), lambda i, ids: (i + base, 0, 0)),
            pl.BlockSpec(g.shape, lambda i, ids: (0, 0, 0)),
            pl.BlockSpec(gamma.shape, lambda i, ids: (0, 0)),
            pl.BlockSpec(beta.shape, lambda i, ids: (0, 0)),
        ]
        args += [lin, val, g, gamma, beta]
        out_specs.append(small)
        out_shape.append(jax.ShapeDtypeStruct((8, columns), F32))
    aliases = {}
    if not first:
        if not layer_one:
            ins.append(small)
            args.append(carried[1])
        ins.append(ANY)
        args.append(carried[0])
        aliases = {len(args): 0}
    return pl.pallas_call(
        functools.partial(backward_kernel, layer_one, first),
        grid_spec=pltpu.PrefetchScalarGridSpec(
            num_scalar_prefetch=1, grid=(steps,), in_specs=ins, out_specs=out_specs
        ),
        out_shape=out_shape,
        input_output_aliases=aliases,
        compiler_params=params(),
        cost_estimate=cost(2 * steps * rows * 4 * depth * columns, steps * rows * (8 * depth + 4 * columns) + 8 * depth * columns),
        name=f"backward_{1 if layer_one else 2}_{k}",
    )(ids, *args)


def weight_kernel(spans, ids_ref, x_ref, *refs):
    hs, out_ref = refs[:-1], refs[-1]
    total = None
    for (low, high), h_ref in zip(spans, hs):
        term = lax.dot_general(
            x_ref[0, low:high, :], h_ref[...], (((0,), (0,)), ((), ())), preferred_element_type=F32
        )
        total = term if total is None else total + term
    out_ref[...] = total.astype(out_ref.dtype)


def weight_terms(ids, everything, hs):
    _, nodes, depth = everything.shape
    columns = hs[0].shape[1]
    spans, low = [], 0
    for h in hs:
        spans.append((low, low + h.shape[0]))
        low += h.shape[0]
    return pl.pallas_call(
        functools.partial(weight_kernel, tuple(spans)),
        grid_spec=pltpu.PrefetchScalarGridSpec(
            num_scalar_prefetch=1,
            grid=(4,),
            in_specs=[pl.BlockSpec((1, nodes, depth), lambda i, ids: (i, 0, 0))]
            + [pl.BlockSpec(h.shape, lambda i, ids: (0, 0)) for h in hs],
            out_specs=pl.BlockSpec((depth, columns), lambda i, ids: (ids[i], 0)),
        ),
        out_shape=jax.ShapeDtypeStruct((4 * depth, columns), BF),
        compiler_params=params(),
        cost_estimate=cost(8 * nodes * depth * columns, 10 * nodes * depth + 8 * depth * columns),
        name="weight_terms",
    )(ids, everything, *hs)


def across(value, axis, distance):
    size = lax.axis_size(axis)
    return lax.ppermute(value, axis, [(i, i ^ distance) for i in range(size)])


def gather_chunks(chunks):
    far = [across(c, "col", 2) for c in chunks]
    near = [across(c, "col", 1) for c in chunks]
    beyond = [across(c, "col", 1) for c in far]
    return [list(blocks) for blocks in zip(chunks, near, far, beyond)]


def weight_rows(weight, q):
    depth = weight.shape[0] // 4
    low, high = q % 2, q // 2
    sent = lax.dynamic_slice_in_dim(weight, (1 - high) * 2 * depth, 2 * depth, 0)
    got = across(sent, "col", 2)
    near = across(lax.dynamic_slice_in_dim(weight, (q ^ 1) * depth, depth, 0), "col", 1)
    beyond = across(lax.dynamic_slice_in_dim(got, (1 - low) * depth, depth, 0), "col", 1)
    return [weight, near, got, beyond]


def reduce_rows(value, axis):
    size = lax.axis_size(axis)
    bits = size.bit_length() - 1
    place = lax.axis_index(axis)
    orders = [list(range(bits)), list(range(1, bits)) + [0]]
    held = list(jnp.split(value, 2, axis=0))
    for s in range(bits):
        for n, order in enumerate(orders):
            bit = (place >> order[s]) & 1
            half = held[n].shape[0] // 2
            keep = lax.dynamic_slice_in_dim(held[n], bit * half, half, 0)
            send = lax.dynamic_slice_in_dim(held[n], (1 - bit) * half, half, 0)
            got = across(send, axis, 1 << order[s])
            held[n] = (keep.astype(F32) + got.astype(F32)).astype(value.dtype)
    for s in reversed(range(bits)):
        for n, order in enumerate(orders):
            bit = (place >> order[s]) & 1
            got = across(held[n], axis, 1 << order[s])
            held[n] = jnp.concatenate(
                [jnp.where(bit == 0, held[n], got), jnp.where(bit == 0, got, held[n])], axis=0
            )
    return jnp.concatenate(held, axis=0).astype(F32)


def chunk_plan(slots):
    step = 2 if slots % 2 == 0 else 1
    total = slots // step
    sizes = []
    while total > 0:
        sizes.append(min(2, total))
        total -= sizes[-1]
    starts = [sum(sizes[:k]) for k in range(len(sizes))]
    return step, starts, sizes


def local(
    features,
    neighbours,
    node_valid,
    weight_one,
    gamma_one,
    beta_one,
    weight_two,
    gamma_two,
    beta_two,
    cotangent,
):
    nodes, columns = features.shape
    plan = chunk_plan(nodes // SLOT)
    step, starts, sizes = plan
    count = len(sizes)
    q = lax.axis_index("col")
    ids = jnp.stack([q, q ^ 1, q ^ 2, q ^ 3, q % 2]).astype(jnp.int32)
    g1, b1, g2, b2 = (v.reshape(1, columns) for v in (gamma_one, beta_one, gamma_two, beta_two))

    rows = [(starts[k] * step * SLOT, (starts[k] + sizes[k]) * step * SLOT) for k in range(count)]
    far = [across(features[a:b], "col", 2) for a, b in rows]
    near = across(features, "col", 1)
    beyond = [across(c, "col", 1) for c in far]
    tiles = build_tiles(neighbours, node_valid)
    _, ht, inv, val = tiles

    carried = None
    for k in range(count):
        carried = forward_chunk(ids, plan, k, [features, near, far[k], beyond[k]], weight_one, tiles, carried)
    lin_one, all_one, stats = carried
    norm_one = small_gather(stats, "row")
    rows_two = weight_rows(weight_two, q)

    hidden = [
        rows_call(hidden_kernel, plan, k, [lin_one], [val], [norm_one, g1, b1], BF, False, f"hidden_{k}", 12)
        for k in range(count)
    ]
    gathered = gather_chunks(hidden)
    carried = None
    for k in range(count):
        carried = forward_chunk(ids, plan, k, gathered[k], weight_two, tiles, carried)
    lin_two, all_two, stats = carried
    norm_two = small_gather(stats, "row")
    rows_one = weight_rows(weight_one, q)

    sums = rows_call(
        sums_kernel, plan, None, [lin_two, cotangent], [val], [norm_two, g2, b2], None, False, "sums_two", 20
    )
    grads_two = small_gather(sums, "row")
    turned = [
        rows_call(
            functools.partial(turn_kernel, step, True),
            plan, k, [lin_two, cotangent], [val, inv, ht], [norm_two, grads_two, g2, b2], BF, False, f"turn_two_{k}", 500,
        )
        for k in range(count)
    ]
    gathered = gather_chunks(turned)
    output = rows_call(hidden_kernel, plan, None, [lin_two], [val], [norm_two, g2, b2], F32, False, "output", 12)
    terms_two = weight_terms(ids, all_two, turned)
    grad_weight_two = lax.psum(terms_two, "row").astype(F32)

    carried = None
    for k in range(count):
        carried = backward_chunk(ids, plan, k, gathered[k], rows_two, (lin_one, val, norm_one, g1, b1), carried)
    grad_one, sums = carried
    grads_one = small_gather(sums, "row")
    turned = [
        rows_call(
            functools.partial(turn_kernel, step, False),
            plan, k, [lin_one, grad_one], [val, inv, ht], [norm_one, grads_one, g1, b1], BF, False, f"turn_one_{k}", 500,
        )
        for k in range(count)
    ]
    gathered = gather_chunks(turned)
    terms_one = weight_terms(ids, all_one, turned)
    grad_weight_one = reduce_rows(terms_one, "row")
    carried = None
    for k in range(count):
        carried = backward_chunk(ids, plan, k, gathered[k], rows_one, None, carried)
    (grad_features,) = carried

    sums_one, sums_two = jnp.sum(grads_one, axis=0), jnp.sum(grads_two, axis=0)
    return (
        output,
        grad_features,
        grad_weight_one,
        sums_one[1],
        sums_one[0],
        grad_weight_two,
        sums_two[1],
        sums_two[0],
    )


def solution(mesh):
    placed = (
        P("row", "col"),
        P("row", None),
        P("row"),
        P(None, "col"),
        P("col"),
        P("col"),
        P(None, "col"),
        P("col"),
        P("col"),
        P("row", "col"),
    )
    return jax.shard_map(
        local,
        mesh=mesh,
        in_specs=placed,
        out_specs=(
            P("row", "col"),
            P("row", "col"),
            P(None, "col"),
            P("col"),
            P("col"),
            P(None, "col"),
            P("col"),
            P("col"),
        ),
        check_vma=False,
    )
```

```python
import functools

import jax
import jax.numpy as jnp
from jax import lax
from jax.experimental import pallas as pl
from jax.experimental.pallas import tpu as pltpu
from jax.sharding import PartitionSpec as P

SLOT = 128
NBR = 32
LANES = 128
EPSILON = 1e-05
ANY = pl.BlockSpec(memory_space=pl.ANY)
BF = jnp.bfloat16
F32 = jnp.float32


def params(limit=48 << 20):
    return pltpu.CompilerParams(dimension_semantics=("arbitrary",), vmem_limit_bytes=limit)


def cost(flops, moved):
    return pl.CostEstimate(flops=int(flops) // 1000, bytes_accessed=int(moved) // 1000, transcendentals=0)


def dot(a, b):
    return jnp.dot(a, b, preferred_element_type=F32)


def dot_t(a, b):
    return lax.dot_general(a, b, (((1,), (1,)), ((), ())), preferred_element_type=F32)


def wide(v, columns):
    return jnp.concatenate([v] * (columns // LANES), axis=1)


def tiles_kernel(nbr_ref, valid_ref, h_ref, ht_ref, inv_ref, val_ref):
    entries = nbr_ref[0]
    rows = lax.broadcasted_iota(jnp.int32, (SLOT, SLOT), 0)
    cols = lax.broadcasted_iota(jnp.int32, (SLOT, SLOT), 1)
    hits = jnp.zeros((SLOT, SLOT), F32)
    degree = jnp.zeros((1, SLOT), F32)
    for k in range(entries.shape[0]):
        one = entries[k : k + 1, :]
        hits += (one == rows).astype(F32)
        degree += (one >= 0).astype(F32)
    eye = (rows == cols).astype(F32)
    joined = hits + eye
    counts = joined + joined * eye
    ht_ref[0] = wide(counts.astype(BF), 2 * SLOT)
    h_ref[0] = wide(counts.T.astype(BF), 2 * SLOT)
    inv_ref[0] = jnp.broadcast_to(1.0 / (degree + 1.0), (SLOT, SLOT)).T
    val_ref[0] = jnp.broadcast_to(valid_ref[0].astype(F32), (SLOT, SLOT)).T


def build_tiles(neighbours, node_valid):
    slots = neighbours.shape[0] // SLOT
    turned = neighbours.reshape(slots, SLOT, NBR).transpose(0, 2, 1)
    square = pl.BlockSpec((1, SLOT, SLOT), lambda i: (i, 0, 0))
    double = pl.BlockSpec((1, SLOT, 2 * SLOT), lambda i: (i, 0, 0))
    return pl.pallas_call(
        tiles_kernel,
        grid=(slots,),
        in_specs=[
            pl.BlockSpec((1, NBR, SLOT), lambda i: (i, 0, 0)),
            pl.BlockSpec((1, 1, SLOT), lambda i: (i, 0, 0)),
        ],
        out_specs=[double, double, square, square],
        out_shape=[jax.ShapeDtypeStruct((slots, SLOT, 2 * SLOT), BF)] * 2
        + [jax.ShapeDtypeStruct((slots, SLOT, SLOT), F32)] * 2,
        compiler_params=params(),
        cost_estimate=cost(slots * SLOT * SLOT * NBR * 3, slots * SLOT * SLOT * 12),
        name="tiles",
    )(turned, node_valid.reshape(slots, 1, SLOT))


def combine(g_ref):
    mref, first, second, count = (g_ref[:, k, :] for k in range(4))
    shift = first / count
    mean_each = mref + shift
    spread_each = second - first * shift
    total = jnp.sum(count, axis=0, keepdims=True)
    mean = jnp.sum(count * mean_each, axis=0, keepdims=True) / total
    away = mean_each - mean
    variance = jnp.sum(spread_each + count * away * away, axis=0, keepdims=True) / total
    return total, mean, lax.rsqrt(variance + EPSILON)


def small_gather(block, axis):
    parts = lax.axis_size(axis)
    copies = jnp.broadcast_to(block[None], (parts,) + block.shape)
    return lax.all_to_all(copies, axis, split_axis=0, concat_axis=0, tiled=True)


def split(value):
    high = value.astype(BF)
    return high, (value - high.astype(F32)).astype(BF)


def fold(value):
    return jnp.sum(value.reshape(value.shape[0] // 8, 8, value.shape[1]), axis=0)


def at(ref, k):
    return ref[k : k + 1, :]


def put(ref, k, value):
    ref[k : k + 1, :] = value


def forward_kernel(step, first, *refs):
    refs = refs[1:]
    xs, ws, (h_ref, inv_ref, val_ref) = refs[:4], refs[4:8], refs[8:11]
    lin_ref, all_ref, st_ref, acc_ref = refs[-4:]
    i = pl.program_id(0)
    columns = lin_ref.shape[1]
    total = None
    for b in range(4):
        x = xs[b][...]
        all_ref[b] = x
        term = dot(x, ws[b][...])
        total = term if total is None else total + term
    high, low = split(total)
    for s in range(step):
        rows = slice(s * SLOT, (s + 1) * SLOT)
        both = jnp.concatenate([high[rows], low[rows]], axis=0)
        lin_ref[rows, :] = dot(h_ref[s], both) * wide(inv_ref[s], columns)

    @pl.when(i == 0)
    def _():
        acc_ref[...] = jnp.zeros_like(acc_ref)
        if first:
            v = jnp.concatenate([val_ref[s] for s in range(step)], axis=0)
            count = jnp.sum(v, axis=0, keepdims=True)
            st_ref[...] = jnp.zeros_like(st_ref)
            put(st_ref, 0, jnp.sum(lin_ref[...] * wide(v, columns), axis=0, keepdims=True) / wide(count, columns))
        else:
            st_ref[...] = refs[11][...]

    mref = at(st_ref, 0)
    for s, inner, rows in parts_of(step):
        v = val_ref[s, inner, :]
        away = (lin_ref[rows, :] - mref) * wide(v, columns)
        acc_ref[0] += fold(away)
        acc_ref[1] += fold(away * away)
        acc_ref[2, :, :LANES] += fold(v)

    @pl.when(i == pl.num_programs(0) - 1)
    def _():
        st_ref[1:2, :] += jnp.sum(acc_ref[0], axis=0, keepdims=True)
        st_ref[2:3, :] += jnp.sum(acc_ref[1], axis=0, keepdims=True)
        st_ref[3:4, :] += wide(jnp.sum(acc_ref[2, :, :LANES], axis=0, keepdims=True), columns)


def forward_chunk(ids, plan, k, blocks, weight, tiles, carried, name):
    step, starts, sizes = plan
    base, steps = starts[k], sizes[k]
    rows = step * SLOT
    h, _, inv, val = tiles
    nodes, columns = h.shape[0] * SLOT, weight.shape[1]
    depth = weight.shape[0] // 4
    first = carried is None

    def rows_of(x):
        off = base if x.shape[0] == nodes else 0
        return pl.BlockSpec((rows, depth), lambda i, ids: (i + off, 0))

    tile = pl.BlockSpec((step, SLOT, SLOT), lambda i, ids: (i + base, 0, 0))
    double = pl.BlockSpec((step, SLOT, 2 * SLOT), lambda i, ids: (i + base, 0, 0))
    small = pl.BlockSpec((8, columns), lambda i, ids: (0, 0))
    ins = [rows_of(x) for x in blocks]
    ins += [pl.BlockSpec((depth, columns), lambda i, ids, b=b: (ids[b], 0)) for b in range(4)]
    ins += [double, tile, tile]
    args = [*blocks, *[weight] * 4, h, inv, val]
    aliases = {}
    if not first:
        lin, everything, stats = carried
        ins += [small, ANY, ANY]
        args += [stats, lin, everything]
        aliases = {13: 0, 14: 1}
    return pl.pallas_call(
        functools.partial(forward_kernel, step, first),
        grid_spec=pltpu.PrefetchScalarGridSpec(
            num_scalar_prefetch=1,
            grid=(steps,),
            in_specs=ins,
            out_specs=[
                pl.BlockSpec((rows, columns), lambda i, ids: (i + base, 0)),
                pl.BlockSpec((4, rows, depth), lambda i, ids: (0, i + base, 0)),
                small,
            ],
            scratch_shapes=[pltpu.VMEM((3, 8, columns), F32)],
        ),
        out_shape=[
            jax.ShapeDtypeStruct((nodes, columns), F32),
            jax.ShapeDtypeStruct((4, nodes, depth), BF),
            jax.ShapeDtypeStruct((8, columns), F32),
        ],
        input_output_aliases=aliases,
        compiler_params=params(),
        cost_estimate=cost(32 * steps * rows * depth * columns, steps * rows * 40 * depth),
        name=name,
    )(ids, *args)


def columns_of(g_ref, gamma_ref, beta_ref, co_ref):
    total, mean, inv_std = combine(g_ref)
    put(co_ref, 0, mean)
    put(co_ref, 1, 0.5 * gamma_ref[...] * inv_std)
    put(co_ref, 2, 0.5 * beta_ref[...])
    put(co_ref, 3, inv_std)
    put(co_ref, 4, total)


def silu_of(away, co_ref):
    u = away * at(co_ref, 1) + at(co_ref, 2)
    return u + u * jnp.tanh(u)


def double_slope(away, co_ref):
    u = away * at(co_ref, 1) + at(co_ref, 2)
    t = jnp.tanh(u)
    return (1.0 + t) * (1.0 + u * (1.0 - t))


def parts_of(step, part=32):
    for s in range(step):
        for r in range(SLOT // part):
            yield s, slice(r * part, (r + 1) * part), slice(s * SLOT + r * part, s * SLOT + (r + 1) * part)


def result_kernel(step, lin_ref, val_ref, g_ref, gamma_ref, beta_ref, out_ref, co_ref):
    @pl.when(pl.program_id(0) == 0)
    def _():
        columns_of(g_ref, gamma_ref, beta_ref, co_ref)

    columns = lin_ref.shape[1]
    for s, inner, rows in parts_of(step):
        value = silu_of(lin_ref[rows, :] - at(co_ref, 0), co_ref)
        out_ref[rows, :] = (wide(val_ref[s, inner, :], columns) * value).astype(out_ref.dtype)


def sums_kernel(step, lin_ref, cot_ref, val_ref, g_ref, gamma_ref, beta_ref, st_ref, co_ref, acc_ref):
    i = pl.program_id(0)

    @pl.when(i == 0)
    def _():
        columns_of(g_ref, gamma_ref, beta_ref, co_ref)
        acc_ref[...] = jnp.zeros_like(acc_ref)

    columns = lin_ref.shape[1]
    for s, inner, rows in parts_of(step):
        away = lin_ref[rows, :] - at(co_ref, 0)
        grad = cot_ref[rows, :].astype(F32) * wide(val_ref[s, inner, :], columns) * double_slope(away, co_ref)
        acc_ref[0] += fold(grad)
        acc_ref[1] += fold(grad * away)

    finish_sums(st_ref, co_ref, acc_ref)


def finish_sums(st_ref, co_ref, acc_ref, before_ref=None):
    @pl.when(pl.program_id(0) == pl.num_programs(0) - 1)
    def _():
        st_ref[...] = jnp.zeros_like(st_ref) if before_ref is None else before_ref[...]
        st_ref[0:1, :] += 0.5 * jnp.sum(acc_ref[0], axis=0, keepdims=True)
        st_ref[1:2, :] += 0.5 * at(co_ref, 3) * jnp.sum(acc_ref[1], axis=0, keepdims=True)


def turn_kernel(step, from_cot, lin_ref, grad_ref, val_ref, inv_ref, ht_ref, g_ref, sg_ref, gamma_ref, beta_ref, out_ref, co_ref, lg_ref):
    @pl.when(pl.program_id(0) == 0)
    def _():
        columns_of(g_ref, gamma_ref, beta_ref, co_ref)
        sg = sg_ref[...]
        twice = 2.0 / at(co_ref, 4)
        put(co_ref, 5, twice * jnp.sum(sg[:, 0, :], axis=0, keepdims=True))
        put(co_ref, 6, twice * at(co_ref, 3) * jnp.sum(sg[:, 1, :], axis=0, keepdims=True))

    columns = lin_ref.shape[1]
    for s, inner, rows in parts_of(step):
        away = lin_ref[rows, :] - at(co_ref, 0)
        if from_cot:
            grad = grad_ref[rows, :].astype(F32) * double_slope(away, co_ref)
        else:
            grad = grad_ref[rows, :]
        weight = wide(val_ref[s, inner, :] * inv_ref[s, inner, :], columns)
        high, low = split(weight * (grad - (at(co_ref, 5) + away * at(co_ref, 6))))
        lg_ref[s, inner, :] = high
        lg_ref[s, slice(inner.start + SLOT, inner.stop + SLOT), :] = low
    for s in range(step):
        out_ref[s * SLOT : (s + 1) * SLOT, :] = (dot(ht_ref[s], lg_ref[s]) * at(co_ref, 1)).astype(BF)


def rows_call(kernel, plan, k, big, tiles, smalls, out_dtype, scratch, name, ops):
    step, starts, sizes = plan
    base, steps = (0, sum(sizes)) if k is None else (starts[k], sizes[k])
    rows = step * SLOT
    columns = big[0].shape[1]
    ins = [pl.BlockSpec((rows, columns), lambda i: (i + base, 0)) for _ in big]
    ins += [pl.BlockSpec((step,) + t.shape[1:], lambda i: (i + base, 0, 0)) for t in tiles]
    ins += [pl.BlockSpec(s.shape, lambda i, n=s.ndim: (0,) * n) for s in smalls]
    if out_dtype is None:
        out_spec = pl.BlockSpec((8, columns), lambda i: (0, 0))
        out_shape = jax.ShapeDtypeStruct((8, columns), F32)
    else:
        out_spec = pl.BlockSpec((rows, columns), lambda i: (i, 0))
        out_shape = jax.ShapeDtypeStruct((steps * rows, columns), out_dtype)
    return pl.pallas_call(
        functools.partial(kernel, step),
        grid=(steps,),
        in_specs=ins,
        out_specs=out_spec,
        out_shape=out_shape,
        scratch_shapes=[pltpu.VMEM((8, columns), F32)] + scratch,
        compiler_params=params(),
        cost_estimate=cost(ops * steps * rows * columns, 8 * steps * rows * columns),
        name=name,
    )(*big, *tiles, *smalls)


def result_call(plan, k, lin, val, norm, dtype, name):
    return rows_call(result_kernel, plan, k, [lin], [val], norm, dtype, [], name, 12)


def turn_call(from_cot, plan, k, lin, grad, tiles, norm, sums, name):
    _, ht, inv, val = tiles
    columns = lin.shape[1]

    def kernel(step, *refs):
        return turn_kernel(step, from_cot, *refs)

    return rows_call(
        kernel, plan, k, [lin, grad], [val, inv, ht], [norm[0], sums, *norm[1:]], BF,
        [pltpu.VMEM((plan[0], 2 * SLOT, columns), BF)], name, 500,
    )


def backward_kernel(step, last, first, *refs):
    xs, ws, refs = refs[:4], refs[4:8], refs[8:]
    total = dot_t(xs[0][...], ws[0][...])
    for b in range(1, 4):
        total += dot_t(xs[b][...], ws[b][...])
    if last:
        refs[-1][...] = total
        return
    lin_ref, g_ref, gamma_ref, beta_ref = refs[:4]
    out_ref, st_ref, co_ref, acc_ref = refs[-4:]

    @pl.when(pl.program_id(0) == 0)
    def _():
        columns_of(g_ref, gamma_ref, beta_ref, co_ref)
        acc_ref[...] = jnp.zeros_like(acc_ref)

    for _, _, rows in parts_of(step):
        away = lin_ref[rows, :] - at(co_ref, 0)
        grad = total[rows] * double_slope(away, co_ref)
        out_ref[rows, :] = grad
        acc_ref[0] += fold(grad)
        acc_ref[1] += fold(grad * away)

    finish_sums(st_ref, co_ref, acc_ref, None if first else refs[4])


def backward_chunk(plan, k, blocks, pieces, lin, norm, carried, name):
    step, starts, sizes = plan
    base, steps = starts[k], sizes[k]
    rows = step * SLOT
    nodes = sum(sizes) * rows
    depth, columns = blocks[0].shape[1], pieces[0].shape[0]
    last, first = norm is None, carried is None
    flat = pl.BlockSpec((rows, columns), lambda i: (i + base, 0))
    fixed = lambda s: pl.BlockSpec(s.shape, lambda i, n=s.ndim: (0,) * n)
    ins = [pl.BlockSpec((rows, depth), lambda i: (i, 0)) for _ in blocks]
    ins += map(fixed, pieces)
    args = [*blocks, *pieces]
    out_specs = [flat]
    out_shape = [jax.ShapeDtypeStruct((nodes, columns), F32)]
    scratch = []
    small = pl.BlockSpec((8, columns), lambda i: (0, 0))
    if not last:
        ins += [flat, *map(fixed, norm)]
        args += [lin, *norm]
        out_specs.append(small)
        out_shape.append(jax.ShapeDtypeStruct((8, columns), F32))
        scratch = [pltpu.VMEM((8, columns), F32), pltpu.VMEM((2, 8, columns), F32)]
    aliases = {}
    if not first:
        if not last:
            ins.append(small)
            args.append(carried[1])
        aliases = {len(args): 0}
        ins.append(ANY)
        args.append(carried[0])
    return pl.pallas_call(
        functools.partial(backward_kernel, step, last, first),
        grid=(steps,),
        in_specs=ins,
        out_specs=out_specs,
        out_shape=out_shape,
        scratch_shapes=scratch,
        input_output_aliases=aliases,
        compiler_params=params(),
        cost_estimate=cost(32 * steps * rows * depth * columns, steps * rows * 40 * depth),
        name=name,
    )(*args)


def weight_kernel(spans, x_ref, *refs):
    hs, out_ref = refs[:-1], refs[-1]
    total = None
    for (low, high), h_ref in zip(spans, hs):
        x = x_ref[0, low:high, :]
        term = lax.dot_general(x, h_ref[...], (((0,), (0,)), ((), ())), preferred_element_type=F32)
        total = term if total is None else total + term
    out_ref[...] = total.astype(out_ref.dtype)


def weight_terms(everything, base, hs, name):
    _, nodes, depth = everything.shape
    columns = hs[0].shape[1]
    spans, low = [], 0
    for h in hs:
        spans.append((low, low + h.shape[0]))
        low += h.shape[0]
    return pl.pallas_call(
        functools.partial(weight_kernel, tuple(spans)),
        grid=(2,),
        in_specs=[pl.BlockSpec((1, nodes, depth), lambda i: (i + base, 0, 0))]
        + [pl.BlockSpec(h.shape, lambda i: (0, 0)) for h in hs],
        out_specs=pl.BlockSpec((depth, columns), lambda i: (i, 0)),
        out_shape=jax.ShapeDtypeStruct((2 * depth, columns), BF),
        compiler_params=params(),
        cost_estimate=cost(16 * nodes * depth * columns, 6 * nodes * depth),
        name=name,
    )(everything, *hs)


def place_kernel(where_ref, *refs):
    out_ref = refs[-1]
    for k in range(4):

        @pl.when(pl.program_id(0) == k)
        def _():
            out_ref[...] = refs[k][...].astype(F32)


def place_blocks(where, blocks, name):
    depth, columns = blocks[0].shape
    return pl.pallas_call(
        place_kernel,
        grid_spec=pltpu.PrefetchScalarGridSpec(
            num_scalar_prefetch=1,
            grid=(4,),
            in_specs=[pl.BlockSpec((depth, columns), lambda i, where: (0, 0))] * 4,
            out_specs=pl.BlockSpec((depth, columns), lambda i, where: (where[i], 0)),
        ),
        out_shape=jax.ShapeDtypeStruct((4 * depth, columns), F32),
        compiler_params=params(),
        cost_estimate=cost(4 * depth * columns, 24 * depth * columns),
        name=name,
    )(where, *blocks)


def after(value, *deps):
    return lax.optimization_barrier((value, deps))[0]


def across(value, axis, distance):
    size = lax.axis_size(axis)
    return lax.ppermute(value, axis, [(i, i ^ distance) for i in range(size)])


def weight_slices(weight, q):
    depth = weight.shape[0] // 4
    return [lax.dynamic_slice_in_dim(weight, (q ^ d) * depth, depth, 0) for d in range(4)]


def weight_rows(slices):
    far = across(slices[2], "col", 2)
    other = across(slices[3], "col", 2)
    return [slices[0], across(slices[1], "col", 1), far, across(other, "col", 1)]


def reduce_stages(halves, axis):
    size = lax.axis_size(axis)
    bits = size.bit_length() - 1
    place = lax.axis_index(axis)
    orders = [list(range(bits)), list(range(1, bits)) + [0]]
    held = list(halves)
    dtype = held[0].dtype
    for s in range(bits):
        for n, order in enumerate(orders):
            bit = (place >> order[s]) & 1
            part = held[n].shape[0] // 2
            keep = lax.dynamic_slice_in_dim(held[n], bit * part, part, 0)
            send = lax.dynamic_slice_in_dim(held[n], (1 - bit) * part, part, 0)
            got = across(send, axis, 1 << order[s])
            held[n] = (keep.astype(F32) + got.astype(F32)).astype(dtype)
        tie = yield tuple(held)
        if tie is not None:
            held = list(tie)
    for s in reversed(range(1, bits)):
        for n, order in enumerate(orders):
            bit = (place >> order[s]) & 1
            got = across(held[n], axis, 1 << order[s])
            held[n] = jnp.concatenate(
                [jnp.where(bit == 0, held[n], got), jnp.where(bit == 0, got, held[n])], axis=0
            )
        tie = yield tuple(held)
        if tie is not None:
            held = list(tie)
    out = []
    for n, order in enumerate(orders):
        out.append((held[n], across(held[n], axis, 1 << order[0]), (place >> order[0]) & 1))
    yield out


def placed_sum(stages, q, name):
    (held_a, got_a, bit_a), (held_b, got_b, bit_b) = stages
    where = jnp.stack([q ^ bit_a, q ^ 1 ^ bit_a, q ^ 2 ^ bit_b, q ^ 3 ^ bit_b]).astype(jnp.int32)
    return place_blocks(where, [held_a, got_a, held_b, got_b], name)


def chunk_plan(slots):
    step = 2 if slots % 2 == 0 else 1
    total = slots // step
    last = max(1, (2 * total) // 7)
    sizes = [size for size in (total - last, last) if size > 0]
    starts = [sum(sizes[:k]) for k in range(len(sizes))]
    return step, starts, sizes


def gathered_chunks(chunks, near, work, ready=()):
    far = [across(c, "col", 2) for c in chunks]
    carried = None
    for k in range(len(chunks)):
        ties = carried if k else ready
        source = after(far[k], ties) if ties else far[k]
        carried = work(k, [near[k], source, across(source, "col", 1)], carried)
    return carried


def local(
    features,
    neighbours,
    node_valid,
    weight_one,
    gamma_one,
    beta_one,
    weight_two,
    gamma_two,
    beta_two,
    cotangent,
):
    nodes, columns = features.shape
    plan = chunk_plan(nodes // SLOT)
    step, starts, sizes = plan
    chunks = range(len(sizes))
    q = lax.axis_index("col")
    ids = jnp.stack([q, q ^ 1, q ^ 2, q ^ 3]).astype(jnp.int32)
    g1, b1, g2, b2 = (v.reshape(1, columns) for v in (gamma_one, beta_one, gamma_two, beta_two))

    rows = [(starts[k] * step * SLOT, (starts[k] + sizes[k]) * step * SLOT) for k in chunks]
    near = across(features, "col", 1)
    tiles = build_tiles(neighbours, node_valid)
    val = tiles[3]
    slices_one, slices_two = weight_slices(weight_one, q), weight_slices(weight_two, q)

    def work(k, blocks, carried):
        return forward_chunk(ids, plan, k, [features, *blocks], weight_one, tiles, carried, f"forward_one_{k}")

    lin_one, all_one, stats = gathered_chunks(
        [features[a:b] for a, b in rows], [near] * len(sizes), work, (tiles, slices_one, slices_two)
    )
    norm_one = (small_gather(stats, "row"), g1, b1)

    hidden = []
    for k in chunks:
        source = after(lin_one, hidden[-1]) if hidden else lin_one
        hidden.append(result_call(plan, k, source, val, norm_one, BF, f"hidden_{k}"))

    def work(k, blocks, carried):
        return forward_chunk(ids, plan, k, [hidden[k], *blocks], weight_two, tiles, carried, f"forward_two_{k}")

    lin_two, all_two, stats = gathered_chunks(hidden, [across(c, "col", 1) for c in hidden], work)
    norm_two = (small_gather(stats, "row"), g2, b2)
    rows_two = weight_rows(after(slices_two, stats))

    sums = rows_call(
        sums_kernel, plan, None, [lin_two, cotangent], [val], norm_two, None,
        [pltpu.VMEM((2, 8, columns), F32)], "sums_two", 20,
    )
    grads_two = small_gather(sums, "row")
    grads_two = after(grads_two, rows_two[2])
    turned = []
    for k in chunks:
        source = after(lin_two, turned[-1]) if turned else lin_two
        turned.append(turn_call(True, plan, k, source, cotangent, tiles, norm_two, grads_two, f"turn_two_{k}"))
    terms_two = [weight_terms(all_two, b, turned, f"terms_two_{b}") for b in (0, 2)]
    output = result_call(plan, None, lin_two, val, norm_two, F32, "output")
    reduce_two = reduce_stages(terms_two, "row")
    stages = 2 * (lax.axis_size("row").bit_length() - 1)
    state = {"n": 1, "held": next(reduce_two)}

    def beside(value):
        if state["n"] >= stages - 1:
            return value
        value, held = lax.optimization_barrier((value, state["held"]))
        state["held"] = reduce_two.send(held)
        state["n"] += 1
        return value

    def work(k, blocks, carried):
        blocks[0] = beside(blocks[0])
        return backward_chunk(plan, k, [turned[k], *blocks], rows_two, lin_one, norm_one, carried, f"backward_two_{k}")

    grad_one, sums = gathered_chunks(turned, [across(c, "col", 1) for c in turned], work, tuple(terms_two))
    grads_one = small_gather(beside(sums), "row")

    lin_one = beside(lin_one)
    turned = []
    for k in chunks:
        source = after(lin_one, turned[-1]) if turned else lin_one
        turned.append(turn_call(False, plan, k, source, grad_one, tiles, norm_one, grads_one, f"turn_one_{k}"))
    while state["n"] < stages - 1:
        turned[0] = beside(turned[0])
    terms_one = [weight_terms(all_one, b, turned, f"terms_one_{b}") for b in (0, 2)]
    reduce_one = reduce_stages(terms_one, "row")
    held_one, held = lax.optimization_barrier((next(reduce_one), state["held"]))
    stage_last = reduce_two.send(held)
    grad_weight_two = placed_sum(stage_last, q, "place_two")
    held_one = reduce_one.send(held_one)
    for _ in range(stages - 4):
        held_one = next(reduce_one)
    next(reduce_one)
    grad_weight_one = placed_sum(next(reduce_one), q, "place_one")

    rows_one = weight_rows(after(slices_one, turned[-1]))

    def work(k, blocks, carried):
        if k == 1:
            blocks[0] = after(blocks[0], output)
        return backward_chunk(plan, k, [turned[k], *blocks], rows_one, None, None, carried, f"backward_one_{k}")

    (grad_features,) = gathered_chunks(turned, [across(c, "col", 1) for c in turned], work, held_one)

    sums_one, sums_two = jnp.sum(grads_one, axis=0), jnp.sum(grads_two, axis=0)
    return (
        output,
        grad_features,
        grad_weight_one,
        sums_one[1],
        sums_one[0],
        grad_weight_two,
        sums_two[1],
        sums_two[0],
    )


def solution(mesh):
    placed = (
        P("row", "col"),
        P("row", None),
        P("row"),
        P(None, "col"),
        P("col"),
        P("col"),
        P(None, "col"),
        P("col"),
        P("col"),
        P("row", "col"),
    )
    return jax.shard_map(
        local,
        mesh=mesh,
        in_specs=placed,
        out_specs=(
            P("row", "col"),
            P("row", "col"),
            P(None, "col"),
            P("col"),
            P("col"),
            P(None, "col"),
            P("col"),
            P("col"),
        ),
        check_vma=False,
    )
```

```python
import functools

import jax
import jax.numpy as jnp
from jax import lax
from jax.experimental import pallas as pl
from jax.experimental.pallas import tpu as pltpu
from jax.sharding import PartitionSpec as P

SLOT = 128
NBR = 32
LANES = 128
EPSILON = 1e-05
ANY = pl.BlockSpec(memory_space=pl.ANY)
BF = jnp.bfloat16
F32 = jnp.float32


def params(limit):
    return pltpu.CompilerParams(dimension_semantics=("arbitrary",), vmem_limit_bytes=limit << 20)


SMALL = pl.CostEstimate(flops=1000000, bytes_accessed=1000, transcendentals=0)


TOKEN = jax.ShapeDtypeStruct((8, LANES), F32)


def token_spec():
    return pl.BlockSpec((8, LANES), lambda i, *_: (0, 0))


def mark(token_ref):
    token_ref[...] = jnp.zeros_like(token_ref)


def launch(kernel, grid, ins, outs, shapes, args, name, prefetch=(), scratch=(), tokens=(), limit=24):
    count = len(prefetch) + len(args)

    def body(*refs):
        kernel(*refs[:count], *refs[count + len(tokens) :])

    return pl.pallas_call(
        body,
        grid_spec=pltpu.PrefetchScalarGridSpec(
            num_scalar_prefetch=len(prefetch),
            grid=grid,
            in_specs=[*ins, *[pl.BlockSpec(memory_space=pl.ANY)] * len(tokens)],
            out_specs=outs,
            scratch_shapes=list(scratch),
        ),
        out_shape=shapes,
        compiler_params=params(limit),
        cost_estimate=SMALL,
        name=name,
    )(*prefetch, *args, *tokens)


def dot(a, b):
    return jnp.dot(a, b, preferred_element_type=F32)


def dot_t(a, b):
    return lax.dot_general(a, b, (((1,), (1,)), ((), ())), preferred_element_type=F32)


def wide(v, columns):
    return jnp.concatenate([v] * (columns // LANES), axis=1)


def tiles_kernel(nbr_ref, valid_ref, h_ref, ht_ref, inv_ref, val_ref, token_ref):
    mark(token_ref)
    entries = nbr_ref[0]
    rows = lax.broadcasted_iota(jnp.int32, (SLOT, SLOT), 0)
    cols = lax.broadcasted_iota(jnp.int32, (SLOT, SLOT), 1)
    hits = jnp.zeros((SLOT, SLOT), F32)
    degree = jnp.zeros((1, SLOT), F32)
    for k in range(entries.shape[0]):
        one = entries[k : k + 1, :]
        hits += (one == rows).astype(F32)
        degree += (one >= 0).astype(F32)
    eye = (rows == cols).astype(F32)
    joined = hits + eye
    counts = joined + joined * eye
    ht_ref[0] = wide(counts.astype(BF), 2 * SLOT)
    h_ref[0] = wide(counts.T.astype(BF), 2 * SLOT)
    inv_ref[0] = jnp.broadcast_to(1.0 / (degree + 1.0), (SLOT, SLOT)).T
    val_ref[0] = jnp.broadcast_to(valid_ref[0].astype(F32), (SLOT, SLOT)).T


def build_tiles(neighbours, node_valid):
    slots = neighbours.shape[0] // SLOT
    turned = neighbours.reshape(slots, SLOT, NBR).transpose(0, 2, 1)
    square = pl.BlockSpec((1, SLOT, SLOT), lambda i: (i, 0, 0))
    double = pl.BlockSpec((1, SLOT, 2 * SLOT), lambda i: (i, 0, 0))
    return launch(
        tiles_kernel, (slots,),
        [pl.BlockSpec((1, NBR, SLOT), lambda i: (i, 0, 0)), pl.BlockSpec((1, 1, SLOT), lambda i: (i, 0, 0))],
        [double, double, square, square, token_spec()],
        [jax.ShapeDtypeStruct((slots, SLOT, 2 * SLOT), BF)] * 2 + [jax.ShapeDtypeStruct((slots, SLOT, SLOT), F32)] * 2 + [TOKEN],
        [turned, node_valid.reshape(slots, 1, SLOT)], "tiles",
    )


def combine(g_ref):
    mref, first, second, count = (g_ref[:, k, :] for k in range(4))
    shift = first / count
    mean_each = mref + shift
    spread_each = second - first * shift
    total = jnp.sum(count, axis=0, keepdims=True)
    mean = jnp.sum(count * mean_each, axis=0, keepdims=True) / total
    away = mean_each - mean
    variance = jnp.sum(spread_each + count * away * away, axis=0, keepdims=True) / total
    return total, mean, lax.rsqrt(variance + EPSILON)


def small_gather(copies, axis):
    return lax.all_to_all(copies, axis, split_axis=0, concat_axis=0, tiled=True)


def copies_shape(columns):
    return (lax.axis_size("row"), 8, columns)


def spread_rows(out_ref, rows):
    block = jnp.concatenate([*rows, jnp.zeros((8 - len(rows), out_ref.shape[2]), F32)], axis=0)

    def one(n, carry):
        out_ref[n] = block
        return carry

    lax.fori_loop(0, out_ref.shape[0], one, 0)


def split(value):
    high = value.astype(BF)
    return high, (value - high.astype(F32)).astype(BF)


def fold(value):
    return jnp.sum(value.reshape(value.shape[0] // 8, 8, value.shape[1]), axis=0)


def at(ref, k):
    return ref[k : k + 1, :]


def put(ref, k, value):
    ref[k : k + 1, :] = value


def half_kernel(turned, x_ref, y_ref, w_own, w_near, out_ref, token_ref):
    mark(token_ref)
    product = dot_t if turned else dot
    out_ref[...] = product(x_ref[...], w_own[...]) + product(y_ref[...], w_near[...])


def half(ids, big, own, near, weights, turned, name, tokens=()):
    nodes, depth = own.shape
    columns = weights[0][0].shape[1]
    rows = big * SLOT
    flat = pl.BlockSpec((rows, depth), lambda i, ids: (i, 0))

    def kernel(ids_ref, *refs):
        half_kernel(turned, *refs)

    return launch(
        kernel, (nodes // rows,), [flat, flat, *[spec for _, spec in weights]],
        [pl.BlockSpec((rows, columns), lambda i, ids: (i, 0)), token_spec()],
        [jax.ShapeDtypeStruct((nodes, columns), F32), TOKEN],
        [own, near, *[w for w, _ in weights]], name, prefetch=[ids], tokens=tokens,
    )


def weight_block(weight, b):
    depth = weight.shape[0] // 4
    return weight, pl.BlockSpec((depth, weight.shape[1]), lambda i, ids: (ids[b], 0))


def whole_block(piece):
    return piece, pl.BlockSpec(piece.shape, lambda i, ids: (0, 0))


def each_part(big, body, part=32, inner=4):
    def slot(s, carry):
        for r in range(SLOT // part):
            start = pl.multiple_of(s * SLOT + r * part, part)
            body(s, slice(r * part, (r + 1) * part), pl.ds(start, part))
        return carry

    lax.fori_loop(0, big, slot, 0)


def forward_kernel(big, ids_ref, early_ref, x_ref, y_ref, w_far, w_beyond, h_ref, inv_ref, val_ref, lin_ref, st_ref, tot_ref, acc_ref, ref_ref):
    i = pl.program_id(0)
    columns = lin_ref.shape[1]
    tot_ref[...] = early_ref[...] + dot(x_ref[...], w_far[...]) + dot(y_ref[...], w_beyond[...])

    def mix(s, carry):
        rows = pl.ds(pl.multiple_of(s * SLOT, SLOT), SLOT)
        high, low = split(tot_ref[rows, :])
        both = jnp.concatenate([high, low], axis=0)
        lin_ref[rows, :] = dot(h_ref[s], both) * wide(inv_ref[s], columns)
        return carry

    lax.fori_loop(0, big, mix, 0)

    @pl.when(i == 0)
    def _():
        acc_ref[...] = jnp.zeros_like(acc_ref)
        v = val_ref[0]
        count = jnp.sum(v, axis=0, keepdims=True)
        put(ref_ref, 0, jnp.sum(lin_ref[:SLOT, :] * wide(v, columns), axis=0, keepdims=True) / wide(count, columns))

    mref = at(ref_ref, 0)

    def part(s, inner, rows):
        v = val_ref[s, inner, :]
        away = (lin_ref[rows, :] - mref) * wide(v, columns)
        acc_ref[0] += fold(away)
        acc_ref[1] += fold(away * away)
        acc_ref[2, :, :LANES] += fold(v)

    each_part(big, part)

    @pl.when(i == pl.num_programs(0) - 1)
    def _():
        first, second = (jnp.sum(acc_ref[k], axis=0, keepdims=True) for k in range(2))
        count = wide(jnp.sum(acc_ref[2, :, :LANES], axis=0, keepdims=True), columns)
        spread_rows(st_ref, (at(ref_ref, 0), first, second, count))


def forward(ids, big, early, far, beyond, weight, tiles, name, tokens=()):
    h, _, inv, val = tiles
    nodes, columns = early.shape
    rows = big * SLOT
    flat = pl.BlockSpec((rows, columns), lambda i, ids: (i, 0))
    tile = pl.BlockSpec((big, SLOT, SLOT), lambda i, ids: (i, 0, 0))
    double = pl.BlockSpec((big, SLOT, 2 * SLOT), lambda i, ids: (i, 0, 0))
    blocks = [weight_block(weight, 2), weight_block(weight, 3)]
    return launch(
        functools.partial(forward_kernel, big), (nodes // rows,),
        [flat, flat, flat, *[spec for _, spec in blocks], double, tile, tile],
        [flat, pl.BlockSpec(copies_shape(columns), lambda i, ids: (0, 0, 0))],
        [jax.ShapeDtypeStruct((nodes, columns), F32), jax.ShapeDtypeStruct(copies_shape(columns), F32)],
        [early, far, beyond, weight, weight, h, inv, val], name, prefetch=[ids],
        scratch=[pltpu.VMEM((rows, columns), F32), pltpu.VMEM((3, 8, columns), F32), pltpu.VMEM((8, columns), F32)],
        tokens=tokens,
    )


def columns_of(g_ref, gamma_ref, beta_ref, co_ref):
    total, mean, inv_std = combine(g_ref)
    put(co_ref, 0, mean)
    put(co_ref, 1, 0.5 * gamma_ref[...] * inv_std)
    put(co_ref, 2, 0.5 * beta_ref[...])
    put(co_ref, 3, inv_std)
    put(co_ref, 4, total)


def silu_of(away, co_ref):
    u = away * at(co_ref, 1) + at(co_ref, 2)
    return u + u * jnp.tanh(u)


def double_slope(away, co_ref):
    u = away * at(co_ref, 1) + at(co_ref, 2)
    t = jnp.tanh(u)
    return (1.0 + t) * (1.0 + u * (1.0 - t))


def result_kernel(big, lin_ref, val_ref, g_ref, gamma_ref, beta_ref, out_ref, token_ref, co_ref):
    mark(token_ref)

    @pl.when(pl.program_id(0) == 0)
    def _():
        columns_of(g_ref, gamma_ref, beta_ref, co_ref)

    def part(s, inner, rows):
        value = silu_of(lin_ref[rows, :] - at(co_ref, 0), co_ref)
        out_ref[rows, :] = (wide(val_ref[s, inner, :], lin_ref.shape[1]) * value).astype(out_ref.dtype)

    each_part(big, part)


def sums_kernel(big, lin_ref, cot_ref, val_ref, g_ref, gamma_ref, beta_ref, st_ref, co_ref, acc_ref):
    @pl.when(pl.program_id(0) == 0)
    def _():
        columns_of(g_ref, gamma_ref, beta_ref, co_ref)
        acc_ref[...] = jnp.zeros_like(acc_ref)

    def part(s, inner, rows):
        away = lin_ref[rows, :] - at(co_ref, 0)
        valid = wide(val_ref[s, inner, :], lin_ref.shape[1])
        grad = cot_ref[rows, :].astype(F32) * valid * double_slope(away, co_ref)
        acc_ref[0] += fold(grad)
        acc_ref[1] += fold(grad * away)

    each_part(big, part)
    finish_sums(st_ref, co_ref, acc_ref)


def finish_sums(st_ref, co_ref, acc_ref):
    @pl.when(pl.program_id(0) == pl.num_programs(0) - 1)
    def _():
        grad_beta = 0.5 * jnp.sum(acc_ref[0], axis=0, keepdims=True)
        grad_gamma = 0.5 * at(co_ref, 3) * jnp.sum(acc_ref[1], axis=0, keepdims=True)
        spread_rows(st_ref, (grad_beta, grad_gamma))


def turn_kernel(from_cot, big, lin_ref, grad_ref, val_ref, inv_ref, ht_ref, g_ref, sg_ref, gamma_ref, beta_ref, out_ref, token_ref, co_ref, lg_ref):
    mark(token_ref)

    @pl.when(pl.program_id(0) == 0)
    def _():
        columns_of(g_ref, gamma_ref, beta_ref, co_ref)
        sg = sg_ref[...]
        twice = 2.0 / at(co_ref, 4)
        put(co_ref, 5, twice * jnp.sum(sg[:, 0, :], axis=0, keepdims=True))
        put(co_ref, 6, twice * at(co_ref, 3) * jnp.sum(sg[:, 1, :], axis=0, keepdims=True))

    columns = lin_ref.shape[1]

    def part(s, inner, rows):
        away = lin_ref[rows, :] - at(co_ref, 0)
        if from_cot:
            grad = grad_ref[rows, :].astype(F32) * double_slope(away, co_ref)
        else:
            grad = grad_ref[rows, :]
        weight = wide(val_ref[s, inner, :] * inv_ref[s, inner, :], columns)
        high, low = split(weight * (grad - (at(co_ref, 5) + away * at(co_ref, 6))))
        lg_ref[s, inner, :] = high
        lg_ref[s, slice(inner.start + SLOT, inner.stop + SLOT), :] = low

    each_part(big, part)

    def mix(s, carry):
        rows = pl.ds(pl.multiple_of(s * SLOT, SLOT), SLOT)
        out_ref[rows, :] = (dot(ht_ref[s], lg_ref[s]) * at(co_ref, 1)).astype(BF)
        return carry

    lax.fori_loop(0, big, mix, 0)


def rows_call(kernel, big, arrays, tiles, smalls, out_dtype, scratch, name, tokens=(), limit=24):
    rows = big * SLOT
    nodes, columns = arrays[0].shape
    flat = pl.BlockSpec((rows, columns), lambda i: (i, 0))
    ins = [flat for _ in arrays]
    ins += [pl.BlockSpec((big,) + t.shape[1:], lambda i: (i, 0, 0)) for t in tiles]
    ins += [pl.BlockSpec(s.shape, lambda i, n=s.ndim: (0,) * n) for s in smalls]
    if out_dtype is None:
        out_spec = pl.BlockSpec(copies_shape(columns), lambda i: (0, 0, 0))
        out_shape = jax.ShapeDtypeStruct(copies_shape(columns), F32)
    else:
        out_spec = [flat, token_spec()]
        out_shape = [jax.ShapeDtypeStruct((nodes, columns), out_dtype), TOKEN]
    return launch(
        functools.partial(kernel, big), (nodes // rows,), ins, out_spec, out_shape, [*arrays, *tiles, *smalls], name,
        scratch=[pltpu.VMEM((8, columns), F32)] + scratch, tokens=tokens, limit=limit,
    )


def turn_call(from_cot, big, lin, grad, tiles, norm, sums, name, tokens=()):
    _, ht, inv, val = tiles
    return rows_call(
        functools.partial(turn_kernel, from_cot), big, [lin, grad], [val, inv, ht], [norm[0], sums, *norm[1:]], BF,
        [pltpu.VMEM((big, 2 * SLOT, lin.shape[1]), BF)], name, tokens, 60,
    )


def backward_kernel(big, last, early_ref, x_ref, y_ref, w_far, w_beyond, *refs):
    total = early_ref[...] + dot_t(x_ref[...], w_far[...]) + dot_t(y_ref[...], w_beyond[...])
    if last:
        refs[-2][...] = total
        mark(refs[-1])
        return
    lin_ref, g_ref, gamma_ref, beta_ref, out_ref, st_ref, co_ref, acc_ref = refs
    out_ref[...] = total

    @pl.when(pl.program_id(0) == 0)
    def _():
        columns_of(g_ref, gamma_ref, beta_ref, co_ref)
        acc_ref[...] = jnp.zeros_like(acc_ref)

    def part(s, inner, rows):
        away = lin_ref[rows, :] - at(co_ref, 0)
        grad = out_ref[rows, :] * double_slope(away, co_ref)
        out_ref[rows, :] = grad
        acc_ref[0] += fold(grad)
        acc_ref[1] += fold(grad * away)

    each_part(big, part)
    finish_sums(st_ref, co_ref, acc_ref)


def backward(big, early, far, beyond, pieces, lin, norm, name, tokens=()):
    nodes, columns = early.shape
    depth = far.shape[1]
    rows = big * SLOT
    last = norm is None
    flat = pl.BlockSpec((rows, columns), lambda i: (i, 0))
    fixed = lambda s: pl.BlockSpec(s.shape, lambda i, n=s.ndim: (0,) * n)
    ins = [flat, flat, flat, *map(fixed, pieces)]
    args = [early, far, beyond, *pieces]
    out_specs = [flat]
    out_shape = [jax.ShapeDtypeStruct((nodes, columns), F32)]
    scratch = []
    if last:
        out_specs.append(token_spec())
        out_shape.append(TOKEN)
    else:
        ins += [flat, *map(fixed, norm)]
        args += [lin, *norm]
        out_specs.append(pl.BlockSpec(copies_shape(columns), lambda i: (0, 0, 0)))
        out_shape.append(jax.ShapeDtypeStruct(copies_shape(columns), F32))
        scratch = [pltpu.VMEM((8, columns), F32), pltpu.VMEM((2, 8, columns), F32)]
    return launch(
        functools.partial(backward_kernel, big, last), (nodes // rows,), ins, out_specs, out_shape, args, name,
        scratch=scratch, tokens=tokens,
    )


def weight_kernel(spans, other, meta_ref, *refs):
    sources, h_hbm, outs, (token_ref, buf_ref, h_ref, sem) = refs[:4], refs[4], refs[5:7], refs[7:]
    mark(token_ref)
    for m in range(2):
        for n, span in enumerate(spans):
            rows = pl.ds(*span)
            if m == 0:
                pltpu.make_async_copy(h_hbm.at[rows, :], h_ref.at[rows, :], sem.at[2, n]).start()
            for k in range(2):

                @pl.when((meta_ref[4 + m] ^ other) == k)
                def _():
                    pltpu.make_async_copy(
                        sources[2 * m + k].at[rows, :], buf_ref.at[m, rows, :], sem.at[m, n]
                    ).start()

    for m in range(2):
        total = None
        for n, (start, size) in enumerate(spans):
            rows = pl.ds(start, size)
            if m == 0:
                pltpu.make_async_copy(h_hbm.at[rows, :], h_ref.at[rows, :], sem.at[2, n]).wait()
            pltpu.make_async_copy(sources[2 * m].at[rows, :], buf_ref.at[m, rows, :], sem.at[m, n]).wait()
            x, h = buf_ref[m, start : start + size, :], h_ref[start : start + size, :]
            term = lax.dot_general(x, h, (((0,), (0,)), ((), ())), preferred_element_type=F32)
            total = term if total is None else total + term
        outs[m][...] = total.astype(outs[m].dtype)


def weight_terms(meta, other, pairs, h, name, tokens=()):
    nodes, depth = pairs[0][0].shape
    columns = h.shape[1]
    pieces = 2 if nodes % 32 == 0 else 1
    spans = tuple((n * (nodes // pieces), nodes // pieces) for n in range(pieces))
    whole = pl.BlockSpec((depth, columns), lambda i, meta: (0, 0))
    return launch(
        functools.partial(weight_kernel, spans, other), (1,), [pl.BlockSpec(memory_space=pl.ANY)] * 5,
        [whole, whole, token_spec()],
        [jax.ShapeDtypeStruct((depth, columns), BF)] * 2 + [TOKEN], [*pairs[0], *pairs[1], h], name, prefetch=[meta],
        scratch=[
            pltpu.VMEM((2, nodes, depth), BF), pltpu.VMEM((nodes, columns), BF), pltpu.SemaphoreType.DMA((3, pieces))
        ],
        tokens=tokens, limit=60,
    )


def place_kernel(orders, meta_ref, *refs):
    out_ref, token_ref = refs[-2:]
    mark(token_ref)
    pieces = 1 << (len(orders[0]) - 1)
    size = out_ref.shape[0] // pieces
    for k in range(4):

        @pl.when(pl.program_id(0) == k)
        def _():
            mask = 0
            for b in orders[k // 2][1:]:
                mask = 2 * mask + meta_ref[4 + b]
            for n in range(pieces):
                start = pl.multiple_of((mask ^ n) * size, size)
                out_ref[pl.ds(start, size), :] = refs[k][n * size : (n + 1) * size, :].astype(F32)


def place_blocks(meta, blocks, orders, name, limit, tokens):
    depth, columns = blocks[0].shape
    return launch(
        functools.partial(place_kernel, orders), (4,), [pl.BlockSpec((depth, columns), lambda i, meta: (0, 0))] * 4,
        [
            pl.BlockSpec((depth, columns), lambda i, meta: (meta[0] ^ (i // 2 * 2) ^ (i % 2) ^ meta[4 + i // 2], 0)),
            token_spec(),
        ],
        [jax.ShapeDtypeStruct((4 * depth, columns), F32), TOKEN], blocks, name, prefetch=[meta], limit=limit,
        tokens=tokens,
    )


def after(value, *tokens):
    value, tokens = lax.optimization_barrier((value, tokens))
    return value, tokens


def across(value, axis, distance):
    size = lax.axis_size(axis)
    return lax.ppermute(value, axis, [(i, i ^ distance) for i in range(size)])


def slices_kernel(ids_ref, one_ref, two_ref, *refs):
    outs, (token_ref, sem) = refs[:6], refs[6:]
    mark(token_ref)
    depth = outs[0].shape[0]
    copies = []
    for n, out_ref in enumerate(outs):
        start = pl.multiple_of(ids_ref[1 + n % 3] * depth, depth)
        source = (one_ref, two_ref)[n // 3].at[pl.ds(start, depth), :]
        copies.append(pltpu.make_async_copy(source, out_ref, sem.at[n]))
    for copy in copies:
        copy.start()
    for copy in copies:
        copy.wait()


def weight_slices(ids, one, two):
    depth, columns = one.shape[0] // 4, one.shape[1]
    hbm = pl.BlockSpec(memory_space=pltpu.HBM)
    outs = launch(
        slices_kernel, (1,), [hbm, hbm], [hbm] * 6 + [token_spec()],
        [jax.ShapeDtypeStruct((depth, columns), one.dtype)] * 6 + [TOKEN], [one, two], "weight_slices",
        prefetch=[ids], scratch=[pltpu.SemaphoreType.DMA((6,))],
    )
    return outs[:3], outs[3:6], outs[6]


def weight_rows(slices):
    far = across(slices[1], "col", 2)
    other = across(slices[2], "col", 2)
    return [across(slices[0], "col", 1), far, across(other, "col", 1)], (far, other)


def fold_kernel(last, place, meta_ref, keep_ref, got_ref, *refs):
    mark(refs[-1])
    if last:
        refs[0][...] = (keep_ref[...].astype(F32) + got_ref[...].astype(F32)).astype(BF)
        return
    part = refs[0].shape[0]
    bit = meta_ref[4 + place]
    for out_ref, which in zip(refs[:2], (1 - bit, bit)):
        rows = pl.ds(pl.multiple_of(which * part, part), part)
        out_ref[...] = (keep_ref[rows, :].astype(F32) + got_ref[rows, :].astype(F32)).astype(BF)


def join_kernel(meta_ref, keep_ref, got_ref, out_ref, token_ref):
    mark(token_ref)
    part = keep_ref.shape[0]
    out_ref[:part, :] = keep_ref[...]
    out_ref[part:, :] = got_ref[...]


def small_call(kernel, meta, keep, got, rows, name, tokens):
    columns = keep.shape[1]
    whole = lambda r: pl.BlockSpec((r, columns), lambda i, bit: (0, 0))
    return launch(
        kernel, (1,), [whole(keep.shape[0])] * 2, [whole(r) for r in rows] + [token_spec()],
        [jax.ShapeDtypeStruct((r, columns), BF) for r in rows] + [TOKEN], [keep, got], name, prefetch=[meta], tokens=tokens,
    )


class RowSum:
    def __init__(self, axis, meta, terms, name):
        self.axis, self.meta, self.name = axis, meta, name
        self.bits = lax.axis_size(axis).bit_length() - 1
        self.stages = 2 * self.bits
        self.orders = [list(range(self.bits)), list(range(1, self.bits)) + [0]]
        *self.send, self.sent = terms(1, ())
        *self.keep, self.kept = terms(0, (self.sent,))
        self.stage = 0
        self.step(())

    def step(self, tokens):
        s, bits = self.stage, self.bits
        self.stage += 1
        started = []
        for n in range(2):
            rows = self.keep[n].shape[0]
            call = lambda kernel, sizes: small_call(
                kernel, self.meta, self.keep[n], self.got[n], sizes, f"{self.name}_{n}_{s}", tokens
            )
            if 0 < s < bits:
                fold = functools.partial(fold_kernel, False, self.orders[n][s])
                self.send[n], self.keep[n], token = call(fold, [rows // 2] * 2)
            elif s == bits:
                self.keep[n], token = call(functools.partial(fold_kernel, True, 0), [rows])
            elif s > bits:
                self.keep[n], token = call(join_kernel, [2 * rows])
            if s > 0:
                started.append(token)
        level = s if s < bits else 2 * bits - 1 - s
        moved = self.send if s < bits else self.keep
        self.got = [across(moved[n], self.axis, 1 << self.orders[n][level]) for n in range(2)]
        return tuple(started)

    def next(self, *tokens):
        return self.step(tokens) if self.stage < self.stages else tokens

    def placed(self, limit, tokens=()):
        while self.stage < self.stages:
            self.step(())
        blocks = [v for n in range(2) for v in (self.keep[n], self.got[n])]
        return place_blocks(self.meta, blocks, self.orders, f"place_{self.name}", limit, tokens)


def local(
    features,
    neighbours,
    node_valid,
    weight_one,
    gamma_one,
    beta_one,
    weight_two,
    gamma_two,
    beta_two,
    cotangent,
):
    nodes, columns = features.shape
    slots = nodes // SLOT
    big = slots // 2 if slots % 2 == 0 else slots
    q = lax.axis_index("col")
    place = lax.axis_index("row")
    bits = [(place >> b) & 1 for b in range(lax.axis_size("row").bit_length() - 1)]
    ids = jnp.stack([q, q ^ 1, q ^ 2, q ^ 3, *bits]).astype(jnp.int32)
    g1, b1, g2, b2 = (v.reshape(1, columns) for v in (gamma_one, beta_one, gamma_two, beta_two))

    far_one = across(features, "col", 2)
    near_one = across(features, "col", 1)
    *tiles, tiles_token = build_tiles(neighbours, node_valid)
    val = tiles[3]
    slices_one, slices_two, slices_token = weight_slices(ids, weight_one, weight_two)
    early, token = half(ids, big, features, near_one, [weight_block(weight_one, b) for b in (0, 1)], False, "half_one")
    far_one, tokens = after(far_one, token, tiles_token, slices_token)
    beyond_one = across(far_one, "col", 1)
    lin_one, stats = forward(ids, big, early, far_one, beyond_one, weight_one, tiles, "forward_one", tokens)
    norm_one = (small_gather(stats, "row"), g1, b1)

    hidden, _ = rows_call(result_kernel, big, [lin_one], [val], norm_one, BF, [], "hidden")
    far_two, near_two = across(hidden, "col", 2), across(hidden, "col", 1)
    early, token = half(ids, big, hidden, near_two, [weight_block(weight_two, b) for b in (0, 1)], False, "half_two")
    far_two, tokens = after(far_two, token)
    beyond_two = across(far_two, "col", 1)
    slices_two, (far_two,) = after(slices_two, far_two)
    rows_two, crossing = weight_rows(slices_two)
    lin_two, stats = forward(ids, big, early, far_two, beyond_two, weight_two, tiles, "forward_two", tokens)
    norm_two = (small_gather(stats, "row"), g2, b2)

    sums = rows_call(
        sums_kernel, big, [lin_two, cotangent], [val], norm_two, None, [pltpu.VMEM((2, 8, columns), F32)], "sums_two"
    )
    grads_two = small_gather(sums, "row")
    turned, _ = turn_call(True, big, lin_two, cotangent, tiles, norm_two, grads_two, "turn_two", crossing)
    far, near = across(turned, "col", 2), across(turned, "col", 1)

    def terms_two(other, tokens, h=turned):
        return weight_terms(ids, other, ((hidden, near_two), (far_two, beyond_two)), h, "terms_two", tokens)

    sum_two = RowSum("row", ids, terms_two, "two")
    weights = [weight_block(weight_two, 0), whole_block(rows_two[0])]
    early, token = half(ids, big, turned, near, weights, True, "half_back_two", (sum_two.kept,))
    far, tokens = after(far, *sum_two.next(*sum_two.next(token)))
    beyond = across(far, "col", 1)
    slices_one, (far,) = after(slices_one, far)
    rows_one, crossing = weight_rows(slices_one)
    grad_one, sums = backward(big, early, far, beyond, rows_two[1:], lin_one, norm_one, "backward_two", tokens)
    sums, tokens = after(sums, *sum_two.next(sums))
    grads_one = small_gather(sums, "row")

    tokens = (*tokens, *crossing, *sum_two.next())
    turned, _ = turn_call(False, big, lin_one, grad_one, tiles, norm_one, grads_one, "turn_one", tokens)
    far, near = across(turned, "col", 2), across(turned, "col", 1)

    def terms_one(other, tokens, h=turned):
        return weight_terms(ids, other, ((features, near_one), (far_one, beyond_one)), h, "terms_one", tokens)

    sum_one = RowSum("row", ids, terms_one, "one")
    weights = [weight_block(weight_one, 0), whole_block(rows_one[0])]
    early, token = half(ids, big, turned, near, weights, True, "half_back_one", (sum_one.kept,))
    sum_two.next(sum_one.kept)
    output, token = rows_call(result_kernel, big, [lin_two], [val], norm_two, F32, [], "output", sum_one.next(token))
    grad_weight_two, token = sum_two.placed(60, (token,))
    sum_one.next(token)
    far, tokens = after(far, *sum_one.next())
    beyond = across(far, "col", 1)
    grad_features, token = backward(big, early, far, beyond, rows_one[1:], None, None, "backward_one", tokens)
    while sum_one.stage < sum_one.stages - 1:
        sum_one.next()
    sum_one.next(token)
    grad_weight_one, _ = sum_one.placed(24)

    sums_one, sums_two = jnp.sum(grads_one, axis=0), jnp.sum(grads_two, axis=0)
    return (
        output,
        grad_features,
        grad_weight_one,
        sums_one[1],
        sums_one[0],
        grad_weight_two,
        sums_two[1],
        sums_two[0],
    )


def solution(mesh):
    placed = (
        P("row", "col"),
        P("row", None),
        P("row"),
        P(None, "col"),
        P("col"),
        P("col"),
        P(None, "col"),
        P("col"),
        P("col"),
        P("row", "col"),
    )
    return jax.shard_map(
        local,
        mesh=mesh,
        in_specs=placed,
        out_specs=(
            P("row", "col"),
            P("row", "col"),
            P(None, "col"),
            P("col"),
            P("col"),
            P(None, "col"),
            P("col"),
            P("col"),
        ),
        check_vma=False,
    )
```

```python
import functools

import jax
import jax.numpy as jnp
from jax import lax
from jax.experimental import pallas as pl
from jax.experimental.pallas import tpu as pltpu
from jax.sharding import PartitionSpec as P

SLOT = 128
NBR = 32
LANES = 128
EPSILON = 1e-05
ANY = pl.BlockSpec(memory_space=pl.ANY)
BF = jnp.bfloat16
F32 = jnp.float32


def params(limit):
    return pltpu.CompilerParams(dimension_semantics=("arbitrary",), vmem_limit_bytes=limit << 20)


SMALL = pl.CostEstimate(flops=1000000, bytes_accessed=1000, transcendentals=0)


TOKEN = jax.ShapeDtypeStruct((8, LANES), F32)


def token_spec():
    return pl.BlockSpec((8, LANES), lambda i, *_: (0, 0))


def mark(token_ref):
    token_ref[...] = jnp.zeros_like(token_ref)


def launch(kernel, grid, ins, outs, shapes, args, name, prefetch=(), scratch=(), tokens=(), limit=24):
    count = len(prefetch) + len(args)

    def body(*refs):
        kernel(*refs[:count], *refs[count + len(tokens) :])

    return pl.pallas_call(
        body,
        grid_spec=pltpu.PrefetchScalarGridSpec(
            num_scalar_prefetch=len(prefetch),
            grid=grid,
            in_specs=[*ins, *[pl.BlockSpec(memory_space=pl.ANY)] * len(tokens)],
            out_specs=outs,
            scratch_shapes=list(scratch),
        ),
        out_shape=shapes,
        compiler_params=params(limit),
        cost_estimate=SMALL,
        name=name,
    )(*prefetch, *args, *tokens)


def dot(a, b):
    return jnp.dot(a, b, preferred_element_type=F32)


def dot_t(a, b):
    return lax.dot_general(a, b, (((1,), (1,)), ((), ())), preferred_element_type=F32)


def wide(v, columns):
    return jnp.concatenate([v] * (columns // LANES), axis=1)


def tiles_kernel(nbr_ref, valid_ref, h_ref, ht_ref, inv_ref, val_ref, token_ref):
    mark(token_ref)
    entries = nbr_ref[0]
    rows = lax.broadcasted_iota(jnp.int32, (SLOT, SLOT), 0)
    cols = lax.broadcasted_iota(jnp.int32, (SLOT, SLOT), 1)
    hits = jnp.zeros((SLOT, SLOT), F32)
    degree = jnp.zeros((1, SLOT), F32)
    for k in range(entries.shape[0]):
        one = entries[k : k + 1, :]
        hits += (one == rows).astype(F32)
        degree += (one >= 0).astype(F32)
    eye = (rows == cols).astype(F32)
    joined = hits + eye
    counts = joined + joined * eye
    ht_ref[0] = wide(counts.astype(BF), 2 * SLOT)
    h_ref[0] = wide(counts.T.astype(BF), 2 * SLOT)
    valid = valid_ref[0].astype(F32)
    inv_ref[0] = jnp.broadcast_to(valid / (degree + 1.0), (SLOT, SLOT)).T
    val_ref[0] = jnp.broadcast_to(valid, (SLOT, SLOT)).T


def build_tiles(neighbours, node_valid):
    slots = neighbours.shape[0] // SLOT
    turned = neighbours.reshape(slots, SLOT, NBR).transpose(0, 2, 1)
    square = pl.BlockSpec((1, SLOT, SLOT), lambda i: (i, 0, 0))
    double = pl.BlockSpec((1, SLOT, 2 * SLOT), lambda i: (i, 0, 0))
    return launch(
        tiles_kernel, (slots,),
        [pl.BlockSpec((1, NBR, SLOT), lambda i: (i, 0, 0)), pl.BlockSpec((1, 1, SLOT), lambda i: (i, 0, 0))],
        [double, double, square, square, token_spec()],
        [jax.ShapeDtypeStruct((slots, SLOT, 2 * SLOT), BF)] * 2 + [jax.ShapeDtypeStruct((slots, SLOT, SLOT), F32)] * 2 + [TOKEN],
        [turned, node_valid.reshape(slots, 1, SLOT)], "tiles",
    )


def combine(g_ref):
    mref, first, second, count = (g_ref[:, k, :] for k in range(4))
    shift = first / count
    mean_each = mref + shift
    spread_each = second - first * shift
    total = jnp.sum(count, axis=0, keepdims=True)
    mean = jnp.sum(count * mean_each, axis=0, keepdims=True) / total
    away = mean_each - mean
    variance = jnp.sum(spread_each + count * away * away, axis=0, keepdims=True) / total
    return total, mean, lax.rsqrt(variance + EPSILON)


def small_gather(copies, axis):
    return lax.all_to_all(copies, axis, split_axis=0, concat_axis=0, tiled=True)


def copies_shape(columns):
    return (lax.axis_size("row"), 8, columns)


def spread_rows(out_ref, rows):
    block = jnp.concatenate([*rows, jnp.zeros((8 - len(rows), out_ref.shape[2]), F32)], axis=0)

    def one(n, carry):
        out_ref[n] = block
        return carry

    lax.fori_loop(0, out_ref.shape[0], one, 0)


def split(value):
    high = value.astype(BF)
    return high, (value - high.astype(F32)).astype(BF)


def fold(value):
    return jnp.sum(value.reshape(value.shape[0] // 8, 8, value.shape[1]), axis=0)


def at(ref, k):
    return ref[k : k + 1, :]


def put(ref, k, value):
    ref[k : k + 1, :] = value


def half_kernel(turned, x_ref, y_ref, w_own, w_near, out_ref, token_ref):
    mark(token_ref)
    product = dot_t if turned else dot
    out_ref[...] = product(x_ref[...], w_own[...]) + product(y_ref[...], w_near[...])


def half(ids, big, own, near, weights, turned, name, tokens=()):
    nodes, depth = own.shape
    columns = weights[0][0].shape[1]
    rows = big * SLOT
    flat = pl.BlockSpec((rows, depth), lambda i, ids: (i, 0))

    def kernel(ids_ref, *refs):
        half_kernel(turned, *refs)

    return launch(
        kernel, (nodes // rows,), [flat, flat, *[spec for _, spec in weights]],
        [pl.BlockSpec((rows, columns), lambda i, ids: (i, 0)), token_spec()],
        [jax.ShapeDtypeStruct((nodes, columns), F32), TOKEN],
        [own, near, *[w for w, _ in weights]], name, prefetch=[ids], tokens=tokens,
    )


def weight_block(weight, b):
    depth = weight.shape[0] // 4
    return weight, pl.BlockSpec((depth, weight.shape[1]), lambda i, ids: (ids[b], 0))


def whole_block(piece):
    return piece, pl.BlockSpec(piece.shape, lambda i, ids: (0, 0))


def each_part(big, body, part=32, inner=4):
    def slot(s, carry):
        for r in range(SLOT // part):
            start = pl.multiple_of(s * SLOT + r * part, part)
            body(s, slice(r * part, (r + 1) * part), pl.ds(start, part))
        return carry

    lax.fori_loop(0, big, slot, 0)


def forward_kernel(big, ids_ref, early_ref, x_ref, y_ref, w_far, w_beyond, h_ref, inv_ref, val_ref, lin_ref, st_ref, tot_ref, acc_ref, ref_ref):
    i = pl.program_id(0)
    columns = lin_ref.shape[1]
    tot_ref[...] = early_ref[...] + dot(x_ref[...], w_far[...]) + dot(y_ref[...], w_beyond[...])

    def mix(s, carry):
        rows = pl.ds(pl.multiple_of(s * SLOT, SLOT), SLOT)
        high, low = split(tot_ref[rows, :])
        both = jnp.concatenate([high, low], axis=0)
        lin_ref[rows, :] = dot(h_ref[s], both) * wide(inv_ref[s], columns)
        return carry

    lax.fori_loop(0, big, mix, 0)

    @pl.when(i == 0)
    def _():
        acc_ref[...] = jnp.zeros_like(acc_ref)
        v = val_ref[0]
        count = jnp.sum(v, axis=0, keepdims=True)
        put(ref_ref, 0, jnp.sum(lin_ref[:SLOT, :] * wide(v, columns), axis=0, keepdims=True) / wide(count, columns))

    mref = at(ref_ref, 0)

    def part(s, inner, rows):
        v = val_ref[s, inner, :]
        away = (lin_ref[rows, :] - mref) * wide(v, columns)
        acc_ref[0] += fold(away)
        acc_ref[1] += fold(away * away)
        acc_ref[2, :, :LANES] += fold(v)

    each_part(big, part)

    @pl.when(i == pl.num_programs(0) - 1)
    def _():
        first, second = (jnp.sum(acc_ref[k], axis=0, keepdims=True) for k in range(2))
        count = wide(jnp.sum(acc_ref[2, :, :LANES], axis=0, keepdims=True), columns)
        spread_rows(st_ref, (at(ref_ref, 0), first, second, count))


def forward(ids, big, early, far, beyond, weight, tiles, name, tokens=()):
    h, _, inv, val = tiles
    nodes, columns = early.shape
    rows = big * SLOT
    flat = pl.BlockSpec((rows, columns), lambda i, ids: (i, 0))
    tile = pl.BlockSpec((big, SLOT, SLOT), lambda i, ids: (i, 0, 0))
    double = pl.BlockSpec((big, SLOT, 2 * SLOT), lambda i, ids: (i, 0, 0))
    blocks = [weight_block(weight, 2), weight_block(weight, 3)]
    return launch(
        functools.partial(forward_kernel, big), (nodes // rows,),
        [flat, flat, flat, *[spec for _, spec in blocks], double, tile, tile],
        [flat, pl.BlockSpec(copies_shape(columns), lambda i, ids: (0, 0, 0))],
        [jax.ShapeDtypeStruct((nodes, columns), F32), jax.ShapeDtypeStruct(copies_shape(columns), F32)],
        [early, far, beyond, weight, weight, h, inv, val], name, prefetch=[ids],
        scratch=[pltpu.VMEM((rows, columns), F32), pltpu.VMEM((3, 8, columns), F32), pltpu.VMEM((8, columns), F32)],
        tokens=tokens,
    )


def columns_of(g_ref, gamma_ref, beta_ref, co_ref):
    total, mean, inv_std = combine(g_ref)
    put(co_ref, 0, mean)
    put(co_ref, 1, 0.5 * gamma_ref[...] * inv_std)
    put(co_ref, 2, 0.5 * beta_ref[...])
    put(co_ref, 3, inv_std)
    put(co_ref, 4, total)


def silu_of(away, co_ref):
    u = away * at(co_ref, 1) + at(co_ref, 2)
    return u + u * jnp.tanh(u)


def double_slope(away, co_ref):
    u = away * at(co_ref, 1) + at(co_ref, 2)
    t = jnp.tanh(u)
    return (1.0 + t) * (1.0 + u * (1.0 - t))


def result_kernel(big, lin_ref, val_ref, g_ref, gamma_ref, beta_ref, out_ref, token_ref, co_ref):
    mark(token_ref)

    @pl.when(pl.program_id(0) == 0)
    def _():
        columns_of(g_ref, gamma_ref, beta_ref, co_ref)

    def part(s, inner, rows):
        value = silu_of(lin_ref[rows, :] - at(co_ref, 0), co_ref)
        out_ref[rows, :] = (wide(val_ref[s, inner, :], lin_ref.shape[1]) * value).astype(out_ref.dtype)

    each_part(big, part)


def sums_kernel(big, lin_ref, cot_ref, val_ref, g_ref, gamma_ref, beta_ref, st_ref, co_ref, acc_ref):
    @pl.when(pl.program_id(0) == 0)
    def _():
        columns_of(g_ref, gamma_ref, beta_ref, co_ref)
        acc_ref[...] = jnp.zeros_like(acc_ref)

    def part(s, inner, rows):
        away = lin_ref[rows, :] - at(co_ref, 0)
        valid = wide(val_ref[s, inner, :], lin_ref.shape[1])
        grad = cot_ref[rows, :].astype(F32) * valid * double_slope(away, co_ref)
        acc_ref[0] += fold(grad)
        acc_ref[1] += fold(grad * away)

    each_part(big, part)
    finish_sums(st_ref, co_ref, acc_ref)


def finish_sums(st_ref, co_ref, acc_ref):
    @pl.when(pl.program_id(0) == pl.num_programs(0) - 1)
    def _():
        grad_beta = 0.5 * jnp.sum(acc_ref[0], axis=0, keepdims=True)
        grad_gamma = 0.5 * at(co_ref, 3) * jnp.sum(acc_ref[1], axis=0, keepdims=True)
        spread_rows(st_ref, (grad_beta, grad_gamma))


def turn_kernel(from_cot, big, lin_ref, grad_ref, inv_ref, ht_ref, g_ref, sg_ref, gamma_ref, beta_ref, out_ref, token_ref, co_ref, lg_ref):
    mark(token_ref)

    @pl.when(pl.program_id(0) == 0)
    def _():
        columns_of(g_ref, gamma_ref, beta_ref, co_ref)
        sg = sg_ref[...]
        twice = 2.0 / at(co_ref, 4)
        put(co_ref, 5, twice * jnp.sum(sg[:, 0, :], axis=0, keepdims=True))
        put(co_ref, 6, twice * at(co_ref, 3) * jnp.sum(sg[:, 1, :], axis=0, keepdims=True))

    columns = lin_ref.shape[1]

    def part(s, inner, rows):
        away = lin_ref[rows, :] - at(co_ref, 0)
        if from_cot:
            grad = grad_ref[rows, :].astype(F32) * double_slope(away, co_ref)
        else:
            grad = grad_ref[rows, :]
        weight = wide(inv_ref[s, inner, :], columns)
        high, low = split(weight * (grad - (at(co_ref, 5) + away * at(co_ref, 6))))
        lg_ref[s, inner, :] = high
        lg_ref[s, slice(inner.start + SLOT, inner.stop + SLOT), :] = low

    each_part(big, part)

    def mix(s, carry):
        rows = pl.ds(pl.multiple_of(s * SLOT, SLOT), SLOT)
        out_ref[rows, :] = (dot(ht_ref[s], lg_ref[s]) * at(co_ref, 1)).astype(BF)
        return carry

    lax.fori_loop(0, big, mix, 0)


def rows_call(kernel, big, arrays, tiles, smalls, out_dtype, scratch, name, tokens=(), limit=24):
    rows = big * SLOT
    nodes, columns = arrays[0].shape
    flat = pl.BlockSpec((rows, columns), lambda i: (i, 0))
    ins = [flat for _ in arrays]
    ins += [pl.BlockSpec((big,) + t.shape[1:], lambda i: (i, 0, 0)) for t in tiles]
    ins += [pl.BlockSpec(s.shape, lambda i, n=s.ndim: (0,) * n) for s in smalls]
    if out_dtype is None:
        out_spec = pl.BlockSpec(copies_shape(columns), lambda i: (0, 0, 0))
        out_shape = jax.ShapeDtypeStruct(copies_shape(columns), F32)
    else:
        out_spec = [flat, token_spec()]
        out_shape = [jax.ShapeDtypeStruct((nodes, columns), out_dtype), TOKEN]
    return launch(
        functools.partial(kernel, big), (nodes // rows,), ins, out_spec, out_shape, [*arrays, *tiles, *smalls], name,
        scratch=[pltpu.VMEM((8, columns), F32)] + scratch, tokens=tokens, limit=limit,
    )


def turn_call(from_cot, big, lin, grad, tiles, norm, sums, name, tokens=()):
    _, ht, inv, _ = tiles
    return rows_call(
        functools.partial(turn_kernel, from_cot), big, [lin, grad], [inv, ht], [norm[0], sums, *norm[1:]], BF,
        [pltpu.VMEM((big, 2 * SLOT, lin.shape[1]), BF)], name, tokens, 60,
    )


def backward_kernel(big, last, early_ref, x_ref, y_ref, w_far, w_beyond, *refs):
    total = early_ref[...] + dot_t(x_ref[...], w_far[...]) + dot_t(y_ref[...], w_beyond[...])
    if last:
        refs[-2][...] = total
        mark(refs[-1])
        return
    lin_ref, g_ref, gamma_ref, beta_ref, out_ref, st_ref, co_ref, acc_ref = refs
    out_ref[...] = total

    @pl.when(pl.program_id(0) == 0)
    def _():
        columns_of(g_ref, gamma_ref, beta_ref, co_ref)
        acc_ref[...] = jnp.zeros_like(acc_ref)

    def part(s, inner, rows):
        away = lin_ref[rows, :] - at(co_ref, 0)
        grad = out_ref[rows, :] * double_slope(away, co_ref)
        out_ref[rows, :] = grad
        acc_ref[0] += fold(grad)
        acc_ref[1] += fold(grad * away)

    each_part(big, part)
    finish_sums(st_ref, co_ref, acc_ref)


def backward(big, early, far, beyond, pieces, lin, norm, name, tokens=()):
    nodes, columns = early.shape
    depth = far.shape[1]
    rows = big * SLOT
    last = norm is None
    flat = pl.BlockSpec((rows, columns), lambda i: (i, 0))
    fixed = lambda s: pl.BlockSpec(s.shape, lambda i, n=s.ndim: (0,) * n)
    ins = [flat, flat, flat, *map(fixed, pieces)]
    args = [early, far, beyond, *pieces]
    out_specs = [flat]
    out_shape = [jax.ShapeDtypeStruct((nodes, columns), F32)]
    scratch = []
    if last:
        out_specs.append(token_spec())
        out_shape.append(TOKEN)
    else:
        ins += [flat, *map(fixed, norm)]
        args += [lin, *norm]
        out_specs.append(pl.BlockSpec(copies_shape(columns), lambda i: (0, 0, 0)))
        out_shape.append(jax.ShapeDtypeStruct(copies_shape(columns), F32))
        scratch = [pltpu.VMEM((8, columns), F32), pltpu.VMEM((2, 8, columns), F32)]
    return launch(
        functools.partial(backward_kernel, big, last), (nodes // rows,), ins, out_specs, out_shape, args, name,
        scratch=scratch, tokens=tokens,
    )


def weight_kernel(spans, other, meta_ref, *refs):
    sources, h_hbm, outs, (token_ref, buf_ref, h_ref, sem) = refs[:4], refs[4], refs[5:7], refs[7:]
    mark(token_ref)
    for m in range(2):
        for n, span in enumerate(spans):
            rows = pl.ds(*span)
            if m == 0:
                pltpu.make_async_copy(h_hbm.at[rows, :], h_ref.at[rows, :], sem.at[2, n]).start()
            for k in range(2):

                @pl.when((meta_ref[4 + m] ^ other) == k)
                def _():
                    pltpu.make_async_copy(
                        sources[2 * m + k].at[rows, :], buf_ref.at[m, rows, :], sem.at[m, n]
                    ).start()

    for m in range(2):
        total = None
        for n, (start, size) in enumerate(spans):
            rows = pl.ds(start, size)
            if m == 0:
                pltpu.make_async_copy(h_hbm.at[rows, :], h_ref.at[rows, :], sem.at[2, n]).wait()
            pltpu.make_async_copy(sources[2 * m].at[rows, :], buf_ref.at[m, rows, :], sem.at[m, n]).wait()
            x, h = buf_ref[m, start : start + size, :], h_ref[start : start + size, :]
            term = lax.dot_general(x, h, (((0,), (0,)), ((), ())), preferred_element_type=F32)
            total = term if total is None else total + term
        outs[m][...] = total.astype(outs[m].dtype)


def weight_terms(meta, other, pairs, h, name, tokens=()):
    nodes, depth = pairs[0][0].shape
    columns = h.shape[1]
    pieces = 2 if nodes % 32 == 0 else 1
    spans = tuple((n * (nodes // pieces), nodes // pieces) for n in range(pieces))
    whole = pl.BlockSpec((depth, columns), lambda i, meta: (0, 0))
    return launch(
        functools.partial(weight_kernel, spans, other), (1,), [pl.BlockSpec(memory_space=pl.ANY)] * 5,
        [whole, whole, token_spec()],
        [jax.ShapeDtypeStruct((depth, columns), BF)] * 2 + [TOKEN], [*pairs[0], *pairs[1], h], name, prefetch=[meta],
        scratch=[
            pltpu.VMEM((2, nodes, depth), BF), pltpu.VMEM((nodes, columns), BF), pltpu.SemaphoreType.DMA((3, pieces))
        ],
        tokens=tokens, limit=60,
    )


def place_kernel(orders, meta_ref, *refs):
    out_ref, token_ref = refs[-2:]
    mark(token_ref)
    pieces = 1 << (len(orders[0]) - 2)
    size = out_ref.shape[0] // pieces
    for k in range(4):

        @pl.when(pl.program_id(0) == k)
        def _():
            mask = 0
            for b in orders[k // 2][1:-1]:
                mask = 2 * mask + meta_ref[4 + b]
            for n in range(pieces):
                start = pl.multiple_of((mask ^ n) * size, size)
                out_ref[pl.ds(start, size), :] = refs[k][n * size : (n + 1) * size, :].astype(F32)


def place_blocks(meta, blocks, orders, name, limit, tokens):
    depth, columns = blocks[0].shape
    return launch(
        functools.partial(place_kernel, orders), (4,), [pl.BlockSpec((depth, columns), lambda i, meta: (0, 0))] * 4,
        [
            pl.BlockSpec((depth, columns), lambda i, meta: (meta[0] ^ (i // 2 * 2) ^ (i % 2) ^ meta[4 + i // 2], 0)),
            token_spec(),
        ],
        [jax.ShapeDtypeStruct((4 * depth, columns), F32), TOKEN], blocks, name, prefetch=[meta], limit=limit,
        tokens=tokens,
    )


def after(value, *tokens):
    value, tokens = lax.optimization_barrier((value, tokens))
    return value, tokens


def across(value, axis, distance):
    size = lax.axis_size(axis)
    return lax.ppermute(value, axis, [(i, i ^ distance) for i in range(size)])


def slices_kernel(ids_ref, one_ref, two_ref, *refs):
    outs, (token_ref, sem) = refs[:6], refs[6:]
    mark(token_ref)
    depth = outs[0].shape[0]
    copies = []
    for n, out_ref in enumerate(outs):
        start = pl.multiple_of(ids_ref[1 + n % 3] * depth, depth)
        source = (one_ref, two_ref)[n // 3].at[pl.ds(start, depth), :]
        copies.append(pltpu.make_async_copy(source, out_ref, sem.at[n]))
    for copy in copies:
        copy.start()
    for copy in copies:
        copy.wait()


def weight_slices(ids, one, two):
    depth, columns = one.shape[0] // 4, one.shape[1]
    hbm = pl.BlockSpec(memory_space=pltpu.HBM)
    outs = launch(
        slices_kernel, (1,), [hbm, hbm], [hbm] * 6 + [token_spec()],
        [jax.ShapeDtypeStruct((depth, columns), one.dtype)] * 6 + [TOKEN], [one, two], "weight_slices",
        prefetch=[ids], scratch=[pltpu.SemaphoreType.DMA((6,))],
    )
    return outs[:3], outs[3:6], outs[6]


def weight_rows(slices):
    far = across(slices[1], "col", 2)
    other = across(slices[2], "col", 2)
    return [across(slices[0], "col", 1), far, across(other, "col", 1)], (far, other)


def fold_kernel(last, place, meta_ref, keep_ref, got_ref, *refs):
    mark(refs[-1])
    if last:
        refs[0][...] = (keep_ref[...].astype(F32) + got_ref[...].astype(F32)).astype(BF)
        return
    part = refs[0].shape[0]
    bit = meta_ref[4 + place]
    for out_ref, which in zip(refs[:2], (1 - bit, bit)):
        rows = pl.ds(pl.multiple_of(which * part, part), part)
        out_ref[...] = (keep_ref[rows, :].astype(F32) + got_ref[rows, :].astype(F32)).astype(BF)


def join_kernel(meta_ref, keep_ref, got_ref, out_ref, token_ref):
    mark(token_ref)
    part = keep_ref.shape[0]
    out_ref[:part, :] = keep_ref[...]
    out_ref[part:, :] = got_ref[...]


def small_call(kernel, meta, keep, got, rows, name, tokens):
    columns = keep.shape[1]
    whole = lambda r: pl.BlockSpec((r, columns), lambda i, bit: (0, 0))
    return launch(
        kernel, (1,), [whole(keep.shape[0])] * 2, [whole(r) for r in rows] + [token_spec()],
        [jax.ShapeDtypeStruct((r, columns), BF) for r in rows] + [TOKEN], [keep, got], name, prefetch=[meta], tokens=tokens,
    )


class RowSum:
    def __init__(self, axis, meta, terms, name, between=tuple):
        self.axis, self.meta, self.name = axis, meta, name
        self.bits = lax.axis_size(axis).bit_length() - 1
        self.stages = 2 * self.bits - 1
        self.orders = [list(range(self.bits)), list(range(1, self.bits)) + [0]]
        *self.send, self.sent = terms(1, ())
        *self.keep, self.kept = terms(0, (self.sent, *between()))
        self.stage = 0
        self.step(())

    def step(self, tokens):
        s, last = self.stage, self.bits - 1
        self.stage += 1
        started = []
        for n in range(2):
            rows = self.keep[n].shape[0]
            call = lambda kernel, sizes: small_call(
                kernel, self.meta, self.keep[n], self.got[n], sizes, f"{self.name}_{n}_{s}", tokens
            )
            if 0 < s < last:
                fold = functools.partial(fold_kernel, False, self.orders[n][s])
                self.send[n], self.keep[n], token = call(fold, [rows // 2] * 2)
            elif s == last or s == last + 1:
                self.keep[n], token = call(functools.partial(fold_kernel, True, 0), [rows])
            elif s > last + 1:
                self.keep[n], token = call(join_kernel, [2 * rows])
            if s > 0:
                started.append(token)
        level = s if s <= last else 2 * last - s
        moved = self.send if s < last else self.keep
        self.got = [across(moved[n], self.axis, 1 << self.orders[n][level]) for n in range(2)]
        return tuple(started)

    def next(self, *tokens):
        return self.step(tokens) if self.stage < self.stages else tokens

    def placed(self, limit, tokens=()):
        while self.stage < self.stages:
            self.step(())
        blocks = [v for n in range(2) for v in (self.keep[n], self.got[n])]
        return place_blocks(self.meta, blocks, self.orders, f"place_{self.name}", limit, tokens)


def local(
    features,
    neighbours,
    node_valid,
    weight_one,
    gamma_one,
    beta_one,
    weight_two,
    gamma_two,
    beta_two,
    cotangent,
):
    nodes, columns = features.shape
    slots = nodes // SLOT
    big = slots // 2 if slots % 2 == 0 else slots
    q = lax.axis_index("col")
    place = lax.axis_index("row")
    bits = [(place >> b) & 1 for b in range(lax.axis_size("row").bit_length() - 1)]
    ids = jnp.stack([q, q ^ 1, q ^ 2, q ^ 3, *bits]).astype(jnp.int32)
    g1, b1, g2, b2 = (v.reshape(1, columns) for v in (gamma_one, beta_one, gamma_two, beta_two))

    far_one = across(features, "col", 2)
    near_one = across(features, "col", 1)
    *tiles, tiles_token = build_tiles(neighbours, node_valid)
    val = tiles[3]
    slices_one, slices_two, slices_token = weight_slices(ids, weight_one, weight_two)
    early, token = half(ids, big, features, near_one, [weight_block(weight_one, b) for b in (0, 1)], False, "half_one")
    far_one, tokens = after(far_one, token, tiles_token, slices_token)
    beyond_one = across(far_one, "col", 1)
    lin_one, stats = forward(ids, big, early, far_one, beyond_one, weight_one, tiles, "forward_one", tokens)
    norm_one = (small_gather(stats, "row"), g1, b1)

    hidden, _ = rows_call(result_kernel, big, [lin_one], [val], norm_one, BF, [], "hidden")
    far_two, near_two = across(hidden, "col", 2), across(hidden, "col", 1)
    early, token = half(ids, big, hidden, near_two, [weight_block(weight_two, b) for b in (0, 1)], False, "half_two")
    far_two, tokens = after(far_two, token)
    beyond_two = across(far_two, "col", 1)
    slices_two, (far_two,) = after(slices_two, far_two)
    rows_two, crossing = weight_rows(slices_two)
    lin_two, stats = forward(ids, big, early, far_two, beyond_two, weight_two, tiles, "forward_two", tokens)
    norm_two = (small_gather(stats, "row"), g2, b2)

    sums = rows_call(
        sums_kernel, big, [lin_two, cotangent], [val], norm_two, None, [pltpu.VMEM((2, 8, columns), F32)], "sums_two"
    )
    grads_two = small_gather(sums, "row")
    turned, _ = turn_call(True, big, lin_two, cotangent, tiles, norm_two, grads_two, "turn_two", crossing)
    far, near = across(turned, "col", 2), across(turned, "col", 1)

    def terms_two(other, tokens, h=turned):
        return weight_terms(ids, other, ((hidden, near_two), (far_two, beyond_two)), h, "terms_two", tokens)

    sum_two = RowSum("row", ids, terms_two, "two")
    weights = [weight_block(weight_two, 0), whole_block(rows_two[0])]
    early, token = half(ids, big, turned, near, weights, True, "half_back_two", (sum_two.kept,))
    far, tokens = after(far, *sum_two.next(*sum_two.next(token)))
    beyond = across(far, "col", 1)
    slices_one, (far,) = after(slices_one, far)
    rows_one, crossing = weight_rows(slices_one)
    grad_one, sums = backward(big, early, far, beyond, rows_two[1:], lin_one, norm_one, "backward_two", tokens)
    tokens = (*crossing, *sum_two.next(*sum_two.next(sums)))
    grads_one = small_gather(sums, "row")

    turned, _ = turn_call(False, big, lin_one, grad_one, tiles, norm_one, grads_one, "turn_one", tokens)
    far, near = across(turned, "col", 2), across(turned, "col", 1)

    def terms_one(other, tokens, h=turned):
        return weight_terms(ids, other, ((features, near_one), (far_one, beyond_one)), h, "terms_one", tokens)

    sum_one = RowSum("row", ids, terms_one, "one")
    weights = [weight_block(weight_one, 0), whole_block(rows_one[0])]
    early, token = half(ids, big, turned, near, weights, True, "half_back_one", (sum_one.kept,))
    output, token = rows_call(result_kernel, big, [lin_two], [val], norm_two, F32, [], "output", sum_one.next(token))
    grad_weight_two, token = sum_two.placed(60, (token,))
    sum_one.next(token)
    far, tokens = after(far, *sum_one.next())
    beyond = across(far, "col", 1)
    grad_features, token = backward(big, early, far, beyond, rows_one[1:], None, None, "backward_one", tokens)
    while sum_one.stage < sum_one.stages - 1:
        sum_one.next()
    sum_one.next(token)
    grad_weight_one, _ = sum_one.placed(24)

    sums_one, sums_two = jnp.sum(grads_one, axis=0), jnp.sum(grads_two, axis=0)
    return (
        output,
        grad_features,
        grad_weight_one,
        sums_one[1],
        sums_one[0],
        grad_weight_two,
        sums_two[1],
        sums_two[0],
    )


def solution(mesh):
    placed = (
        P("row", "col"),
        P("row", None),
        P("row"),
        P(None, "col"),
        P("col"),
        P("col"),
        P(None, "col"),
        P("col"),
        P("col"),
        P("row", "col"),
    )
    return jax.shard_map(
        local,
        mesh=mesh,
        in_specs=placed,
        out_specs=(
            P("row", "col"),
            P("row", "col"),
            P(None, "col"),
            P("col"),
            P("col"),
            P(None, "col"),
            P("col"),
            P("col"),
        ),
        check_vma=False,
    )
```

```python
import functools

import jax
import jax.numpy as jnp
from jax import lax
from jax.experimental import pallas as pl
from jax.experimental.pallas import tpu as pltpu
from jax.sharding import PartitionSpec as P

SLOT = 128
NBR = 32
PART = 32
LANES = 128
EPSILON = 1e-05
ANY = pl.BlockSpec(memory_space=pl.ANY)
BF = jnp.bfloat16
F32 = jnp.float32


def params(limit):
    return pltpu.CompilerParams(dimension_semantics=("arbitrary",), vmem_limit_bytes=limit << 20)


SMALL = pl.CostEstimate(flops=1000000, bytes_accessed=1000, transcendentals=0)


TOKEN = jax.ShapeDtypeStruct((8, LANES), F32)


def token_spec():
    return pl.BlockSpec((8, LANES), lambda i, *_: (0, 0))


def mark(token_ref):
    token_ref[...] = jnp.zeros_like(token_ref)


def launch(kernel, grid, ins, outs, shapes, args, name, prefetch=(), scratch=(), tokens=(), limit=24):
    count = len(prefetch) + len(args)

    def body(*refs):
        kernel(*refs[:count], *refs[count + len(tokens) :])

    return pl.pallas_call(
        body,
        grid_spec=pltpu.PrefetchScalarGridSpec(
            num_scalar_prefetch=len(prefetch),
            grid=grid,
            in_specs=[*ins, *[pl.BlockSpec(memory_space=pl.ANY)] * len(tokens)],
            out_specs=outs,
            scratch_shapes=list(scratch),
        ),
        out_shape=shapes,
        compiler_params=params(limit),
        cost_estimate=SMALL,
        name=name,
    )(*prefetch, *args, *tokens)


def dot(a, b):
    return jnp.dot(a, b, preferred_element_type=F32)


def dot_t(a, b):
    return lax.dot_general(a, b, (((1,), (1,)), ((), ())), preferred_element_type=F32)


def wide(v, columns):
    return jnp.concatenate([v] * (columns // LANES), axis=1)


def tiles_kernel(nbr_ref, valid_ref, h_ref, ht_ref, inv_ref, val_ref, token_ref):
    mark(token_ref)
    entries = nbr_ref[0]
    rows = lax.broadcasted_iota(jnp.int32, (SLOT, SLOT), 0)
    cols = lax.broadcasted_iota(jnp.int32, (SLOT, SLOT), 1)
    hits = jnp.zeros((SLOT, SLOT), F32)
    degree = jnp.zeros((1, SLOT), F32)
    for k in range(entries.shape[0]):
        one = entries[k : k + 1, :]
        hits += (one == rows).astype(F32)
        degree += (one >= 0).astype(F32)
    eye = (rows == cols).astype(F32)
    joined = hits + eye
    counts = joined + joined * eye
    ht_ref[0] = wide(counts.astype(BF), 2 * SLOT)
    h_ref[0] = wide(counts.T.astype(BF), 2 * SLOT)
    valid = valid_ref[0].astype(F32)
    inv_ref[0] = jnp.broadcast_to(valid / (degree + 1.0), (SLOT, SLOT)).T
    val_ref[0] = jnp.broadcast_to(valid, (SLOT, SLOT)).T


def build_tiles(neighbours, node_valid):
    slots = neighbours.shape[0] // SLOT
    turned = neighbours.reshape(slots, SLOT, NBR).transpose(0, 2, 1)
    square = pl.BlockSpec((1, SLOT, SLOT), lambda i: (i, 0, 0))
    double = pl.BlockSpec((1, SLOT, 2 * SLOT), lambda i: (i, 0, 0))
    return launch(
        tiles_kernel, (slots,),
        [pl.BlockSpec((1, NBR, SLOT), lambda i: (i, 0, 0)), pl.BlockSpec((1, 1, SLOT), lambda i: (i, 0, 0))],
        [double, double, square, square, token_spec()],
        [jax.ShapeDtypeStruct((slots, SLOT, 2 * SLOT), BF)] * 2 + [jax.ShapeDtypeStruct((slots, SLOT, SLOT), F32)] * 2 + [TOKEN],
        [turned, node_valid.reshape(slots, 1, SLOT)], "tiles",
    )


def combine(g_ref):
    mref, first, second, count = (g_ref[:, k, :] for k in range(4))
    shift = first / count
    mean_each = mref + shift
    spread_each = second - first * shift
    total = jnp.sum(count, axis=0, keepdims=True)
    mean = jnp.sum(count * mean_each, axis=0, keepdims=True) / total
    away = mean_each - mean
    variance = jnp.sum(spread_each + count * away * away, axis=0, keepdims=True) / total
    return total, mean, lax.rsqrt(variance + EPSILON)


def small_gather(copies, axis):
    return lax.all_to_all(copies, axis, split_axis=0, concat_axis=0, tiled=True)


def copies_shape(columns):
    return (lax.axis_size("row"), 8, columns)


def spread_rows(out_ref, rows):
    block = jnp.concatenate([*rows, jnp.zeros((8 - len(rows), out_ref.shape[2]), F32)], axis=0)

    def one(n, carry):
        out_ref[n] = block
        return carry

    lax.fori_loop(0, out_ref.shape[0], one, 0)


def split(value):
    high = value.astype(BF)
    return high, (value - high.astype(F32)).astype(BF)


def fold(value):
    return jnp.sum(value.reshape(value.shape[0] // 8, 8, value.shape[1]), axis=0)


def at(ref, k):
    return ref[k : k + 1, :]


def put(ref, k, value):
    ref[k : k + 1, :] = value


def half(ids, big, sources, weights, turned, name, tokens=(), early=None):
    nodes, depth = sources[0].shape
    columns = weights[0][0].shape[1]
    rows = big * SLOT
    n = len(sources)
    before = [] if early is None else [early]
    product = dot_t if turned else dot

    def kernel(ids_ref, *refs):
        out_ref, token_ref = refs[-2:]
        mark(token_ref)
        terms = [product(x_ref[...], w_ref[...]) for x_ref, w_ref in zip(refs[:n], refs[n : 2 * n])]
        terms += [e_ref[...] for e_ref in refs[2 * n : -2]]
        out_ref[...] = sum(terms[1:], terms[0])

    flat = pl.BlockSpec((rows, depth), lambda i, ids: (i, 0))
    wide_flat = pl.BlockSpec((rows, columns), lambda i, ids: (i, 0))
    return launch(
        kernel, (nodes // rows,), [flat] * n + [spec for _, spec in weights] + [wide_flat for _ in before],
        [wide_flat, token_spec()], [jax.ShapeDtypeStruct((nodes, columns), F32), TOKEN],
        [*sources, *[w for w, _ in weights], *before], name, prefetch=[ids], tokens=tokens,
    )


def weight_block(weight, b):
    depth = weight.shape[0] // 4
    return weight, pl.BlockSpec((depth, weight.shape[1]), lambda i, ids: (ids[b], 0))


def whole_block(piece):
    return piece, pl.BlockSpec(piece.shape, lambda i, ids: (0, 0))


def each_part(big, body, part=32):
    for s in range(big):
        for r in range(SLOT // part):
            body(s, slice(r * part, (r + 1) * part), slice(s * SLOT + r * part, s * SLOT + (r + 1) * part))


def forward_kernel(big, ids_ref, early_ref, y_ref, w_beyond, h_ref, inv_ref, val_ref, lin_ref, st_ref, tot_ref, acc_ref, ref_ref):
    i = pl.program_id(0)
    columns = lin_ref.shape[1]
    tot_ref[...] = early_ref[...] + dot(y_ref[...], w_beyond[...])

    def mixed(s):
        high, low = split(tot_ref[s * SLOT : (s + 1) * SLOT, :])
        return dot(h_ref[s], jnp.concatenate([high, low], axis=0)) * wide(inv_ref[s], columns)

    @pl.when(i == 0)
    def _():
        acc_ref[...] = jnp.zeros_like(acc_ref)
        v = val_ref[0]
        count = jnp.sum(v, axis=0, keepdims=True)
        put(ref_ref, 0, jnp.sum(mixed(0) * wide(v, columns), axis=0, keepdims=True) / wide(count, columns))

    mref = at(ref_ref, 0)
    for s in range(big):
        lin_ref[s * SLOT : (s + 1) * SLOT, :] = mixed(s)
        for r in range(SLOT // 32):
            v = val_ref[s, r * 32 : (r + 1) * 32, :]
            away = (lin_ref[s * SLOT + r * 32 : s * SLOT + (r + 1) * 32, :] - mref) * wide(v, columns)
            acc_ref[0] += fold(away)
            acc_ref[1] += fold(away * away)
            acc_ref[2, :, :LANES] += fold(v)

    @pl.when(i == pl.num_programs(0) - 1)
    def _():
        first, second = (jnp.sum(acc_ref[k], axis=0, keepdims=True) for k in range(2))
        count = wide(jnp.sum(acc_ref[2, :, :LANES], axis=0, keepdims=True), columns)
        spread_rows(st_ref, (at(ref_ref, 0), first, second, count))


def forward(ids, big, early, beyond, weight, tiles, name, tokens=()):
    h, _, inv, val = tiles
    nodes, columns = early.shape
    rows = big * SLOT
    flat = pl.BlockSpec((rows, columns), lambda i, ids: (i, 0))
    tile = pl.BlockSpec((big, SLOT, SLOT), lambda i, ids: (i, 0, 0))
    double = pl.BlockSpec((big, SLOT, 2 * SLOT), lambda i, ids: (i, 0, 0))
    _, block = weight_block(weight, 3)
    return launch(
        functools.partial(forward_kernel, big), (nodes // rows,),
        [flat, flat, block, double, tile, tile],
        [flat, pl.BlockSpec(copies_shape(columns), lambda i, ids: (0, 0, 0))],
        [jax.ShapeDtypeStruct((nodes, columns), F32), jax.ShapeDtypeStruct(copies_shape(columns), F32)],
        [early, beyond, weight, h, inv, val], name, prefetch=[ids],
        scratch=[pltpu.VMEM((rows, columns), F32), pltpu.VMEM((3, 8, columns), F32), pltpu.VMEM((8, columns), F32)],
        tokens=tokens,
    )


def columns_of(g_ref, gamma_ref, beta_ref, co_ref):
    total, mean, inv_std = combine(g_ref)
    put(co_ref, 0, mean)
    put(co_ref, 1, 0.5 * gamma_ref[...] * inv_std)
    put(co_ref, 2, 0.5 * beta_ref[...])
    put(co_ref, 3, inv_std)
    put(co_ref, 4, total)


def silu_of(away, co_ref):
    u = away * at(co_ref, 1) + at(co_ref, 2)
    return u + u * jnp.tanh(u)


def double_slope(away, co_ref):
    u = away * at(co_ref, 1) + at(co_ref, 2)
    t = jnp.tanh(u)
    return (1.0 + t) * (1.0 + u * (1.0 - t))


def result_kernel(big, lin_ref, val_ref, g_ref, gamma_ref, beta_ref, out_ref, token_ref, co_ref):
    mark(token_ref)

    @pl.when(pl.program_id(0) == 0)
    def _():
        columns_of(g_ref, gamma_ref, beta_ref, co_ref)

    def part(s, inner, rows):
        value = silu_of(lin_ref[rows, :] - at(co_ref, 0), co_ref)
        out_ref[rows, :] = (wide(val_ref[s, inner, :], lin_ref.shape[1]) * value).astype(out_ref.dtype)

    each_part(big, part)


def sums_kernel(big, lin_ref, cot_ref, val_ref, g_ref, gamma_ref, beta_ref, st_ref, co_ref, acc_ref):
    @pl.when(pl.program_id(0) == 0)
    def _():
        columns_of(g_ref, gamma_ref, beta_ref, co_ref)
        acc_ref[...] = jnp.zeros_like(acc_ref)

    def part(s, inner, rows):
        away = lin_ref[rows, :] - at(co_ref, 0)
        valid = wide(val_ref[s, inner, :], lin_ref.shape[1])
        grad = cot_ref[rows, :].astype(F32) * valid * double_slope(away, co_ref)
        acc_ref[0] += fold(grad)
        acc_ref[1] += fold(grad * away)

    each_part(big, part)
    finish_sums(st_ref, co_ref, acc_ref)


def finish_sums(st_ref, co_ref, acc_ref):
    @pl.when(pl.program_id(0) == pl.num_programs(0) - 1)
    def _():
        grad_beta = 0.5 * jnp.sum(acc_ref[0], axis=0, keepdims=True)
        grad_gamma = 0.5 * at(co_ref, 3) * jnp.sum(acc_ref[1], axis=0, keepdims=True)
        spread_rows(st_ref, (grad_beta, grad_gamma))


def turn_kernel(from_cot, big, lin_ref, grad_ref, inv_ref, ht_ref, g_ref, sg_ref, gamma_ref, beta_ref, out_ref, token_ref, co_ref, lg_ref):
    mark(token_ref)

    @pl.when(pl.program_id(0) == 0)
    def _():
        columns_of(g_ref, gamma_ref, beta_ref, co_ref)
        sg = sg_ref[...]
        twice = 2.0 / at(co_ref, 4)
        put(co_ref, 5, twice * jnp.sum(sg[:, 0, :], axis=0, keepdims=True))
        put(co_ref, 6, twice * at(co_ref, 3) * jnp.sum(sg[:, 1, :], axis=0, keepdims=True))

    columns = lin_ref.shape[1]

    for s in range(big):
        for r in range(SLOT // PART):
            inner = slice(r * PART, (r + 1) * PART)
            rows = slice(s * SLOT + r * PART, s * SLOT + (r + 1) * PART)
            away = lin_ref[rows, :] - at(co_ref, 0)
            if from_cot:
                grad = grad_ref[rows, :].astype(F32) * double_slope(away, co_ref)
            else:
                grad = grad_ref[rows, :]
            weight = wide(inv_ref[s, inner, :], columns)
            high, low = split(weight * (grad - (at(co_ref, 5) + away * at(co_ref, 6))))
            lg_ref[s, inner, :] = high
            lg_ref[s, SLOT + r * PART : SLOT + (r + 1) * PART, :] = low
        out_ref[s * SLOT : (s + 1) * SLOT, :] = (dot(ht_ref[s], lg_ref[s]) * at(co_ref, 1)).astype(BF)


def rows_call(kernel, big, arrays, tiles, smalls, out_dtype, scratch, name, tokens=(), limit=24):
    rows = big * SLOT
    nodes, columns = arrays[0].shape
    flat = pl.BlockSpec((rows, columns), lambda i: (i, 0))
    ins = [flat for _ in arrays]
    ins += [pl.BlockSpec((big,) + t.shape[1:], lambda i: (i, 0, 0)) for t in tiles]
    ins += [pl.BlockSpec(s.shape, lambda i, n=s.ndim: (0,) * n) for s in smalls]
    if out_dtype is None:
        out_spec = pl.BlockSpec(copies_shape(columns), lambda i: (0, 0, 0))
        out_shape = jax.ShapeDtypeStruct(copies_shape(columns), F32)
    else:
        out_spec = [flat, token_spec()]
        out_shape = [jax.ShapeDtypeStruct((nodes, columns), out_dtype), TOKEN]
    return launch(
        functools.partial(kernel, big), (nodes // rows,), ins, out_spec, out_shape, [*arrays, *tiles, *smalls], name,
        scratch=[pltpu.VMEM((8, columns), F32)] + scratch, tokens=tokens, limit=limit,
    )


def turn_call(from_cot, big, lin, grad, tiles, norm, sums, name, tokens=()):
    _, ht, inv, _ = tiles
    return rows_call(
        functools.partial(turn_kernel, from_cot), big, [lin, grad], [inv, ht], [norm[0], sums, *norm[1:]], BF,
        [pltpu.VMEM((big, 2 * SLOT, lin.shape[1]), BF)], name, tokens, 60,
    )


def backward_kernel(big, last, early_ref, y_ref, w_beyond, *refs):
    total = early_ref[...] + dot_t(y_ref[...], w_beyond[...])
    if last:
        refs[-2][...] = total
        mark(refs[-1])
        return
    lin_ref, g_ref, gamma_ref, beta_ref, out_ref, st_ref, co_ref, acc_ref = refs
    out_ref[...] = total

    @pl.when(pl.program_id(0) == 0)
    def _():
        columns_of(g_ref, gamma_ref, beta_ref, co_ref)
        acc_ref[...] = jnp.zeros_like(acc_ref)

    def part(s, inner, rows):
        away = lin_ref[rows, :] - at(co_ref, 0)
        grad = out_ref[rows, :] * double_slope(away, co_ref)
        out_ref[rows, :] = grad
        acc_ref[0] += fold(grad)
        acc_ref[1] += fold(grad * away)

    each_part(big, part)
    finish_sums(st_ref, co_ref, acc_ref)


def backward(big, early, beyond, piece, lin, norm, name, tokens=()):
    nodes, columns = early.shape
    rows = big * SLOT
    last = norm is None
    flat = pl.BlockSpec((rows, columns), lambda i: (i, 0))
    fixed = lambda s: pl.BlockSpec(s.shape, lambda i, n=s.ndim: (0,) * n)
    ins = [flat, flat, fixed(piece)]
    args = [early, beyond, piece]
    out_specs = [flat]
    out_shape = [jax.ShapeDtypeStruct((nodes, columns), F32)]
    scratch = []
    if last:
        out_specs.append(token_spec())
        out_shape.append(TOKEN)
    else:
        ins += [flat, *map(fixed, norm)]
        args += [lin, *norm]
        out_specs.append(pl.BlockSpec(copies_shape(columns), lambda i: (0, 0, 0)))
        out_shape.append(jax.ShapeDtypeStruct(copies_shape(columns), F32))
        scratch = [pltpu.VMEM((8, columns), F32), pltpu.VMEM((2, 8, columns), F32)]
    return launch(
        functools.partial(backward_kernel, big, last), (nodes // rows,), ins, out_specs, out_shape, args, name,
        scratch=scratch, tokens=tokens,
    )


def weight_kernel(spans, other, meta_ref, *refs):
    sources, h_hbm, outs, (token_ref, buf_ref, h_ref, sem) = refs[:4], refs[4], refs[5:7], refs[7:]
    mark(token_ref)
    for m in range(2):
        for n, span in enumerate(spans):
            rows = pl.ds(*span)
            if m == 0:
                pltpu.make_async_copy(h_hbm.at[rows, :], h_ref.at[rows, :], sem.at[2, n]).start()
            for k in range(2):

                @pl.when((meta_ref[4 + m] ^ other) == k)
                def _():
                    pltpu.make_async_copy(
                        sources[2 * m + k].at[rows, :], buf_ref.at[m, rows, :], sem.at[m, n]
                    ).start()

    for m in range(2):
        total = None
        for n, (start, size) in enumerate(spans):
            rows = pl.ds(start, size)
            if m == 0:
                pltpu.make_async_copy(h_hbm.at[rows, :], h_ref.at[rows, :], sem.at[2, n]).wait()
            pltpu.make_async_copy(sources[2 * m].at[rows, :], buf_ref.at[m, rows, :], sem.at[m, n]).wait()
            x, h = buf_ref[m, start : start + size, :], h_ref[start : start + size, :]
            term = lax.dot_general(x, h, (((0,), (0,)), ((), ())), preferred_element_type=F32)
            total = term if total is None else total + term
        outs[m][...] = total.astype(outs[m].dtype)


def weight_terms(meta, other, pairs, h, name, tokens=()):
    nodes, depth = pairs[0][0].shape
    columns = h.shape[1]
    pieces = 2 if nodes % 32 == 0 else 1
    spans = tuple((n * (nodes // pieces), nodes // pieces) for n in range(pieces))
    whole = pl.BlockSpec((depth, columns), lambda i, meta: (0, 0))
    return launch(
        functools.partial(weight_kernel, spans, other), (1,), [pl.BlockSpec(memory_space=pl.ANY)] * 5,
        [whole, whole, token_spec()],
        [jax.ShapeDtypeStruct((depth, columns), BF)] * 2 + [TOKEN], [*pairs[0], *pairs[1], h], name, prefetch=[meta],
        scratch=[
            pltpu.VMEM((2, nodes, depth), BF), pltpu.VMEM((nodes, columns), BF), pltpu.SemaphoreType.DMA((3, pieces))
        ],
        tokens=tokens, limit=60,
    )


def place_kernel(orders, meta_ref, *refs):
    out_ref, token_ref = refs[-2:]
    mark(token_ref)
    pieces = 1 << (len(orders[0]) - 2)
    size = out_ref.shape[0] // pieces
    for k in range(4):

        @pl.when(pl.program_id(0) == k)
        def _():
            mask = 0
            for b in orders[k // 2][1:-1]:
                mask = 2 * mask + meta_ref[4 + b]
            for n in range(pieces):
                start = pl.multiple_of((mask ^ n) * size, size)
                out_ref[pl.ds(start, size), :] = refs[k][n * size : (n + 1) * size, :].astype(F32)


def place_blocks(meta, blocks, orders, name, limit, tokens):
    depth, columns = blocks[0].shape
    return launch(
        functools.partial(place_kernel, orders), (4,), [pl.BlockSpec((depth, columns), lambda i, meta: (0, 0))] * 4,
        [
            pl.BlockSpec((depth, columns), lambda i, meta: (meta[0] ^ (i // 2 * 2) ^ (i % 2) ^ meta[4 + i // 2], 0)),
            token_spec(),
        ],
        [jax.ShapeDtypeStruct((4 * depth, columns), F32), TOKEN], blocks, name, prefetch=[meta], limit=limit,
        tokens=tokens,
    )


def after(value, *tokens):
    value, tokens = lax.optimization_barrier((value, tokens))
    return value, tokens


def across(value, axis, distance):
    size = lax.axis_size(axis)
    return lax.ppermute(value, axis, [(i, i ^ distance) for i in range(size)])


def slices_kernel(ids_ref, one_ref, two_ref, *refs):
    outs, (token_ref, sem) = refs[:6], refs[6:]
    mark(token_ref)
    depth = outs[0].shape[0]
    copies = []
    for n, out_ref in enumerate(outs):
        start = pl.multiple_of(ids_ref[1 + n % 3] * depth, depth)
        source = (one_ref, two_ref)[n // 3].at[pl.ds(start, depth), :]
        copies.append(pltpu.make_async_copy(source, out_ref, sem.at[n]))
    for copy in copies:
        copy.start()
    for copy in copies:
        copy.wait()


def weight_slices(ids, one, two):
    depth, columns = one.shape[0] // 4, one.shape[1]
    hbm = pl.BlockSpec(memory_space=pltpu.HBM)
    outs = launch(
        slices_kernel, (1,), [hbm, hbm], [hbm] * 6 + [token_spec()],
        [jax.ShapeDtypeStruct((depth, columns), one.dtype)] * 6 + [TOKEN], [one, two], "weight_slices",
        prefetch=[ids], scratch=[pltpu.SemaphoreType.DMA((6,))],
    )
    return outs[:3], outs[3:6], outs[6]


def weight_rows(slices):
    far = across(slices[1], "col", 2)
    other = across(slices[2], "col", 2)
    return [across(slices[0], "col", 1), far, across(other, "col", 1)], (far, other)


def fold_kernel(last, place, meta_ref, keep_ref, got_ref, *refs):
    mark(refs[-1])
    if last:
        refs[0][...] = (keep_ref[...].astype(F32) + got_ref[...].astype(F32)).astype(BF)
        return
    part = refs[0].shape[0]
    bit = meta_ref[4 + place]
    for out_ref, which in zip(refs[:2], (1 - bit, bit)):
        rows = pl.ds(pl.multiple_of(which * part, part), part)
        out_ref[...] = (keep_ref[rows, :].astype(F32) + got_ref[rows, :].astype(F32)).astype(BF)


def join_kernel(meta_ref, keep_ref, got_ref, out_ref, token_ref):
    mark(token_ref)
    part = keep_ref.shape[0]
    out_ref[:part, :] = keep_ref[...]
    out_ref[part:, :] = got_ref[...]


def small_call(kernel, meta, keep, got, rows, name, tokens):
    columns = keep.shape[1]
    whole = lambda r: pl.BlockSpec((r, columns), lambda i, bit: (0, 0))
    return launch(
        kernel, (1,), [whole(keep.shape[0])] * 2, [whole(r) for r in rows] + [token_spec()],
        [jax.ShapeDtypeStruct((r, columns), BF) for r in rows] + [TOKEN], [keep, got], name, prefetch=[meta], tokens=tokens,
    )


class RowSum:
    def __init__(self, axis, meta, terms, name, between=tuple):
        self.axis, self.meta, self.name = axis, meta, name
        self.bits = lax.axis_size(axis).bit_length() - 1
        self.stages = 2 * self.bits - 1
        self.orders = [list(range(self.bits)), list(range(1, self.bits)) + [0]]
        *self.send, self.sent = terms(1, ())
        *self.keep, self.kept = terms(0, (self.sent, *between()))
        self.stage = 0
        self.step(())

    def step(self, tokens):
        s, last = self.stage, self.bits - 1
        self.stage += 1
        started = []
        for n in range(2):
            rows = self.keep[n].shape[0]
            call = lambda kernel, sizes: small_call(
                kernel, self.meta, self.keep[n], self.got[n], sizes, f"{self.name}_{n}_{s}", tokens
            )
            if 0 < s < last:
                fold = functools.partial(fold_kernel, False, self.orders[n][s])
                self.send[n], self.keep[n], token = call(fold, [rows // 2] * 2)
            elif s == last or s == last + 1:
                self.keep[n], token = call(functools.partial(fold_kernel, True, 0), [rows])
            elif s > last + 1:
                self.keep[n], token = call(join_kernel, [2 * rows])
            if s > 0:
                started.append(token)
        level = s if s <= last else 2 * last - s
        moved = self.send if s < last else self.keep
        self.got = [across(moved[n], self.axis, 1 << self.orders[n][level]) for n in range(2)]
        return tuple(started)

    def next(self, *tokens):
        return self.step(tokens) if self.stage < self.stages else tokens

    def placed(self, limit, tokens=()):
        while self.stage < self.stages:
            self.step(())
        blocks = [v for n in range(2) for v in (self.keep[n], self.got[n])]
        return place_blocks(self.meta, blocks, self.orders, f"place_{self.name}", limit, tokens)


def local(
    features,
    neighbours,
    node_valid,
    weight_one,
    gamma_one,
    beta_one,
    weight_two,
    gamma_two,
    beta_two,
    cotangent,
):
    nodes, columns = features.shape
    slots = nodes // SLOT
    big = slots // 2 if slots % 2 == 0 else slots
    q = lax.axis_index("col")
    place = lax.axis_index("row")
    bits = [(place >> b) & 1 for b in range(lax.axis_size("row").bit_length() - 1)]
    ids = jnp.stack([q, q ^ 1, q ^ 2, q ^ 3, *bits]).astype(jnp.int32)
    g1, b1, g2, b2 = (v.reshape(1, columns) for v in (gamma_one, beta_one, gamma_two, beta_two))

    far_one = across(features, "col", 2)
    near_one = across(features, "col", 1)
    *tiles, tiles_token = build_tiles(neighbours, node_valid)
    val = tiles[3]
    slices_one, slices_two, slices_token = weight_slices(ids, weight_one, weight_two)
    early, token = half(ids, big, [features, near_one], [weight_block(weight_one, b) for b in (0, 1)], False, "half_one")
    far_one, tokens = after(far_one, token, tiles_token, slices_token)
    beyond_one = across(far_one, "col", 1)
    early, _ = half(ids, big, [far_one], [weight_block(weight_one, 2)], False, "far_half_one", tokens, early)
    lin_one, stats = forward(ids, big, early, beyond_one, weight_one, tiles, "forward_one", tokens)
    norm_one = (small_gather(stats, "row"), g1, b1)

    hidden, _ = rows_call(result_kernel, big, [lin_one], [val], norm_one, BF, [], "hidden")
    far_two, near_two = across(hidden, "col", 2), across(hidden, "col", 1)
    early, token = half(ids, big, [hidden, near_two], [weight_block(weight_two, b) for b in (0, 1)], False, "half_two")
    far_two, tokens = after(far_two, token)
    beyond_two = across(far_two, "col", 1)
    slices_two, (far_two,) = after(slices_two, far_two)
    rows_two, crossing = weight_rows(slices_two)
    early, _ = half(ids, big, [far_two], [weight_block(weight_two, 2)], False, "far_half_two", tokens, early)
    lin_two, stats = forward(ids, big, early, beyond_two, weight_two, tiles, "forward_two", tokens)
    norm_two = (small_gather(stats, "row"), g2, b2)

    sums = rows_call(
        sums_kernel, big, [lin_two, cotangent], [val], norm_two, None, [pltpu.VMEM((2, 8, columns), F32)], "sums_two"
    )
    grads_two = small_gather(sums, "row")
    turned, _ = turn_call(True, big, lin_two, cotangent, tiles, norm_two, grads_two, "turn_two", crossing)
    far, near = across(turned, "col", 2), across(turned, "col", 1)

    def terms_two(other, tokens, h=turned):
        return weight_terms(ids, other, ((hidden, near_two), (far_two, beyond_two)), h, "terms_two", tokens)

    sum_two = RowSum("row", ids, terms_two, "two")
    weights = [weight_block(weight_two, 0), whole_block(rows_two[0])]
    early, token = half(ids, big, [turned, near], weights, True, "half_back_two", (sum_two.kept,))
    far, tokens = after(far, *sum_two.next(*sum_two.next(token)))
    beyond = across(far, "col", 1)
    slices_one, (far,) = after(slices_one, far)
    rows_one, crossing = weight_rows(slices_one)
    early, _ = half(ids, big, [far], [whole_block(rows_two[1])], True, "far_half_back_two", tokens, early)
    grad_one, sums = backward(big, early, beyond, rows_two[2], lin_one, norm_one, "backward_two", tokens)
    tokens = (*crossing, *sum_two.next(*sum_two.next(sums)))
    grads_one = small_gather(sums, "row")

    turned, _ = turn_call(False, big, lin_one, grad_one, tiles, norm_one, grads_one, "turn_one", tokens)
    far, near = across(turned, "col", 2), across(turned, "col", 1)

    def terms_one(other, tokens, h=turned):
        return weight_terms(ids, other, ((features, near_one), (far_one, beyond_one)), h, "terms_one", tokens)

    sum_one = RowSum("row", ids, terms_one, "one", lambda: tuple(sum_two.got))
    weights = [weight_block(weight_one, 0), whole_block(rows_one[0])]
    early, token = half(ids, big, [turned, near], weights, True, "half_back_one", sum_one.next())
    output, token = rows_call(result_kernel, big, [lin_two], [val], norm_two, F32, [], "output", (token,))
    started = sum_one.next(token)
    far, tokens = after(far, *started)
    beyond = across(far, "col", 1)
    grad_weight_two, token = sum_two.placed(60, started)
    tokens = (*tokens, *sum_one.next(token))
    early, _ = half(ids, big, [far], [whole_block(rows_one[1])], True, "far_half_back_one", tokens, early)
    grad_features, token = backward(big, early, beyond, rows_one[2], None, None, "backward_one", tokens)
    while sum_one.stage < sum_one.stages - 1:
        sum_one.next()
    sum_one.next(token)
    grad_weight_one, _ = sum_one.placed(24)

    sums_one, sums_two = jnp.sum(grads_one, axis=0), jnp.sum(grads_two, axis=0)
    return (
        output,
        grad_features,
        grad_weight_one,
        sums_one[1],
        sums_one[0],
        grad_weight_two,
        sums_two[1],
        sums_two[0],
    )


def solution(mesh):
    placed = (
        P("row", "col"),
        P("row", None),
        P("row"),
        P(None, "col"),
        P("col"),
        P("col"),
        P(None, "col"),
        P("col"),
        P("col"),
        P("row", "col"),
    )
    return jax.shard_map(
        local,
        mesh=mesh,
        in_specs=placed,
        out_specs=(
            P("row", "col"),
            P("row", "col"),
            P(None, "col"),
            P("col"),
            P("col"),
            P(None, "col"),
            P("col"),
            P("col"),
        ),
        check_vma=False,
    )
```

```python
import functools

import jax
import jax.numpy as jnp
from jax import lax
from jax.experimental import pallas as pl
from jax.experimental.pallas import tpu as pltpu
from jax.sharding import PartitionSpec as P

SLOT = 128
NBR = 32
TAIL = 16
PART = 32
LANES = 128
EPSILON = 1e-05
ANY = pl.BlockSpec(memory_space=pl.ANY)
BF = jnp.bfloat16
F32 = jnp.float32


def params(limit):
    return pltpu.CompilerParams(dimension_semantics=("arbitrary",), vmem_limit_bytes=limit << 20)


SMALL = pl.CostEstimate(flops=1000000, bytes_accessed=1000, transcendentals=0)


TOKEN = jax.ShapeDtypeStruct((8, LANES), F32)


def token_spec():
    return pl.BlockSpec((8, LANES), lambda i, *_: (0, 0))


def mark(token_ref):
    token_ref[...] = jnp.zeros_like(token_ref)


def launch(kernel, grid, ins, outs, shapes, args, name, prefetch=(), scratch=(), tokens=(), limit=24):
    count = len(prefetch) + len(args)

    def body(*refs):
        kernel(*refs[:count], *refs[count + len(tokens) :])

    return pl.pallas_call(
        body,
        grid_spec=pltpu.PrefetchScalarGridSpec(
            num_scalar_prefetch=len(prefetch),
            grid=grid,
            in_specs=[*ins, *[pl.BlockSpec(memory_space=pl.ANY)] * len(tokens)],
            out_specs=outs,
            scratch_shapes=list(scratch),
        ),
        out_shape=shapes,
        compiler_params=params(limit),
        cost_estimate=SMALL,
        name=name,
    )(*prefetch, *args, *tokens)


def dot(a, b):
    return jnp.dot(a, b, preferred_element_type=F32)


def dot_t(a, b):
    return lax.dot_general(a, b, (((1,), (1,)), ((), ())), preferred_element_type=F32)


def wide(v, columns):
    return jnp.concatenate([v] * (columns // LANES), axis=1)


def tiles_kernel(nbr_ref, valid_ref, h_ref, ht_ref, inv_ref, val_ref, token_ref):
    mark(token_ref)
    entries = nbr_ref[0]
    rows = lax.broadcasted_iota(jnp.int32, (SLOT, SLOT), 0)
    cols = lax.broadcasted_iota(jnp.int32, (SLOT, SLOT), 1)
    hits = jnp.zeros((SLOT, SLOT), F32)
    degree = jnp.zeros((1, SLOT), F32)
    for k in range(entries.shape[0]):
        one = entries[k : k + 1, :]
        hits += (one == rows).astype(F32)
        degree += (one >= 0).astype(F32)
    eye = (rows == cols).astype(F32)
    joined = hits + eye
    counts = joined + joined * eye
    ht_ref[0] = wide(counts.astype(BF), 2 * SLOT)
    h_ref[0] = wide(counts.T.astype(BF), 2 * SLOT)
    valid = valid_ref[0].astype(F32)
    inv_ref[0] = jnp.broadcast_to(valid / (degree + 1.0), (SLOT, SLOT)).T
    val_ref[0] = jnp.broadcast_to(valid, (SLOT, SLOT)).T


def build_tiles(neighbours, node_valid):
    slots = neighbours.shape[0] // SLOT
    turned = neighbours.reshape(slots, SLOT, NBR).transpose(0, 2, 1)
    square = pl.BlockSpec((1, SLOT, SLOT), lambda i: (i, 0, 0))
    double = pl.BlockSpec((1, SLOT, 2 * SLOT), lambda i: (i, 0, 0))
    return launch(
        tiles_kernel, (slots,),
        [pl.BlockSpec((1, NBR, SLOT), lambda i: (i, 0, 0)), pl.BlockSpec((1, 1, SLOT), lambda i: (i, 0, 0))],
        [double, double, square, square, token_spec()],
        [jax.ShapeDtypeStruct((slots, SLOT, 2 * SLOT), BF)] * 2 + [jax.ShapeDtypeStruct((slots, SLOT, SLOT), F32)] * 2 + [TOKEN],
        [turned, node_valid.reshape(slots, 1, SLOT)], "tiles",
    )


def combine(g_ref):
    mref, first, second, count = (g_ref[:, k, :] for k in range(4))
    shift = first / count
    mean_each = mref + shift
    spread_each = second - first * shift
    total = jnp.sum(count, axis=0, keepdims=True)
    mean = jnp.sum(count * mean_each, axis=0, keepdims=True) / total
    away = mean_each - mean
    variance = jnp.sum(spread_each + count * away * away, axis=0, keepdims=True) / total
    return total, mean, lax.rsqrt(variance + EPSILON)


def small_gather(copies, axis):
    return lax.all_to_all(copies, axis, split_axis=0, concat_axis=0, tiled=True)


def copies_shape(columns):
    return (lax.axis_size("row"), 8, columns)


def spread_rows(out_ref, rows):
    block = jnp.concatenate([*rows, jnp.zeros((8 - len(rows), out_ref.shape[2]), F32)], axis=0)

    def one(n, carry):
        out_ref[n] = block
        return carry

    lax.fori_loop(0, out_ref.shape[0], one, 0)


def split(value):
    high = value.astype(BF)
    return high, (value - high.astype(F32)).astype(BF)


def fold(value):
    return jnp.sum(value.reshape(value.shape[0] // 8, 8, value.shape[1]), axis=0)


def at(ref, k):
    return ref[k : k + 1, :]


def put(ref, k, value):
    ref[k : k + 1, :] = value


def half(ids, big, sources, weights, turned, name, tokens=(), early=None):
    nodes, depth = sources[0].shape
    columns = weights[0][0].shape[1]
    rows = big * SLOT
    n = len(sources)
    before = [] if early is None else [early]
    product = dot_t if turned else dot

    def kernel(ids_ref, *refs):
        out_ref, token_ref = refs[-2:]
        mark(token_ref)
        terms = [product(x_ref[...], w_ref[...]) for x_ref, w_ref in zip(refs[:n], refs[n : 2 * n])]
        terms += [e_ref[...] for e_ref in refs[2 * n : -2]]
        out_ref[...] = sum(terms[1:], terms[0])

    flat = pl.BlockSpec((rows, depth), lambda i, ids: (i, 0))
    wide_flat = pl.BlockSpec((rows, columns), lambda i, ids: (i, 0))
    return launch(
        kernel, (nodes // rows,), [flat] * n + [spec for _, spec in weights] + [wide_flat for _ in before],
        [wide_flat, token_spec()], [jax.ShapeDtypeStruct((nodes, columns), F32), TOKEN],
        [*sources, *[w for w, _ in weights], *before], name, prefetch=[ids], tokens=tokens,
    )


def weight_block(weight, b):
    depth = weight.shape[0] // 4
    return weight, pl.BlockSpec((depth, weight.shape[1]), lambda i, ids: (ids[b], 0))


def whole_block(piece):
    return piece, pl.BlockSpec(piece.shape, lambda i, ids: (0, 0))


def each_part(big, body, part=32):
    for s in range(big):
        for r in range(SLOT // part):
            body(s, slice(r * part, (r + 1) * part), slice(s * SLOT + r * part, s * SLOT + (r + 1) * part))


def split_three(value):
    high, rest = split(value)
    middle, low = split(value - high.astype(F32) - rest.astype(F32))
    return high, rest, middle


def coef_rows(ref, base):
    rows = ref[base : base + TAIL, :].astype(F32)
    return tuple(rows[k : k + 1] + rows[k + 1 : k + 2] + rows[k + 2 : k + 3] for k in (0, 3))


def receive(big, lead, i, lead_ref, rest_ref, val_ref, to_ref):
    columns = to_ref.shape[1]
    scale, shift = coef_rows(rest_ref, rest_ref.shape[0] - TAIL)
    for s in range(big):
        rows = slice(s * SLOT, (s + 1) * SLOT)
        if s < lead:

            @pl.when(i == 0)
            def _():
                to_ref[rows, :] = lead_ref[rows, :]

            @pl.when(i > 0)
            def _():
                to_ref[rows, :] = rest_ref[pl.ds(pl.multiple_of((i * big + s - lead) * SLOT, SLOT), SLOT), :]

        else:
            to_ref[rows, :] = rest_ref[pl.ds(pl.multiple_of((i * big + s - lead) * SLOT, SLOT), SLOT), :]

    def part(s, inner, rows):
        u = to_ref[rows, :].astype(F32) * scale + shift
        to_ref[rows, :] = (wide(val_ref[s, inner, :], columns) * (u + u * jnp.tanh(u))).astype(BF)

    each_part(big, part)


def far_kernel(big, lead, ids_ref, lead_ref, rest_ref, val_ref, w_ref, early_ref, out_ref, to_ref):
    receive(big, lead, pl.program_id(0), lead_ref, rest_ref, val_ref, to_ref)
    out_ref[...] = early_ref[...] + dot(to_ref[...], w_ref[...])


def far_half(ids, big, sent, weight, val, early, name, tokens=()):
    nodes, columns = early.shape
    block, spec = weight
    depth = block.shape[1] if spec.block_shape is None else spec.block_shape[0]
    rows = big * SLOT
    flat = pl.BlockSpec((rows, columns), lambda i, ids: (i, 0))
    to = pl.BlockSpec((rows, depth), lambda i, ids: (i, 0))
    return launch(
        functools.partial(far_kernel, big, sent[0].shape[0] // SLOT), (nodes // rows,),
        [
            *[pl.BlockSpec(x.shape, lambda i, ids: (0, 0)) for x in sent],
            pl.BlockSpec((big, SLOT, SLOT), lambda i, ids: (i, 0, 0)), spec, flat,
        ],
        [flat, to], [jax.ShapeDtypeStruct((nodes, columns), F32), jax.ShapeDtypeStruct((nodes, depth), BF)],
        [*sent, val, block, early], name, prefetch=[ids], tokens=tokens,
    )


def forward_kernel(big, lead, send, got, ids_ref, early_ref, *refs):
    if got:
        lead_ref, rest_ref, w_beyond, h_ref, inv_ref, val_ref, lin_ref, st_ref, y_ref, *refs = refs
        receive(big, lead, pl.program_id(0), lead_ref, rest_ref, val_ref, y_ref)
    else:
        y_ref, w_beyond, h_ref, inv_ref, val_ref, lin_ref, st_ref, *refs = refs
    token_ref, *refs = refs
    mark(token_ref)
    if send:
        lead_ref, rest_ref, *refs = refs
    tot_ref, acc_ref, ref_ref = refs
    forward_body(
        big, early_ref, y_ref, w_beyond, h_ref, inv_ref, val_ref, lin_ref, st_ref, tot_ref, acc_ref, ref_ref
    )
    if not send:
        return
    i = pl.program_id(0)
    mref = at(ref_ref, 0)
    for s in range(big):
        value = (lin_ref[s * SLOT : (s + 1) * SLOT, :] - mref).astype(BF)
        later = pl.ds(pl.multiple_of((i * big + s - lead) * SLOT, SLOT), SLOT)
        if s < lead:

            @pl.when(i == 0)
            def _():
                lead_ref[s * SLOT : (s + 1) * SLOT, :] = value

            @pl.when(i > 0)
            def _():
                rest_ref[later, :] = value

        else:
            rest_ref[later, :] = value


def forward_body(big, early_ref, y_ref, w_beyond, h_ref, inv_ref, val_ref, lin_ref, st_ref, tot_ref, acc_ref, ref_ref):
    i = pl.program_id(0)
    columns = lin_ref.shape[1]
    tot_ref[...] = early_ref[...] + dot(y_ref[...], w_beyond[...])

    def mixed(s):
        high, low = split(tot_ref[s * SLOT : (s + 1) * SLOT, :])
        return dot(h_ref[s], jnp.concatenate([high, low], axis=0)) * wide(inv_ref[s], columns)

    @pl.when(i == 0)
    def _():
        acc_ref[...] = jnp.zeros_like(acc_ref)
        v = val_ref[0]
        count = jnp.sum(v, axis=0, keepdims=True)
        put(ref_ref, 0, jnp.sum(mixed(0) * wide(v, columns), axis=0, keepdims=True) / wide(count, columns))

    mref = at(ref_ref, 0)
    for s in range(big):
        lin_ref[s * SLOT : (s + 1) * SLOT, :] = mixed(s)
        for r in range(SLOT // 32):
            v = val_ref[s, r * 32 : (r + 1) * 32, :]
            away = (lin_ref[s * SLOT + r * 32 : s * SLOT + (r + 1) * 32, :] - mref) * wide(v, columns)
            acc_ref[0] += fold(away)
            acc_ref[1] += fold(away * away)
            acc_ref[2, :, :LANES] += fold(v)

    @pl.when(i == pl.num_programs(0) - 1)
    def _():
        first, second = (jnp.sum(acc_ref[k], axis=0, keepdims=True) for k in range(2))
        count = wide(jnp.sum(acc_ref[2, :, :LANES], axis=0, keepdims=True), columns)
        spread_rows(st_ref, (at(ref_ref, 0), first, second, count))


def forward(ids, big, lead, early, beyond, weight, tiles, name, tokens=(), send=False):
    h, _, inv, val = tiles
    nodes, columns = early.shape
    depth = weight.shape[0] // 4
    rows = big * SLOT
    got = len(beyond) == 2
    flat = pl.BlockSpec((rows, columns), lambda i, ids: (i, 0))
    to = pl.BlockSpec((rows, depth), lambda i, ids: (i, 0))
    whole = lambda shape: pl.BlockSpec(shape, lambda i, ids: (0, 0))
    tile = pl.BlockSpec((big, SLOT, SLOT), lambda i, ids: (i, 0, 0))
    double = pl.BlockSpec((big, SLOT, 2 * SLOT), lambda i, ids: (i, 0, 0))
    _, block = weight_block(weight, 3)
    outs = [flat, pl.BlockSpec(copies_shape(columns), lambda i, ids: (0, 0, 0))]
    shapes = [jax.ShapeDtypeStruct((nodes, columns), F32), jax.ShapeDtypeStruct(copies_shape(columns), F32)]
    if got:
        outs.append(to)
        shapes.append(jax.ShapeDtypeStruct((nodes, depth), BF))
    outs.append(token_spec())
    shapes.append(TOKEN)
    if send:
        for r in (lead * SLOT, nodes - lead * SLOT + TAIL):
            outs.append(whole((r, columns)))
            shapes.append(jax.ShapeDtypeStruct((r, columns), BF))
    return launch(
        functools.partial(forward_kernel, big, lead, send, got), (nodes // rows,),
        [flat, *([whole(x.shape) for x in beyond] if got else [to]), block, double, tile, tile],
        outs, shapes, [early, *beyond, weight, h, inv, val], name, prefetch=[ids],
        scratch=[pltpu.VMEM((rows, columns), F32), pltpu.VMEM((3, 8, columns), F32), pltpu.VMEM((8, columns), F32)],
        tokens=tokens,
    )


def columns_of(g_ref, gamma_ref, beta_ref, co_ref):
    total, mean, inv_std = combine(g_ref)
    put(co_ref, 0, mean)
    put(co_ref, 1, 0.5 * gamma_ref[...] * inv_std)
    put(co_ref, 2, 0.5 * beta_ref[...])
    put(co_ref, 3, inv_std)
    put(co_ref, 4, total)


def silu_of(away, co_ref):
    u = away * at(co_ref, 1) + at(co_ref, 2)
    return u + u * jnp.tanh(u)


def double_slope(away, co_ref):
    u = away * at(co_ref, 1) + at(co_ref, 2)
    t = jnp.tanh(u)
    return (1.0 + t) * (1.0 + u * (1.0 - t))


def coefs_kernel(st_ref, g_ref, gamma_ref, beta_ref, rest_ref, out_ref, token_ref, co_ref):
    mark(token_ref)
    columns_of(g_ref, gamma_ref, beta_ref, co_ref)
    scale = at(co_ref, 1)
    shift = (st_ref[0, 0:1, :] - at(co_ref, 0)) * scale + at(co_ref, 2)
    rows = [*split_three(scale), *split_three(shift)]
    rows.append(jnp.zeros((TAIL - len(rows), scale.shape[1]), BF))
    out_ref[...] = jnp.concatenate([r.astype(F32) for r in rows], axis=0).astype(BF)


def with_coefs(rest, stats, norm, tokens):
    nodes, columns = rest.shape
    args = [stats, *norm, rest]
    return pl.pallas_call(
        lambda *refs: coefs_kernel(*refs[: len(args)], *refs[len(args) + len(tokens) :]),
        grid=(1,),
        in_specs=[pl.BlockSpec((1, 8, columns), lambda i: (0, 0, 0))]
        + [pl.BlockSpec(v.shape, lambda i, n=v.ndim: (0,) * n) for v in norm]
        + [pl.BlockSpec(memory_space=pl.ANY)] * (1 + len(tokens)),
        out_specs=[pl.BlockSpec((TAIL, columns), lambda i: (nodes // TAIL - 1, 0)), token_spec()],
        out_shape=[jax.ShapeDtypeStruct((nodes, columns), BF), TOKEN],
        scratch_shapes=[pltpu.VMEM((8, columns), F32)],
        input_output_aliases={len(args) - 1: 0},
        compiler_params=params(24),
        cost_estimate=SMALL,
        name="coefs",
    )(*args, *tokens)


def result_kernel(big, lin_ref, val_ref, g_ref, gamma_ref, beta_ref, out_ref, token_ref, co_ref):
    mark(token_ref)

    @pl.when(pl.program_id(0) == 0)
    def _():
        columns_of(g_ref, gamma_ref, beta_ref, co_ref)

    def part(s, inner, rows):
        value = silu_of(lin_ref[rows, :] - at(co_ref, 0), co_ref)
        out_ref[rows, :] = (wide(val_ref[s, inner, :], lin_ref.shape[1]) * value).astype(out_ref.dtype)

    each_part(big, part)


def sums_kernel(big, lin_ref, cot_ref, val_ref, g_ref, gamma_ref, beta_ref, st_ref, co_ref, acc_ref):
    @pl.when(pl.program_id(0) == 0)
    def _():
        columns_of(g_ref, gamma_ref, beta_ref, co_ref)
        acc_ref[...] = jnp.zeros_like(acc_ref)

    def part(s, inner, rows):
        away = lin_ref[rows, :] - at(co_ref, 0)
        valid = wide(val_ref[s, inner, :], lin_ref.shape[1])
        grad = cot_ref[rows, :].astype(F32) * valid * double_slope(away, co_ref)
        acc_ref[0] += fold(grad)
        acc_ref[1] += fold(grad * away)

    each_part(big, part)
    finish_sums(st_ref, co_ref, acc_ref)


def finish_sums(st_ref, co_ref, acc_ref):
    @pl.when(pl.program_id(0) == pl.num_programs(0) - 1)
    def _():
        grad_beta = 0.5 * jnp.sum(acc_ref[0], axis=0, keepdims=True)
        grad_gamma = 0.5 * at(co_ref, 3) * jnp.sum(acc_ref[1], axis=0, keepdims=True)
        spread_rows(st_ref, (grad_beta, grad_gamma))


def turn_kernel(from_cot, big, lin_ref, grad_ref, inv_ref, ht_ref, g_ref, sg_ref, gamma_ref, beta_ref, out_ref, token_ref, co_ref, lg_ref):
    mark(token_ref)

    @pl.when(pl.program_id(0) == 0)
    def _():
        columns_of(g_ref, gamma_ref, beta_ref, co_ref)
        sg = sg_ref[...]
        twice = 2.0 / at(co_ref, 4)
        put(co_ref, 5, twice * jnp.sum(sg[:, 0, :], axis=0, keepdims=True))
        put(co_ref, 6, twice * at(co_ref, 3) * jnp.sum(sg[:, 1, :], axis=0, keepdims=True))

    columns = lin_ref.shape[1]

    for s in range(big):
        for r in range(SLOT // PART):
            inner = slice(r * PART, (r + 1) * PART)
            rows = slice(s * SLOT + r * PART, s * SLOT + (r + 1) * PART)
            away = lin_ref[rows, :] - at(co_ref, 0)
            if from_cot:
                grad = grad_ref[rows, :].astype(F32) * double_slope(away, co_ref)
            else:
                grad = grad_ref[rows, :]
            weight = wide(inv_ref[s, inner, :], columns)
            high, low = split(weight * (grad - (at(co_ref, 5) + away * at(co_ref, 6))))
            lg_ref[s, inner, :] = high
            lg_ref[s, SLOT + r * PART : SLOT + (r + 1) * PART, :] = low
        out_ref[s * SLOT : (s + 1) * SLOT, :] = (dot(ht_ref[s], lg_ref[s]) * at(co_ref, 1)).astype(BF)


def rows_call(kernel, big, arrays, tiles, smalls, out_dtype, scratch, name, tokens=(), limit=24):
    rows = big * SLOT
    nodes, columns = arrays[0].shape
    flat = pl.BlockSpec((rows, columns), lambda i: (i, 0))
    ins = [flat for _ in arrays]
    ins += [pl.BlockSpec((big,) + t.shape[1:], lambda i: (i, 0, 0)) for t in tiles]
    ins += [pl.BlockSpec(s.shape, lambda i, n=s.ndim: (0,) * n) for s in smalls]
    if out_dtype is None:
        out_spec = pl.BlockSpec(copies_shape(columns), lambda i: (0, 0, 0))
        out_shape = jax.ShapeDtypeStruct(copies_shape(columns), F32)
    else:
        out_spec = [flat, token_spec()]
        out_shape = [jax.ShapeDtypeStruct((nodes, columns), out_dtype), TOKEN]
    return launch(
        functools.partial(kernel, big), (nodes // rows,), ins, out_spec, out_shape, [*arrays, *tiles, *smalls], name,
        scratch=[pltpu.VMEM((8, columns), F32)] + scratch, tokens=tokens, limit=limit,
    )


def turn_call(from_cot, big, lin, grad, tiles, norm, sums, name, tokens=()):
    _, ht, inv, _ = tiles
    return rows_call(
        functools.partial(turn_kernel, from_cot), big, [lin, grad], [inv, ht], [norm[0], sums, *norm[1:]], BF,
        [pltpu.VMEM((big, 2 * SLOT, lin.shape[1]), BF)], name, tokens, 60,
    )


def backward_kernel(big, last, early_ref, y_ref, w_beyond, *refs):
    total = early_ref[...] + dot_t(y_ref[...], w_beyond[...])
    if last:
        refs[-2][...] = total
        mark(refs[-1])
        return
    lin_ref, g_ref, gamma_ref, beta_ref, out_ref, st_ref, co_ref, acc_ref = refs
    out_ref[...] = total

    @pl.when(pl.program_id(0) == 0)
    def _():
        columns_of(g_ref, gamma_ref, beta_ref, co_ref)
        acc_ref[...] = jnp.zeros_like(acc_ref)

    def part(s, inner, rows):
        away = lin_ref[rows, :] - at(co_ref, 0)
        grad = out_ref[rows, :] * double_slope(away, co_ref)
        out_ref[rows, :] = grad
        acc_ref[0] += fold(grad)
        acc_ref[1] += fold(grad * away)

    each_part(big, part)
    finish_sums(st_ref, co_ref, acc_ref)


def backward(big, early, beyond, piece, lin, norm, name, tokens=()):
    nodes, columns = early.shape
    rows = big * SLOT
    last = norm is None
    flat = pl.BlockSpec((rows, columns), lambda i: (i, 0))
    fixed = lambda s: pl.BlockSpec(s.shape, lambda i, n=s.ndim: (0,) * n)
    ins = [flat, flat, fixed(piece)]
    args = [early, beyond, piece]
    out_specs = [flat]
    out_shape = [jax.ShapeDtypeStruct((nodes, columns), F32)]
    scratch = []
    if last:
        out_specs.append(token_spec())
        out_shape.append(TOKEN)
    else:
        ins += [flat, *map(fixed, norm)]
        args += [lin, *norm]
        out_specs.append(pl.BlockSpec(copies_shape(columns), lambda i: (0, 0, 0)))
        out_shape.append(jax.ShapeDtypeStruct(copies_shape(columns), F32))
        scratch = [pltpu.VMEM((8, columns), F32), pltpu.VMEM((2, 8, columns), F32)]
    return launch(
        functools.partial(backward_kernel, big, last), (nodes // rows,), ins, out_specs, out_shape, args, name,
        scratch=scratch, tokens=tokens,
    )


def weight_kernel(spans, other, meta_ref, *refs):
    sources, h_hbm, outs, (token_ref, buf_ref, h_ref, sem) = refs[:4], refs[4], refs[5:7], refs[7:]
    mark(token_ref)
    for m in range(2):
        for n, span in enumerate(spans):
            rows = pl.ds(*span)
            if m == 0:
                pltpu.make_async_copy(h_hbm.at[rows, :], h_ref.at[rows, :], sem.at[2, n]).start()
            for k in range(2):

                @pl.when((meta_ref[4 + m] ^ other) == k)
                def _():
                    pltpu.make_async_copy(
                        sources[2 * m + k].at[rows, :], buf_ref.at[m, rows, :], sem.at[m, n]
                    ).start()

    for m in range(2):
        total = None
        for n, (start, size) in enumerate(spans):
            rows = pl.ds(start, size)
            if m == 0:
                pltpu.make_async_copy(h_hbm.at[rows, :], h_ref.at[rows, :], sem.at[2, n]).wait()
            pltpu.make_async_copy(sources[2 * m].at[rows, :], buf_ref.at[m, rows, :], sem.at[m, n]).wait()
            x, h = buf_ref[m, start : start + size, :], h_ref[start : start + size, :]
            term = lax.dot_general(x, h, (((0,), (0,)), ((), ())), preferred_element_type=F32)
            total = term if total is None else total + term
        outs[m][...] = total.astype(outs[m].dtype)


def weight_terms(meta, other, pairs, h, name, tokens=()):
    nodes, depth = pairs[0][0].shape
    columns = h.shape[1]
    pieces = 2 if nodes % 32 == 0 else 1
    spans = tuple((n * (nodes // pieces), nodes // pieces) for n in range(pieces))
    whole = pl.BlockSpec((depth, columns), lambda i, meta: (0, 0))
    return launch(
        functools.partial(weight_kernel, spans, other), (1,), [pl.BlockSpec(memory_space=pl.ANY)] * 5,
        [whole, whole, token_spec()],
        [jax.ShapeDtypeStruct((depth, columns), BF)] * 2 + [TOKEN], [*pairs[0], *pairs[1], h], name, prefetch=[meta],
        scratch=[
            pltpu.VMEM((2, nodes, depth), BF), pltpu.VMEM((nodes, columns), BF), pltpu.SemaphoreType.DMA((3, pieces))
        ],
        tokens=tokens, limit=60,
    )


def place_kernel(orders, meta_ref, *refs):
    out_ref, token_ref = refs[-2:]
    mark(token_ref)
    pieces = 1 << (len(orders[0]) - 2)
    size = out_ref.shape[0] // pieces
    for k in range(4):

        @pl.when(pl.program_id(0) == k)
        def _():
            mask = 0
            for b in orders[k // 2][1:-1]:
                mask = 2 * mask + meta_ref[4 + b]
            for n in range(pieces):
                start = pl.multiple_of((mask ^ n) * size, size)
                out_ref[pl.ds(start, size), :] = refs[k][n * size : (n + 1) * size, :].astype(F32)


def place_blocks(meta, blocks, orders, name, limit, tokens):
    depth, columns = blocks[0].shape
    return launch(
        functools.partial(place_kernel, orders), (4,), [pl.BlockSpec((depth, columns), lambda i, meta: (0, 0))] * 4,
        [
            pl.BlockSpec((depth, columns), lambda i, meta: (meta[0] ^ (i // 2 * 2) ^ (i % 2) ^ meta[4 + i // 2], 0)),
            token_spec(),
        ],
        [jax.ShapeDtypeStruct((4 * depth, columns), F32), TOKEN], blocks, name, prefetch=[meta], limit=limit,
        tokens=tokens,
    )


def after(value, *tokens):
    value, tokens = lax.optimization_barrier((value, tokens))
    return value, tokens


def across(value, axis, distance):
    size = lax.axis_size(axis)
    return lax.ppermute(value, axis, [(i, i ^ distance) for i in range(size)])


def slices_kernel(ids_ref, one_ref, two_ref, *refs):
    outs, (token_ref, sem) = refs[:6], refs[6:]
    mark(token_ref)
    depth = outs[0].shape[0]
    copies = []
    for n, out_ref in enumerate(outs):
        start = pl.multiple_of(ids_ref[1 + n % 3] * depth, depth)
        source = (one_ref, two_ref)[n // 3].at[pl.ds(start, depth), :]
        copies.append(pltpu.make_async_copy(source, out_ref, sem.at[n]))
    for copy in copies:
        copy.start()
    for copy in copies:
        copy.wait()


def weight_slices(ids, one, two):
    depth, columns = one.shape[0] // 4, one.shape[1]
    hbm = pl.BlockSpec(memory_space=pltpu.HBM)
    outs = launch(
        slices_kernel, (1,), [hbm, hbm], [hbm] * 6 + [token_spec()],
        [jax.ShapeDtypeStruct((depth, columns), one.dtype)] * 6 + [TOKEN], [one, two], "weight_slices",
        prefetch=[ids], scratch=[pltpu.SemaphoreType.DMA((6,))],
    )
    return outs[:3], outs[3:6], outs[6]


def weight_rows(slices):
    far = across(slices[1], "col", 2)
    other = across(slices[2], "col", 2)
    return [across(slices[0], "col", 1), far, across(other, "col", 1)], (far, other)


def fold_kernel(last, place, meta_ref, keep_ref, got_ref, *refs):
    mark(refs[-1])
    if last:
        refs[0][...] = (keep_ref[...].astype(F32) + got_ref[...].astype(F32)).astype(BF)
        return
    part = refs[0].shape[0]
    bit = meta_ref[4 + place]
    for out_ref, which in zip(refs[:2], (1 - bit, bit)):
        rows = pl.ds(pl.multiple_of(which * part, part), part)
        out_ref[...] = (keep_ref[rows, :].astype(F32) + got_ref[rows, :].astype(F32)).astype(BF)


def join_kernel(meta_ref, keep_ref, got_ref, out_ref, token_ref):
    mark(token_ref)
    part = keep_ref.shape[0]
    out_ref[:part, :] = keep_ref[...]
    out_ref[part:, :] = got_ref[...]


def small_call(kernel, meta, keep, got, rows, name, tokens):
    columns = keep.shape[1]
    whole = lambda r: pl.BlockSpec((r, columns), lambda i, bit: (0, 0))
    return launch(
        kernel, (1,), [whole(keep.shape[0])] * 2, [whole(r) for r in rows] + [token_spec()],
        [jax.ShapeDtypeStruct((r, columns), BF) for r in rows] + [TOKEN], [keep, got], name, prefetch=[meta], tokens=tokens,
    )


class RowSum:
    def __init__(self, axis, meta, terms, name, between=tuple):
        self.axis, self.meta, self.name = axis, meta, name
        self.bits = lax.axis_size(axis).bit_length() - 1
        self.stages = 2 * self.bits - 1
        self.orders = [list(range(self.bits)), list(range(1, self.bits)) + [0]]
        *self.send, self.sent = terms(1, ())
        *self.keep, self.kept = terms(0, (self.sent, *between()))
        self.stage = 0
        self.step(())

    def step(self, tokens):
        s, last = self.stage, self.bits - 1
        self.stage += 1
        started = []
        for n in range(2):
            rows = self.keep[n].shape[0]
            call = lambda kernel, sizes: small_call(
                kernel, self.meta, self.keep[n], self.got[n], sizes, f"{self.name}_{n}_{s}", tokens
            )
            if 0 < s < last:
                fold = functools.partial(fold_kernel, False, self.orders[n][s])
                self.send[n], self.keep[n], token = call(fold, [rows // 2] * 2)
            elif s == last or s == last + 1:
                self.keep[n], token = call(functools.partial(fold_kernel, True, 0), [rows])
            elif s > last + 1:
                self.keep[n], token = call(join_kernel, [2 * rows])
            if s > 0:
                started.append(token)
        level = s if s <= last else 2 * last - s
        moved = self.send if s < last else self.keep
        self.got = [across(moved[n], self.axis, 1 << self.orders[n][level]) for n in range(2)]
        return tuple(started)

    def next(self, *tokens):
        return self.step(tokens) if self.stage < self.stages else tokens

    def placed(self, limit, tokens=()):
        while self.stage < self.stages:
            self.step(())
        blocks = [v for n in range(2) for v in (self.keep[n], self.got[n])]
        return place_blocks(self.meta, blocks, self.orders, f"place_{self.name}", limit, tokens)


def local(
    features,
    neighbours,
    node_valid,
    weight_one,
    gamma_one,
    beta_one,
    weight_two,
    gamma_two,
    beta_two,
    cotangent,
):
    nodes, columns = features.shape
    slots = nodes // SLOT
    big = slots // 2 if slots % 2 == 0 else slots
    lead = max(1, min(big, 5 * slots // 14))
    q = lax.axis_index("col")
    place = lax.axis_index("row")
    bits = [(place >> b) & 1 for b in range(lax.axis_size("row").bit_length() - 1)]
    ids = jnp.stack([q, q ^ 1, q ^ 2, q ^ 3, *bits]).astype(jnp.int32)
    g1, b1, g2, b2 = (v.reshape(1, columns) for v in (gamma_one, beta_one, gamma_two, beta_two))

    far_one = across(features, "col", 2)
    near_one = across(features, "col", 1)
    *tiles, tiles_token = build_tiles(neighbours, node_valid)
    val = tiles[3]
    slices_one, slices_two, slices_token = weight_slices(ids, weight_one, weight_two)
    early, token = half(ids, big, [features, near_one], [weight_block(weight_one, b) for b in (0, 1)], False, "half_one")
    far_one, tokens = after(far_one, token, tiles_token, slices_token)
    beyond_one = across(far_one, "col", 1)
    early, _ = half(ids, big, [far_one], [weight_block(weight_one, 2)], False, "far_half_one", tokens, early)
    lin_one, stats, _, sent, rest = forward(ids, big, lead, early, [beyond_one], weight_one, tiles, "forward_one", tokens, send=True)

    far_lead = across(sent, "col", 2)
    norm_one = (small_gather(stats, "row"), g1, b1)
    rest, token = with_coefs(rest, stats, norm_one, (far_lead,))
    far_rest = across(rest, "col", 2)
    hidden, _ = rows_call(result_kernel, big, [lin_one], [val], norm_one, BF, [], "hidden", (token,))
    near_two = across(hidden, "col", 1)
    early, token = half(
        ids, big, [hidden, near_two], [weight_block(weight_two, b) for b in (0, 1)], False, "half_two"
    )
    far_rest, tokens = after(far_rest, token)
    beyond_two = [across(x, "col", 1) for x in (far_lead, far_rest)]
    early, far_two = far_half(
        ids, big, (far_lead, far_rest), weight_block(weight_two, 2), val, early, "far_half_two", tokens
    )
    lin_two, stats, beyond_two, token = forward(ids, big, lead, early, beyond_two, weight_two, tiles, "forward_two")
    norm_two = (small_gather(stats, "row"), g2, b2)
    slices_two, tokens = after(slices_two, token)
    rows_two, crossing = weight_rows(slices_two)

    sums = rows_call(
        sums_kernel, big, [lin_two, cotangent], [val], norm_two, None, [pltpu.VMEM((2, 8, columns), F32)], "sums_two", tokens
    )
    grads_two = small_gather(sums, "row")
    turned, _ = turn_call(True, big, lin_two, cotangent, tiles, norm_two, grads_two, "turn_two", crossing)
    far, near = across(turned, "col", 2), across(turned, "col", 1)

    def terms_two(other, tokens, h=turned):
        return weight_terms(ids, other, ((hidden, near_two), (far_two, beyond_two)), h, "terms_two", tokens)

    sum_two = RowSum("row", ids, terms_two, "two")
    weights = [weight_block(weight_two, 0), whole_block(rows_two[0])]
    early, token = half(ids, big, [turned, near], weights, True, "half_back_two", (sum_two.kept,))
    far, tokens = after(far, *sum_two.next(*sum_two.next(token)))
    beyond = across(far, "col", 1)
    slices_one, (far,) = after(slices_one, far)
    rows_one, crossing = weight_rows(slices_one)
    early, _ = half(ids, big, [far], [whole_block(rows_two[1])], True, "far_half_back_two", tokens, early)
    grad_one, sums = backward(big, early, beyond, rows_two[2], lin_one, norm_one, "backward_two", tokens)
    tokens = (*crossing, *sum_two.next(*sum_two.next(sums)))
    grads_one = small_gather(sums, "row")

    turned, _ = turn_call(False, big, lin_one, grad_one, tiles, norm_one, grads_one, "turn_one", tokens)
    far, near = across(turned, "col", 2), across(turned, "col", 1)

    def terms_one(other, tokens, h=turned):
        return weight_terms(ids, other, ((features, near_one), (far_one, beyond_one)), h, "terms_one", tokens)

    sum_one = RowSum("row", ids, terms_one, "one", lambda: tuple(sum_two.got))
    weights = [weight_block(weight_one, 0), whole_block(rows_one[0])]
    early, token = half(ids, big, [turned, near], weights, True, "half_back_one", sum_one.next())
    output, token = rows_call(result_kernel, big, [lin_two], [val], norm_two, F32, [], "output", (token,))
    started = sum_one.next(token)
    far, tokens = after(far, *started)
    beyond = across(far, "col", 1)
    grad_weight_two, token = sum_two.placed(60, started)
    tokens = (*tokens, *sum_one.next(token))
    early, _ = half(ids, big, [far], [whole_block(rows_one[1])], True, "far_half_back_one", tokens, early)
    grad_features, token = backward(big, early, beyond, rows_one[2], None, None, "backward_one", tokens)
    while sum_one.stage < sum_one.stages - 1:
        sum_one.next()
    sum_one.next(token)
    grad_weight_one, _ = sum_one.placed(24)

    sums_one, sums_two = jnp.sum(grads_one, axis=0), jnp.sum(grads_two, axis=0)
    return (
        output,
        grad_features,
        grad_weight_one,
        sums_one[1],
        sums_one[0],
        grad_weight_two,
        sums_two[1],
        sums_two[0],
    )


def solution(mesh):
    placed = (
        P("row", "col"),
        P("row", None),
        P("row"),
        P(None, "col"),
        P("col"),
        P("col"),
        P(None, "col"),
        P("col"),
        P("col"),
        P("row", "col"),
    )
    return jax.shard_map(
        local,
        mesh=mesh,
        in_specs=placed,
        out_specs=(
            P("row", "col"),
            P("row", "col"),
            P(None, "col"),
            P("col"),
            P("col"),
            P(None, "col"),
            P("col"),
            P("col"),
        ),
        check_vma=False,
    )
```

```python
import functools

import jax
import jax.numpy as jnp
from jax import lax
from jax.experimental import pallas as pl
from jax.experimental.pallas import tpu as pltpu
from jax.sharding import PartitionSpec as P

SLOT = 128
NBR = 32
TAIL = 16
PART = 32
LANES = 128
EPSILON = 1e-05
ANY = pl.BlockSpec(memory_space=pl.ANY)
BF = jnp.bfloat16
F32 = jnp.float32


def params(limit):
    return pltpu.CompilerParams(dimension_semantics=("arbitrary",), vmem_limit_bytes=limit << 20)


SMALL = pl.CostEstimate(flops=1000000, bytes_accessed=1000, transcendentals=0)


TOKEN = jax.ShapeDtypeStruct((8, LANES), F32)


def token_spec():
    return pl.BlockSpec((8, LANES), lambda i, *_: (0, 0))


def mark(token_ref):
    token_ref[...] = jnp.zeros_like(token_ref)


def launch(kernel, grid, ins, outs, shapes, args, name, prefetch=(), scratch=(), tokens=(), limit=24):
    count = len(prefetch) + len(args)

    def body(*refs):
        kernel(*refs[:count], *refs[count + len(tokens) :])

    return pl.pallas_call(
        body,
        grid_spec=pltpu.PrefetchScalarGridSpec(
            num_scalar_prefetch=len(prefetch),
            grid=grid,
            in_specs=[*ins, *[pl.BlockSpec(memory_space=pl.ANY)] * len(tokens)],
            out_specs=outs,
            scratch_shapes=list(scratch),
        ),
        out_shape=shapes,
        compiler_params=params(limit),
        cost_estimate=SMALL,
        name=name,
    )(*prefetch, *args, *tokens)


def dot(a, b):
    return jnp.dot(a, b, preferred_element_type=F32)


def dot_t(a, b):
    return lax.dot_general(a, b, (((1,), (1,)), ((), ())), preferred_element_type=F32)


def wide(v, columns):
    return jnp.concatenate([v] * (columns // LANES), axis=1)


def tiles_kernel(nbr_ref, valid_ref, h_ref, ht_ref, inv_ref, val_ref, token_ref):
    mark(token_ref)
    entries = nbr_ref[0]
    rows = lax.broadcasted_iota(jnp.int32, (SLOT, SLOT), 0)
    cols = lax.broadcasted_iota(jnp.int32, (SLOT, SLOT), 1)
    hits = jnp.zeros((SLOT, SLOT), F32)
    degree = jnp.zeros((1, SLOT), F32)
    for k in range(entries.shape[0]):
        one = entries[k : k + 1, :]
        hits += (one == rows).astype(F32)
        degree += (one >= 0).astype(F32)
    eye = (rows == cols).astype(F32)
    joined = hits + eye
    counts = joined + joined * eye
    ht_ref[0] = counts.astype(BF)
    h_ref[0] = wide(counts.T.astype(BF), 2 * SLOT)
    valid = valid_ref[0].astype(F32)
    inv_ref[0] = jnp.broadcast_to(valid / (degree + 1.0), (SLOT, SLOT)).T
    val_ref[0] = jnp.broadcast_to(valid, (SLOT, SLOT)).T


def build_tiles(neighbours, node_valid):
    slots = neighbours.shape[0] // SLOT
    turned = neighbours.reshape(slots, SLOT, NBR).transpose(0, 2, 1)
    square = pl.BlockSpec((1, SLOT, SLOT), lambda i: (i, 0, 0))
    double = pl.BlockSpec((1, SLOT, 2 * SLOT), lambda i: (i, 0, 0))
    return launch(
        tiles_kernel, (slots,),
        [pl.BlockSpec((1, NBR, SLOT), lambda i: (i, 0, 0)), pl.BlockSpec((1, 1, SLOT), lambda i: (i, 0, 0))],
        [double, square, square, square, token_spec()],
        [
            jax.ShapeDtypeStruct((slots, SLOT, w), t)
            for w, t in ((2 * SLOT, BF), (SLOT, BF), (SLOT, F32), (SLOT, F32))
        ]
        + [TOKEN],
        [turned, node_valid.reshape(slots, 1, SLOT)], "tiles",
    )


def combine(g_ref):
    mref, first, second, count = (g_ref[:, k, :] for k in range(4))
    shift = first / count
    mean_each = mref + shift
    spread_each = second - first * shift
    total = jnp.sum(count, axis=0, keepdims=True)
    mean = jnp.sum(count * mean_each, axis=0, keepdims=True) / total
    away = mean_each - mean
    variance = jnp.sum(spread_each + count * away * away, axis=0, keepdims=True) / total
    return total, mean, lax.rsqrt(variance + EPSILON)


def small_gather(copies, axis):
    return lax.all_to_all(copies, axis, split_axis=0, concat_axis=0, tiled=True)


def copies_shape(columns):
    return (lax.axis_size("row"), 8, columns)


def spread_rows(out_ref, rows):
    block = jnp.concatenate([*rows, jnp.zeros((8 - len(rows), out_ref.shape[2]), F32)], axis=0)

    def one(n, carry):
        out_ref[n] = block
        return carry

    lax.fori_loop(0, out_ref.shape[0], one, 0)


def split(value):
    high = value.astype(BF)
    return high, (value - high.astype(F32)).astype(BF)


def fold(value):
    return jnp.sum(value.reshape(value.shape[0] // 8, 8, value.shape[1]), axis=0)


def at(ref, k):
    return ref[k : k + 1, :]


def put(ref, k, value):
    ref[k : k + 1, :] = value


def half(ids, big, sources, weights, turned, name, tokens=(), early=None):
    nodes, depth = sources[0].shape
    columns = weights[0][0].shape[1]
    rows = big * SLOT
    n = len(sources)
    before = [] if early is None else [early]
    product = dot_t if turned else dot

    def kernel(ids_ref, *refs):
        out_ref, token_ref = refs[-2:]
        mark(token_ref)
        terms = [product(x_ref[...], w_ref[...]) for x_ref, w_ref in zip(refs[:n], refs[n : 2 * n])]
        terms += [e_ref[...] for e_ref in refs[2 * n : -2]]
        out_ref[...] = sum(terms[1:], terms[0])

    flat = pl.BlockSpec((rows, depth), lambda i, ids: (i, 0))
    wide_flat = pl.BlockSpec((rows, columns), lambda i, ids: (i, 0))
    return launch(
        kernel, (nodes // rows,), [flat] * n + [spec for _, spec in weights] + [wide_flat for _ in before],
        [wide_flat, token_spec()], [jax.ShapeDtypeStruct((nodes, columns), F32), TOKEN],
        [*sources, *[w for w, _ in weights], *before], name, prefetch=[ids], tokens=tokens,
    )


def weight_block(weight, b):
    depth = weight.shape[0] // 4
    return weight, pl.BlockSpec((depth, weight.shape[1]), lambda i, ids: (ids[b], 0))


def whole_block(piece):
    return piece, pl.BlockSpec(piece.shape, lambda i, ids: (0, 0))


def each_part(big, body, part=32):
    for s in range(big):
        for r in range(SLOT // part):
            body(s, slice(r * part, (r + 1) * part), slice(s * SLOT + r * part, s * SLOT + (r + 1) * part))


def split_three(value):
    high, rest = split(value)
    middle, low = split(value - high.astype(F32) - rest.astype(F32))
    return high, rest, middle


def coef_rows(ref, base):
    rows = ref[base : base + TAIL, :].astype(F32)
    return tuple(rows[k : k + 1] + rows[k + 1 : k + 2] + rows[k + 2 : k + 3] for k in (0, 3))


def receive(big, lead, i, lead_ref, rest_ref, val_ref, to_ref):
    columns = to_ref.shape[1]
    scale, shift = coef_rows(rest_ref, rest_ref.shape[0] - TAIL)
    for s in range(big):
        rows = slice(s * SLOT, (s + 1) * SLOT)
        if s < lead:

            @pl.when(i == 0)
            def _():
                to_ref[rows, :] = lead_ref[rows, :]

            @pl.when(i > 0)
            def _():
                to_ref[rows, :] = rest_ref[pl.ds(pl.multiple_of((i * big + s - lead) * SLOT, SLOT), SLOT), :]

        else:
            to_ref[rows, :] = rest_ref[pl.ds(pl.multiple_of((i * big + s - lead) * SLOT, SLOT), SLOT), :]

    def part(s, inner, rows):
        u = to_ref[rows, :].astype(F32) * scale + shift
        to_ref[rows, :] = (wide(val_ref[s, inner, :], columns) * (u + u * jnp.tanh(u))).astype(BF)

    each_part(big, part)


def far_kernel(big, lead, ids_ref, lead_ref, rest_ref, val_ref, w_ref, early_ref, out_ref, to_ref):
    receive(big, lead, pl.program_id(0), lead_ref, rest_ref, val_ref, to_ref)
    out_ref[...] = early_ref[...] + dot(to_ref[...], w_ref[...])


def far_half(ids, big, sent, weight, val, early, name, tokens=()):
    nodes, columns = early.shape
    block, spec = weight
    depth = block.shape[1] if spec.block_shape is None else spec.block_shape[0]
    rows = big * SLOT
    flat = pl.BlockSpec((rows, columns), lambda i, ids: (i, 0))
    to = pl.BlockSpec((rows, depth), lambda i, ids: (i, 0))
    return launch(
        functools.partial(far_kernel, big, sent[0].shape[0] // SLOT), (nodes // rows,),
        [
            *[pl.BlockSpec(x.shape, lambda i, ids: (0, 0)) for x in sent],
            pl.BlockSpec((big, SLOT, SLOT), lambda i, ids: (i, 0, 0)), spec, flat,
        ],
        [flat, to], [jax.ShapeDtypeStruct((nodes, columns), F32), jax.ShapeDtypeStruct((nodes, depth), BF)],
        [*sent, val, block, early], name, prefetch=[ids], tokens=tokens,
    )


def forward_kernel(big, lead, send, got, ids_ref, early_ref, *refs):
    if got:
        lead_ref, rest_ref, w_beyond, h_ref, inv_ref, val_ref, lin_ref, st_ref, y_ref, *refs = refs
        receive(big, lead, pl.program_id(0), lead_ref, rest_ref, val_ref, y_ref)
    else:
        y_ref, w_beyond, h_ref, inv_ref, val_ref, lin_ref, st_ref, *refs = refs
    token_ref, *refs = refs
    mark(token_ref)
    if send:
        lead_ref, rest_ref, *refs = refs
    tot_ref, acc_ref, ref_ref = refs
    forward_body(
        big, early_ref, y_ref, w_beyond, h_ref, inv_ref, val_ref, lin_ref, st_ref, tot_ref, acc_ref, ref_ref
    )
    if not send:
        return
    i = pl.program_id(0)
    mref = at(ref_ref, 0)
    for s in range(big):
        value = (lin_ref[s * SLOT : (s + 1) * SLOT, :] - mref).astype(BF)
        later = pl.ds(pl.multiple_of((i * big + s - lead) * SLOT, SLOT), SLOT)
        if s < lead:

            @pl.when(i == 0)
            def _():
                lead_ref[s * SLOT : (s + 1) * SLOT, :] = value

            @pl.when(i > 0)
            def _():
                rest_ref[later, :] = value

        else:
            rest_ref[later, :] = value


def forward_body(big, early_ref, y_ref, w_beyond, h_ref, inv_ref, val_ref, lin_ref, st_ref, tot_ref, acc_ref, ref_ref):
    i = pl.program_id(0)
    columns = lin_ref.shape[1]
    tot_ref[...] = early_ref[...] + dot(y_ref[...], w_beyond[...])

    def mixed(s):
        high, low = split(tot_ref[s * SLOT : (s + 1) * SLOT, :])
        return dot(h_ref[s], jnp.concatenate([high, low], axis=0)) * wide(inv_ref[s], columns)

    @pl.when(i == 0)
    def _():
        acc_ref[...] = jnp.zeros_like(acc_ref)
        v = val_ref[0]
        count = jnp.sum(v, axis=0, keepdims=True)
        put(ref_ref, 0, jnp.sum(mixed(0) * wide(v, columns), axis=0, keepdims=True) / wide(count, columns))

    mref = at(ref_ref, 0)
    for s in range(big):
        lin_ref[s * SLOT : (s + 1) * SLOT, :] = mixed(s)
        for r in range(SLOT // 32):
            v = val_ref[s, r * 32 : (r + 1) * 32, :]
            away = (lin_ref[s * SLOT + r * 32 : s * SLOT + (r + 1) * 32, :] - mref) * wide(v, columns)
            acc_ref[0] += fold(away)
            acc_ref[1] += fold(away * away)
            acc_ref[2, :, :LANES] += fold(v)

    @pl.when(i == pl.num_programs(0) - 1)
    def _():
        first, second = (jnp.sum(acc_ref[k], axis=0, keepdims=True) for k in range(2))
        count = wide(jnp.sum(acc_ref[2, :, :LANES], axis=0, keepdims=True), columns)
        spread_rows(st_ref, (at(ref_ref, 0), first, second, count))


def forward(ids, big, lead, early, beyond, weight, tiles, name, tokens=(), send=False):
    h, _, inv, val = tiles
    nodes, columns = early.shape
    depth = weight.shape[0] // 4
    rows = big * SLOT
    got = len(beyond) == 2
    flat = pl.BlockSpec((rows, columns), lambda i, ids: (i, 0))
    to = pl.BlockSpec((rows, depth), lambda i, ids: (i, 0))
    whole = lambda shape: pl.BlockSpec(shape, lambda i, ids: (0, 0))
    tile = pl.BlockSpec((big, SLOT, SLOT), lambda i, ids: (i, 0, 0))
    double = pl.BlockSpec((big, SLOT, 2 * SLOT), lambda i, ids: (i, 0, 0))
    _, block = weight_block(weight, 3)
    outs = [flat, pl.BlockSpec(copies_shape(columns), lambda i, ids: (0, 0, 0))]
    shapes = [jax.ShapeDtypeStruct((nodes, columns), F32), jax.ShapeDtypeStruct(copies_shape(columns), F32)]
    if got:
        outs.append(to)
        shapes.append(jax.ShapeDtypeStruct((nodes, depth), BF))
    outs.append(token_spec())
    shapes.append(TOKEN)
    if send:
        for r in (lead * SLOT, nodes - lead * SLOT + TAIL):
            outs.append(whole((r, columns)))
            shapes.append(jax.ShapeDtypeStruct((r, columns), BF))
    return launch(
        functools.partial(forward_kernel, big, lead, send, got), (nodes // rows,),
        [flat, *([whole(x.shape) for x in beyond] if got else [to]), block, double, tile, tile],
        outs, shapes, [early, *beyond, weight, h, inv, val], name, prefetch=[ids],
        scratch=[pltpu.VMEM((rows, columns), F32), pltpu.VMEM((3, 8, columns), F32), pltpu.VMEM((8, columns), F32)],
        tokens=tokens,
    )


def columns_of(g_ref, gamma_ref, beta_ref, co_ref):
    total, mean, inv_std = combine(g_ref)
    put(co_ref, 0, mean)
    put(co_ref, 1, 0.5 * gamma_ref[...] * inv_std)
    put(co_ref, 2, 0.5 * beta_ref[...])
    put(co_ref, 3, inv_std)
    put(co_ref, 4, total)


def silu_of(away, co_ref):
    u = away * at(co_ref, 1) + at(co_ref, 2)
    return u + u * jnp.tanh(u)


def double_slope(away, co_ref):
    u = away * at(co_ref, 1) + at(co_ref, 2)
    t = jnp.tanh(u)
    return (1.0 + t) * (1.0 + u * (1.0 - t))


def coefs_kernel(st_ref, g_ref, gamma_ref, beta_ref, rest_ref, out_ref, token_ref, co_ref):
    mark(token_ref)
    columns_of(g_ref, gamma_ref, beta_ref, co_ref)
    scale = at(co_ref, 1)
    shift = (st_ref[0, 0:1, :] - at(co_ref, 0)) * scale + at(co_ref, 2)
    rows = [*split_three(scale), *split_three(shift)]
    rows.append(jnp.zeros((TAIL - len(rows), scale.shape[1]), BF))
    out_ref[...] = jnp.concatenate([r.astype(F32) for r in rows], axis=0).astype(BF)


def with_coefs(rest, stats, norm, tokens):
    nodes, columns = rest.shape
    args = [stats, *norm, rest]
    return pl.pallas_call(
        lambda *refs: coefs_kernel(*refs[: len(args)], *refs[len(args) + len(tokens) :]),
        grid=(1,),
        in_specs=[pl.BlockSpec((1, 8, columns), lambda i: (0, 0, 0))]
        + [pl.BlockSpec(v.shape, lambda i, n=v.ndim: (0,) * n) for v in norm]
        + [pl.BlockSpec(memory_space=pl.ANY)] * (1 + len(tokens)),
        out_specs=[pl.BlockSpec((TAIL, columns), lambda i: (nodes // TAIL - 1, 0)), token_spec()],
        out_shape=[jax.ShapeDtypeStruct((nodes, columns), BF), TOKEN],
        scratch_shapes=[pltpu.VMEM((8, columns), F32)],
        input_output_aliases={len(args) - 1: 0},
        compiler_params=params(24),
        cost_estimate=SMALL,
        name="coefs",
    )(*args, *tokens)


def result_kernel(big, lin_ref, val_ref, g_ref, gamma_ref, beta_ref, out_ref, token_ref, co_ref):
    mark(token_ref)

    @pl.when(pl.program_id(0) == 0)
    def _():
        columns_of(g_ref, gamma_ref, beta_ref, co_ref)

    def part(s, inner, rows):
        value = silu_of(lin_ref[rows, :] - at(co_ref, 0), co_ref)
        out_ref[rows, :] = (wide(val_ref[s, inner, :], lin_ref.shape[1]) * value).astype(out_ref.dtype)

    each_part(big, part)


def sums_kernel(big, lin_ref, cot_ref, val_ref, g_ref, gamma_ref, beta_ref, st_ref, co_ref, acc_ref):
    @pl.when(pl.program_id(0) == 0)
    def _():
        columns_of(g_ref, gamma_ref, beta_ref, co_ref)
        acc_ref[...] = jnp.zeros_like(acc_ref)

    def part(s, inner, rows):
        away = lin_ref[rows, :] - at(co_ref, 0)
        valid = wide(val_ref[s, inner, :], lin_ref.shape[1])
        grad = cot_ref[rows, :].astype(F32) * valid * double_slope(away, co_ref)
        acc_ref[0] += fold(grad)
        acc_ref[1] += fold(grad * away)

    each_part(big, part)
    finish_sums(st_ref, co_ref, acc_ref)


def finish_sums(st_ref, co_ref, acc_ref):
    @pl.when(pl.program_id(0) == pl.num_programs(0) - 1)
    def _():
        grad_beta = 0.5 * jnp.sum(acc_ref[0], axis=0, keepdims=True)
        grad_gamma = 0.5 * at(co_ref, 3) * jnp.sum(acc_ref[1], axis=0, keepdims=True)
        spread_rows(st_ref, (grad_beta, grad_gamma))


def turn_kernel(from_cot, big, lin_ref, grad_ref, inv_ref, ht_ref, g_ref, sg_ref, gamma_ref, beta_ref, out_ref, token_ref, co_ref, lg_ref):
    mark(token_ref)

    @pl.when(pl.program_id(0) == 0)
    def _():
        columns_of(g_ref, gamma_ref, beta_ref, co_ref)
        sg = sg_ref[...]
        twice = 2.0 / at(co_ref, 4)
        put(co_ref, 5, twice * jnp.sum(sg[:, 0, :], axis=0, keepdims=True))
        put(co_ref, 6, twice * at(co_ref, 3) * jnp.sum(sg[:, 1, :], axis=0, keepdims=True))

    columns = lin_ref.shape[1]

    for s in range(big):
        for r in range(SLOT // PART):
            inner = slice(r * PART, (r + 1) * PART)
            rows = slice(s * SLOT + r * PART, s * SLOT + (r + 1) * PART)
            away = lin_ref[rows, :] - at(co_ref, 0)
            if from_cot:
                grad = grad_ref[rows, :].astype(F32) * double_slope(away, co_ref)
            else:
                grad = grad_ref[rows, :]
            weight = wide(inv_ref[s, inner, :], columns)
            lg_ref[s, inner, :] = (weight * (grad - (at(co_ref, 5) + away * at(co_ref, 6)))).astype(BF)
        out_ref[s * SLOT : (s + 1) * SLOT, :] = (dot(ht_ref[s], lg_ref[s]) * at(co_ref, 1)).astype(BF)


def rows_call(kernel, big, arrays, tiles, smalls, out_dtype, scratch, name, tokens=(), limit=24):
    rows = big * SLOT
    nodes, columns = arrays[0].shape
    flat = pl.BlockSpec((rows, columns), lambda i: (i, 0))
    ins = [flat for _ in arrays]
    ins += [pl.BlockSpec((big,) + t.shape[1:], lambda i: (i, 0, 0)) for t in tiles]
    ins += [pl.BlockSpec(s.shape, lambda i, n=s.ndim: (0,) * n) for s in smalls]
    if out_dtype is None:
        out_spec = pl.BlockSpec(copies_shape(columns), lambda i: (0, 0, 0))
        out_shape = jax.ShapeDtypeStruct(copies_shape(columns), F32)
    else:
        out_spec = [flat, token_spec()]
        out_shape = [jax.ShapeDtypeStruct((nodes, columns), out_dtype), TOKEN]
    return launch(
        functools.partial(kernel, big), (nodes // rows,), ins, out_spec, out_shape, [*arrays, *tiles, *smalls], name,
        scratch=[pltpu.VMEM((8, columns), F32)] + scratch, tokens=tokens, limit=limit,
    )


def turn_call(from_cot, big, lin, grad, tiles, norm, sums, name, tokens=()):
    _, ht, inv, _ = tiles
    return rows_call(
        functools.partial(turn_kernel, from_cot), big, [lin, grad], [inv, ht], [norm[0], sums, *norm[1:]], BF,
        [pltpu.VMEM((big, SLOT, lin.shape[1]), BF)], name, tokens, 60,
    )


def backward_kernel(big, last, early_ref, y_ref, w_beyond, *refs):
    total = early_ref[...] + dot_t(y_ref[...], w_beyond[...])
    if last:
        refs[-2][...] = total
        mark(refs[-1])
        return
    lin_ref, g_ref, gamma_ref, beta_ref, out_ref, st_ref, co_ref, acc_ref = refs
    out_ref[...] = total

    @pl.when(pl.program_id(0) == 0)
    def _():
        columns_of(g_ref, gamma_ref, beta_ref, co_ref)
        acc_ref[...] = jnp.zeros_like(acc_ref)

    def part(s, inner, rows):
        away = lin_ref[rows, :] - at(co_ref, 0)
        grad = out_ref[rows, :] * double_slope(away, co_ref)
        out_ref[rows, :] = grad
        acc_ref[0] += fold(grad)
        acc_ref[1] += fold(grad * away)

    each_part(big, part)
    finish_sums(st_ref, co_ref, acc_ref)


def backward(big, early, beyond, piece, lin, norm, name, tokens=()):
    nodes, columns = early.shape
    rows = big * SLOT
    last = norm is None
    flat = pl.BlockSpec((rows, columns), lambda i: (i, 0))
    fixed = lambda s: pl.BlockSpec(s.shape, lambda i, n=s.ndim: (0,) * n)
    ins = [flat, flat, fixed(piece)]
    args = [early, beyond, piece]
    out_specs = [flat]
    out_shape = [jax.ShapeDtypeStruct((nodes, columns), F32)]
    scratch = []
    if last:
        out_specs.append(token_spec())
        out_shape.append(TOKEN)
    else:
        ins += [flat, *map(fixed, norm)]
        args += [lin, *norm]
        out_specs.append(pl.BlockSpec(copies_shape(columns), lambda i: (0, 0, 0)))
        out_shape.append(jax.ShapeDtypeStruct(copies_shape(columns), F32))
        scratch = [pltpu.VMEM((8, columns), F32), pltpu.VMEM((2, 8, columns), F32)]
    return launch(
        functools.partial(backward_kernel, big, last), (nodes // rows,), ins, out_specs, out_shape, args, name,
        scratch=scratch, tokens=tokens,
    )


def weight_kernel(spans, other, meta_ref, *refs):
    sources, h_hbm, outs, (token_ref, buf_ref, h_ref, sem) = refs[:4], refs[4], refs[5:7], refs[7:]
    mark(token_ref)
    for m in range(2):
        for n, span in enumerate(spans):
            rows = pl.ds(*span)
            if m == 0:
                pltpu.make_async_copy(h_hbm.at[rows, :], h_ref.at[rows, :], sem.at[2, n]).start()
            for k in range(2):

                @pl.when((meta_ref[4 + m] ^ other) == k)
                def _():
                    pltpu.make_async_copy(
                        sources[2 * m + k].at[rows, :], buf_ref.at[m, rows, :], sem.at[m, n]
                    ).start()

    for m in range(2):
        total = None
        for n, (start, size) in enumerate(spans):
            rows = pl.ds(start, size)
            if m == 0:
                pltpu.make_async_copy(h_hbm.at[rows, :], h_ref.at[rows, :], sem.at[2, n]).wait()
            pltpu.make_async_copy(sources[2 * m].at[rows, :], buf_ref.at[m, rows, :], sem.at[m, n]).wait()
            x, h = buf_ref[m, start : start + size, :], h_ref[start : start + size, :]
            term = lax.dot_general(x, h, (((0,), (0,)), ((), ())), preferred_element_type=F32)
            total = term if total is None else total + term
        outs[m][...] = total.astype(outs[m].dtype)


def weight_terms(meta, other, pairs, h, name, tokens=()):
    nodes, depth = pairs[0][0].shape
    columns = h.shape[1]
    pieces = 2 if nodes % 32 == 0 else 1
    spans = tuple((n * (nodes // pieces), nodes // pieces) for n in range(pieces))
    whole = pl.BlockSpec((depth, columns), lambda i, meta: (0, 0))
    return launch(
        functools.partial(weight_kernel, spans, other), (1,), [pl.BlockSpec(memory_space=pl.ANY)] * 5,
        [whole, whole, token_spec()],
        [jax.ShapeDtypeStruct((depth, columns), BF)] * 2 + [TOKEN], [*pairs[0], *pairs[1], h], name, prefetch=[meta],
        scratch=[
            pltpu.VMEM((2, nodes, depth), BF), pltpu.VMEM((nodes, columns), BF), pltpu.SemaphoreType.DMA((3, pieces))
        ],
        tokens=tokens, limit=60,
    )


def place_kernel(orders, meta_ref, *refs):
    out_ref, token_ref = refs[-2:]
    mark(token_ref)
    pieces = 1 << (len(orders[0]) - 2)
    size = out_ref.shape[0] // pieces
    for k in range(4):

        @pl.when(pl.program_id(0) == k)
        def _():
            mask = 0
            for b in orders[k // 2][1:-1]:
                mask = 2 * mask + meta_ref[4 + b]
            for n in range(pieces):
                start = pl.multiple_of((mask ^ n) * size, size)
                out_ref[pl.ds(start, size), :] = refs[k][n * size : (n + 1) * size, :].astype(F32)


def place_blocks(meta, blocks, orders, name, limit, tokens):
    depth, columns = blocks[0].shape
    return launch(
        functools.partial(place_kernel, orders), (4,), [pl.BlockSpec((depth, columns), lambda i, meta: (0, 0))] * 4,
        [
            pl.BlockSpec((depth, columns), lambda i, meta: (meta[0] ^ (i // 2 * 2) ^ (i % 2) ^ meta[4 + i // 2], 0)),
            token_spec(),
        ],
        [jax.ShapeDtypeStruct((4 * depth, columns), F32), TOKEN], blocks, name, prefetch=[meta], limit=limit,
        tokens=tokens,
    )


def after(value, *tokens):
    value, tokens = lax.optimization_barrier((value, tokens))
    return value, tokens


def across(value, axis, distance):
    size = lax.axis_size(axis)
    return lax.ppermute(value, axis, [(i, i ^ distance) for i in range(size)])


def slices_kernel(ids_ref, one_ref, two_ref, *refs):
    outs, (token_ref, sem) = refs[:6], refs[6:]
    mark(token_ref)
    depth = outs[0].shape[0]
    copies = []
    for n, out_ref in enumerate(outs):
        start = pl.multiple_of(ids_ref[1 + n % 3] * depth, depth)
        source = (one_ref, two_ref)[n // 3].at[pl.ds(start, depth), :]
        copies.append(pltpu.make_async_copy(source, out_ref, sem.at[n]))
    for copy in copies:
        copy.start()
    for copy in copies:
        copy.wait()


def weight_slices(ids, one, two):
    depth, columns = one.shape[0] // 4, one.shape[1]
    hbm = pl.BlockSpec(memory_space=pltpu.HBM)
    outs = launch(
        slices_kernel, (1,), [hbm, hbm], [hbm] * 6 + [token_spec()],
        [jax.ShapeDtypeStruct((depth, columns), one.dtype)] * 6 + [TOKEN], [one, two], "weight_slices",
        prefetch=[ids], scratch=[pltpu.SemaphoreType.DMA((6,))],
    )
    return outs[:3], outs[3:6], outs[6]


def weight_rows(slices):
    far = across(slices[1], "col", 2)
    other = across(slices[2], "col", 2)
    return [across(slices[0], "col", 1), far, across(other, "col", 1)], (far, other)


def fold_kernel(last, place, meta_ref, keep_ref, got_ref, *refs):
    mark(refs[-1])
    if last:
        refs[0][...] = (keep_ref[...].astype(F32) + got_ref[...].astype(F32)).astype(BF)
        return
    part = refs[0].shape[0]
    bit = meta_ref[4 + place]
    for out_ref, which in zip(refs[:2], (1 - bit, bit)):
        rows = pl.ds(pl.multiple_of(which * part, part), part)
        out_ref[...] = (keep_ref[rows, :].astype(F32) + got_ref[rows, :].astype(F32)).astype(BF)


def join_kernel(meta_ref, keep_ref, got_ref, out_ref, token_ref):
    mark(token_ref)
    part = keep_ref.shape[0]
    out_ref[:part, :] = keep_ref[...]
    out_ref[part:, :] = got_ref[...]


def small_call(kernel, meta, keep, got, rows, name, tokens):
    columns = keep.shape[1]
    whole = lambda r: pl.BlockSpec((r, columns), lambda i, bit: (0, 0))
    return launch(
        kernel, (1,), [whole(keep.shape[0])] * 2, [whole(r) for r in rows] + [token_spec()],
        [jax.ShapeDtypeStruct((r, columns), BF) for r in rows] + [TOKEN], [keep, got], name, prefetch=[meta], tokens=tokens,
    )


class RowSum:
    def __init__(self, axis, meta, terms, name, between=tuple):
        self.axis, self.meta, self.name = axis, meta, name
        self.bits = lax.axis_size(axis).bit_length() - 1
        self.stages = 2 * self.bits - 1
        self.orders = [list(range(self.bits)), list(range(1, self.bits)) + [0]]
        *self.send, self.sent = terms(1, ())
        *self.keep, self.kept = terms(0, (self.sent, *between()))
        self.stage = 0
        self.step(())

    def step(self, tokens):
        s, last = self.stage, self.bits - 1
        self.stage += 1
        started = []
        for n in range(2):
            rows = self.keep[n].shape[0]
            call = lambda kernel, sizes: small_call(
                kernel, self.meta, self.keep[n], self.got[n], sizes, f"{self.name}_{n}_{s}", tokens
            )
            if 0 < s < last:
                fold = functools.partial(fold_kernel, False, self.orders[n][s])
                self.send[n], self.keep[n], token = call(fold, [rows // 2] * 2)
            elif s == last or s == last + 1:
                self.keep[n], token = call(functools.partial(fold_kernel, True, 0), [rows])
            elif s > last + 1:
                self.keep[n], token = call(join_kernel, [2 * rows])
            if s > 0:
                started.append(token)
        level = s if s <= last else 2 * last - s
        moved = self.send if s < last else self.keep
        self.got = [across(moved[n], self.axis, 1 << self.orders[n][level]) for n in range(2)]
        return tuple(started)

    def next(self, *tokens):
        return self.step(tokens) if self.stage < self.stages else tokens

    def placed(self, limit, tokens=()):
        while self.stage < self.stages:
            self.step(())
        blocks = [v for n in range(2) for v in (self.keep[n], self.got[n])]
        return place_blocks(self.meta, blocks, self.orders, f"place_{self.name}", limit, tokens)


def local(
    features,
    neighbours,
    node_valid,
    weight_one,
    gamma_one,
    beta_one,
    weight_two,
    gamma_two,
    beta_two,
    cotangent,
):
    nodes, columns = features.shape
    slots = nodes // SLOT
    big = slots // 2 if slots % 2 == 0 else slots
    lead = max(1, min(big, 5 * slots // 14))
    q = lax.axis_index("col")
    place = lax.axis_index("row")
    bits = [(place >> b) & 1 for b in range(lax.axis_size("row").bit_length() - 1)]
    ids = jnp.stack([q, q ^ 1, q ^ 2, q ^ 3, *bits]).astype(jnp.int32)
    g1, b1, g2, b2 = (v.reshape(1, columns) for v in (gamma_one, beta_one, gamma_two, beta_two))

    far_one = across(features, "col", 2)
    near_one = across(features, "col", 1)
    *tiles, tiles_token = build_tiles(neighbours, node_valid)
    val = tiles[3]
    slices_one, slices_two, slices_token = weight_slices(ids, weight_one, weight_two)
    early, token = half(ids, big, [features, near_one], [weight_block(weight_one, b) for b in (0, 1)], False, "half_one")
    far_one, tokens = after(far_one, token, tiles_token, slices_token)
    beyond_one = across(far_one, "col", 1)
    early, _ = half(ids, big, [far_one], [weight_block(weight_one, 2)], False, "far_half_one", tokens, early)
    lin_one, stats, _, sent, rest = forward(ids, big, lead, early, [beyond_one], weight_one, tiles, "forward_one", tokens, send=True)

    far_lead = across(sent, "col", 2)
    norm_one = (small_gather(stats, "row"), g1, b1)
    rest, token = with_coefs(rest, stats, norm_one, (far_lead,))
    far_rest = across(rest, "col", 2)
    hidden, _ = rows_call(result_kernel, big, [lin_one], [val], norm_one, BF, [], "hidden", (token,))
    near_two = across(hidden, "col", 1)
    early, token = half(
        ids, big, [hidden, near_two], [weight_block(weight_two, b) for b in (0, 1)], False, "half_two"
    )
    far_rest, tokens = after(far_rest, token)
    beyond_two = [across(x, "col", 1) for x in (far_lead, far_rest)]
    early, far_two = far_half(
        ids, big, (far_lead, far_rest), weight_block(weight_two, 2), val, early, "far_half_two", tokens
    )
    lin_two, stats, beyond_two, token = forward(ids, big, lead, early, beyond_two, weight_two, tiles, "forward_two")
    norm_two = (small_gather(stats, "row"), g2, b2)
    slices_two, tokens = after(slices_two, token)
    rows_two, crossing = weight_rows(slices_two)

    sums = rows_call(
        sums_kernel, big, [lin_two, cotangent], [val], norm_two, None, [pltpu.VMEM((2, 8, columns), F32)], "sums_two", tokens
    )
    grads_two = small_gather(sums, "row")
    turned, _ = turn_call(True, big, lin_two, cotangent, tiles, norm_two, grads_two, "turn_two", crossing)
    far, near = across(turned, "col", 2), across(turned, "col", 1)

    def terms_two(other, tokens, h=turned):
        return weight_terms(ids, other, ((hidden, near_two), (far_two, beyond_two)), h, "terms_two", tokens)

    sum_two = RowSum("row", ids, terms_two, "two")
    weights = [weight_block(weight_two, 0), whole_block(rows_two[0])]
    early, token = half(ids, big, [turned, near], weights, True, "half_back_two", (sum_two.kept,))
    far, tokens = after(far, *sum_two.next(*sum_two.next(token)))
    beyond = across(far, "col", 1)
    slices_one, (far,) = after(slices_one, far)
    rows_one, crossing = weight_rows(slices_one)
    early, _ = half(ids, big, [far], [whole_block(rows_two[1])], True, "far_half_back_two", tokens, early)
    grad_one, sums = backward(big, early, beyond, rows_two[2], lin_one, norm_one, "backward_two", tokens)
    tokens = (*crossing, *sum_two.next(*sum_two.next(sums)))
    grads_one = small_gather(sums, "row")

    turned, _ = turn_call(False, big, lin_one, grad_one, tiles, norm_one, grads_one, "turn_one", tokens)
    far, near = across(turned, "col", 2), across(turned, "col", 1)

    def terms_one(other, tokens, h=turned):
        return weight_terms(ids, other, ((features, near_one), (far_one, beyond_one)), h, "terms_one", tokens)

    sum_one = RowSum("row", ids, terms_one, "one", lambda: (sum_two.got[1],))
    weights = [weight_block(weight_one, 0), whole_block(rows_one[0])]
    early, token = half(ids, big, [turned, near], weights, True, "half_back_one", sum_one.next())
    output, token = rows_call(result_kernel, big, [lin_two], [val], norm_two, F32, [], "output", (token,))
    started = sum_one.next(token)
    far, tokens = after(far, *started)
    beyond = across(far, "col", 1)
    tokens = (*tokens, *sum_one.next())
    early, _ = half(ids, big, [far], [whole_block(rows_one[1])], True, "far_half_back_one", tokens, early)
    grad_features, token = backward(big, early, beyond, rows_one[2], None, None, "backward_one", tokens)
    while sum_one.stage < sum_one.stages - 1:
        sum_one.next()
    tokens = sum_one.next(token)
    grad_weight_two, _ = sum_two.placed(60, tokens)
    grad_weight_one, _ = sum_one.placed(24)

    sums_one, sums_two = jnp.sum(grads_one, axis=0), jnp.sum(grads_two, axis=0)
    return (
        output,
        grad_features,
        grad_weight_one,
        sums_one[1],
        sums_one[0],
        grad_weight_two,
        sums_two[1],
        sums_two[0],
    )


def solution(mesh):
    placed = (
        P("row", "col"),
        P("row", None),
        P("row"),
        P(None, "col"),
        P("col"),
        P("col"),
        P(None, "col"),
        P("col"),
        P("col"),
        P("row", "col"),
    )
    return jax.shard_map(
        local,
        mesh=mesh,
        in_specs=placed,
        out_specs=(
            P("row", "col"),
            P("row", "col"),
            P(None, "col"),
            P("col"),
            P("col"),
            P(None, "col"),
            P("col"),
            P("col"),
        ),
        check_vma=False,
    )
```

```python
import functools

import jax
import jax.numpy as jnp
from jax import lax
from jax.experimental import pallas as pl
from jax.experimental.pallas import tpu as pltpu
from jax.sharding import PartitionSpec as P

SLOT = 128
NBR = 32
TAIL = 16
PART = 32
LANES = 128
EPSILON = 1e-05
ANY = pl.BlockSpec(memory_space=pl.ANY)
BF = jnp.bfloat16
F32 = jnp.float32


def params(limit):
    return pltpu.CompilerParams(dimension_semantics=("arbitrary",), vmem_limit_bytes=limit << 20)


SMALL = pl.CostEstimate(flops=1000000, bytes_accessed=1000, transcendentals=0)


TOKEN = jax.ShapeDtypeStruct((8, LANES), F32)


def token_spec():
    return pl.BlockSpec((8, LANES), lambda i, *_: (0, 0))


def mark(token_ref):
    token_ref[...] = jnp.zeros_like(token_ref)


def launch(kernel, grid, ins, outs, shapes, args, name, prefetch=(), scratch=(), tokens=(), limit=24):
    count = len(prefetch) + len(args)

    def body(*refs):
        kernel(*refs[:count], *refs[count + len(tokens) :])

    return pl.pallas_call(
        body,
        grid_spec=pltpu.PrefetchScalarGridSpec(
            num_scalar_prefetch=len(prefetch),
            grid=grid,
            in_specs=[*ins, *[pl.BlockSpec(memory_space=pl.ANY)] * len(tokens)],
            out_specs=outs,
            scratch_shapes=list(scratch),
        ),
        out_shape=shapes,
        compiler_params=params(limit),
        cost_estimate=SMALL,
        name=name,
    )(*prefetch, *args, *tokens)


def dot(a, b):
    return jnp.dot(a, b, preferred_element_type=F32)


def dot_t(a, b):
    return lax.dot_general(a, b, (((1,), (1,)), ((), ())), preferred_element_type=F32)


def wide(v, columns):
    return jnp.concatenate([v] * (columns // LANES), axis=1)


def tiles_kernel(nbr_ref, valid_ref, h_ref, ht_ref, inv_ref, val_ref, token_ref):
    mark(token_ref)
    entries = nbr_ref[0]
    rows = lax.broadcasted_iota(jnp.int32, (SLOT, SLOT), 0)
    cols = lax.broadcasted_iota(jnp.int32, (SLOT, SLOT), 1)
    hits = jnp.zeros((SLOT, SLOT), F32)
    degree = jnp.zeros((1, SLOT), F32)
    for k in range(entries.shape[0]):
        one = entries[k : k + 1, :]
        hits += (one == rows).astype(F32)
        degree += (one >= 0).astype(F32)
    eye = (rows == cols).astype(F32)
    joined = hits + eye
    counts = joined + joined * eye
    ht_ref[0] = counts.astype(BF)
    h_ref[0] = wide(counts.T.astype(BF), 2 * SLOT)
    valid = valid_ref[0].astype(F32)
    inv_ref[0] = jnp.broadcast_to(valid / (degree + 1.0), (SLOT, SLOT)).T
    val_ref[0] = jnp.broadcast_to(valid, (SLOT, SLOT)).T


def build_tiles(neighbours, node_valid):
    slots = neighbours.shape[0] // SLOT
    turned = neighbours.reshape(slots, SLOT, NBR).transpose(0, 2, 1)
    square = pl.BlockSpec((1, SLOT, SLOT), lambda i: (i, 0, 0))
    double = pl.BlockSpec((1, SLOT, 2 * SLOT), lambda i: (i, 0, 0))
    return launch(
        tiles_kernel, (slots,),
        [pl.BlockSpec((1, NBR, SLOT), lambda i: (i, 0, 0)), pl.BlockSpec((1, 1, SLOT), lambda i: (i, 0, 0))],
        [double, square, square, square, token_spec()],
        [
            jax.ShapeDtypeStruct((slots, SLOT, w), t)
            for w, t in ((2 * SLOT, BF), (SLOT, BF), (SLOT, F32), (SLOT, F32))
        ]
        + [TOKEN],
        [turned, node_valid.reshape(slots, 1, SLOT)], "tiles",
    )


def combine(g_ref, columns):
    mref, first, second, count = (unpacked(g_ref, k, columns) for k in range(4))
    shift = first / count
    mean_each = mref + shift
    spread_each = second - first * shift
    total = jnp.sum(count, axis=0, keepdims=True)
    mean = jnp.sum(count * mean_each, axis=0, keepdims=True) / total
    away = mean_each - mean
    variance = jnp.sum(spread_each + count * away * away, axis=0, keepdims=True) / total
    return total, mean, lax.rsqrt(variance + EPSILON)


def small_gather(copies, axis):
    return lax.all_to_all(copies, axis, split_axis=0, concat_axis=0, tiled=True)


def copies_shape(columns, count):
    rows = count * columns // LANES
    return (lax.axis_size("row"), rows + -rows % 8, LANES)


def spread_rows(out_ref, rows):
    pieces = [row[:, j : j + LANES] for row in rows for j in range(0, row.shape[1], LANES)]
    if len(pieces) < out_ref.shape[1]:
        pieces.append(jnp.zeros((out_ref.shape[1] - len(pieces), LANES), F32))
    block = jnp.concatenate(pieces, axis=0)

    def one(n, carry):
        out_ref[n] = block
        return carry

    lax.fori_loop(0, out_ref.shape[0], one, 0)


def unpacked(ref, k, columns):
    per = columns // LANES
    return jnp.concatenate([ref[:, k * per + j, :] for j in range(per)], axis=1)


def split(value):
    high = value.astype(BF)
    return high, (value - high.astype(F32)).astype(BF)


def fold(value):
    return jnp.sum(value.reshape(value.shape[0] // 8, 8, value.shape[1]), axis=0)


def at(ref, k):
    return ref[k : k + 1, :]


def put(ref, k, value):
    ref[k : k + 1, :] = value


def half(ids, big, sources, weights, turned, name, tokens=(), early=None):
    nodes, depth = sources[0].shape
    columns = weights[0][0].shape[1]
    rows = big * SLOT
    n = len(sources)
    before = [] if early is None else [early]
    product = dot_t if turned else dot

    def kernel(ids_ref, *refs):
        out_ref, token_ref = refs[-2:]
        mark(token_ref)
        terms = [product(x_ref[...], w_ref[...]) for x_ref, w_ref in zip(refs[:n], refs[n : 2 * n])]
        terms += [e_ref[...] for e_ref in refs[2 * n : -2]]
        out_ref[...] = sum(terms[1:], terms[0])

    flat = pl.BlockSpec((rows, depth), lambda i, ids: (i, 0))
    wide_flat = pl.BlockSpec((rows, columns), lambda i, ids: (i, 0))
    return launch(
        kernel, (nodes // rows,), [flat] * n + [spec for _, spec in weights] + [wide_flat for _ in before],
        [wide_flat, token_spec()], [jax.ShapeDtypeStruct((nodes, columns), F32), TOKEN],
        [*sources, *[w for w, _ in weights], *before], name, prefetch=[ids], tokens=tokens,
    )


def weight_block(weight, b):
    depth = weight.shape[0] // 4
    return weight, pl.BlockSpec((depth, weight.shape[1]), lambda i, ids: (ids[b], 0))


def whole_block(piece):
    return piece, pl.BlockSpec(piece.shape, lambda i, ids: (0, 0))


def each_part(big, body, part=32):
    for s in range(big):
        for r in range(SLOT // part):
            body(s, slice(r * part, (r + 1) * part), slice(s * SLOT + r * part, s * SLOT + (r + 1) * part))


def split_three(value):
    high, rest = split(value)
    middle, low = split(value - high.astype(F32) - rest.astype(F32))
    return high, rest, middle


def coef_rows(ref, base):
    rows = ref[base : base + TAIL, :].astype(F32)
    return tuple(rows[k : k + 1] + rows[k + 1 : k + 2] + rows[k + 2 : k + 3] for k in (0, 3))


def receive(big, lead, i, lead_ref, rest_ref, val_ref, to_ref):
    columns = to_ref.shape[1]
    scale, shift = coef_rows(rest_ref, rest_ref.shape[0] - TAIL)
    for s in range(big):
        rows = slice(s * SLOT, (s + 1) * SLOT)
        if s < lead:

            @pl.when(i == 0)
            def _():
                to_ref[rows, :] = lead_ref[rows, :]

            @pl.when(i > 0)
            def _():
                to_ref[rows, :] = rest_ref[pl.ds(pl.multiple_of((i * big + s - lead) * SLOT, SLOT), SLOT), :]

        else:
            to_ref[rows, :] = rest_ref[pl.ds(pl.multiple_of((i * big + s - lead) * SLOT, SLOT), SLOT), :]

    def part(s, inner, rows):
        u = to_ref[rows, :].astype(F32) * scale + shift
        to_ref[rows, :] = (wide(val_ref[s, inner, :], columns) * (u + u * jnp.tanh(u))).astype(BF)

    each_part(big, part)


def far_kernel(big, lead, ids_ref, lead_ref, rest_ref, val_ref, w_ref, early_ref, out_ref, to_ref):
    receive(big, lead, pl.program_id(0), lead_ref, rest_ref, val_ref, to_ref)
    out_ref[...] = early_ref[...] + dot(to_ref[...], w_ref[...])


def far_half(ids, big, sent, weight, val, early, name, tokens=()):
    nodes, columns = early.shape
    block, spec = weight
    depth = block.shape[1] if spec.block_shape is None else spec.block_shape[0]
    rows = big * SLOT
    flat = pl.BlockSpec((rows, columns), lambda i, ids: (i, 0))
    to = pl.BlockSpec((rows, depth), lambda i, ids: (i, 0))
    return launch(
        functools.partial(far_kernel, big, sent[0].shape[0] // SLOT), (nodes // rows,),
        [
            *[pl.BlockSpec(x.shape, lambda i, ids: (0, 0)) for x in sent],
            pl.BlockSpec((big, SLOT, SLOT), lambda i, ids: (i, 0, 0)), spec, flat,
        ],
        [flat, to], [jax.ShapeDtypeStruct((nodes, columns), F32), jax.ShapeDtypeStruct((nodes, depth), BF)],
        [*sent, val, block, early], name, prefetch=[ids], tokens=tokens,
    )


def forward_kernel(big, lead, send, got, ids_ref, early_ref, *refs):
    if got:
        lead_ref, rest_ref, w_beyond, h_ref, inv_ref, val_ref, lin_ref, st_ref, y_ref, *refs = refs
        receive(big, lead, pl.program_id(0), lead_ref, rest_ref, val_ref, y_ref)
    else:
        y_ref, w_beyond, h_ref, inv_ref, val_ref, lin_ref, st_ref, *refs = refs
    token_ref, *refs = refs
    mark(token_ref)
    if send:
        lead_ref, rest_ref, *refs = refs
    tot_ref, acc_ref, ref_ref = refs
    forward_body(
        big, early_ref, y_ref, w_beyond, h_ref, inv_ref, val_ref, lin_ref, st_ref, tot_ref, acc_ref, ref_ref
    )
    if not send:
        return
    i = pl.program_id(0)
    mref = at(ref_ref, 0)
    for s in range(big):
        value = (lin_ref[s * SLOT : (s + 1) * SLOT, :] - mref).astype(BF)
        later = pl.ds(pl.multiple_of((i * big + s - lead) * SLOT, SLOT), SLOT)
        if s < lead:

            @pl.when(i == 0)
            def _():
                lead_ref[s * SLOT : (s + 1) * SLOT, :] = value

            @pl.when(i > 0)
            def _():
                rest_ref[later, :] = value

        else:
            rest_ref[later, :] = value


def forward_body(big, early_ref, y_ref, w_beyond, h_ref, inv_ref, val_ref, lin_ref, st_ref, tot_ref, acc_ref, ref_ref):
    i = pl.program_id(0)
    columns = lin_ref.shape[1]
    tot_ref[...] = early_ref[...] + dot(y_ref[...], w_beyond[...])

    def mixed(s):
        high, low = split(tot_ref[s * SLOT : (s + 1) * SLOT, :])
        return dot(h_ref[s], jnp.concatenate([high, low], axis=0)) * wide(inv_ref[s], columns)

    @pl.when(i == 0)
    def _():
        acc_ref[...] = jnp.zeros_like(acc_ref)
        v = val_ref[0]
        count = jnp.sum(v, axis=0, keepdims=True)
        put(ref_ref, 0, jnp.sum(mixed(0) * wide(v, columns), axis=0, keepdims=True) / wide(count, columns))

    mref = at(ref_ref, 0)
    for s in range(big):
        lin_ref[s * SLOT : (s + 1) * SLOT, :] = mixed(s)
        for r in range(SLOT // 32):
            v = val_ref[s, r * 32 : (r + 1) * 32, :]
            away = (lin_ref[s * SLOT + r * 32 : s * SLOT + (r + 1) * 32, :] - mref) * wide(v, columns)
            acc_ref[0] += fold(away)
            acc_ref[1] += fold(away * away)
            acc_ref[2, :, :LANES] += fold(v)

    @pl.when(i == pl.num_programs(0) - 1)
    def _():
        first, second = (jnp.sum(acc_ref[k], axis=0, keepdims=True) for k in range(2))
        count = wide(jnp.sum(acc_ref[2, :, :LANES], axis=0, keepdims=True), columns)
        spread_rows(st_ref, (at(ref_ref, 0), first, second, count))


def forward(ids, big, lead, early, beyond, weight, tiles, name, tokens=(), send=False):
    h, _, inv, val = tiles
    nodes, columns = early.shape
    depth = weight.shape[0] // 4
    rows = big * SLOT
    got = len(beyond) == 2
    flat = pl.BlockSpec((rows, columns), lambda i, ids: (i, 0))
    to = pl.BlockSpec((rows, depth), lambda i, ids: (i, 0))
    whole = lambda shape: pl.BlockSpec(shape, lambda i, ids: (0, 0))
    tile = pl.BlockSpec((big, SLOT, SLOT), lambda i, ids: (i, 0, 0))
    double = pl.BlockSpec((big, SLOT, 2 * SLOT), lambda i, ids: (i, 0, 0))
    _, block = weight_block(weight, 3)
    outs = [flat, pl.BlockSpec(copies_shape(columns, 4), lambda i, ids: (0, 0, 0))]
    shapes = [jax.ShapeDtypeStruct((nodes, columns), F32), jax.ShapeDtypeStruct(copies_shape(columns, 4), F32)]
    if got:
        outs.append(to)
        shapes.append(jax.ShapeDtypeStruct((nodes, depth), BF))
    outs.append(token_spec())
    shapes.append(TOKEN)
    if send:
        for r in (lead * SLOT, nodes - lead * SLOT + TAIL):
            outs.append(whole((r, columns)))
            shapes.append(jax.ShapeDtypeStruct((r, columns), BF))
    return launch(
        functools.partial(forward_kernel, big, lead, send, got), (nodes // rows,),
        [flat, *([whole(x.shape) for x in beyond] if got else [to]), block, double, tile, tile],
        outs, shapes, [early, *beyond, weight, h, inv, val], name, prefetch=[ids],
        scratch=[pltpu.VMEM((rows, columns), F32), pltpu.VMEM((3, 8, columns), F32), pltpu.VMEM((8, columns), F32)],
        tokens=tokens,
    )


def columns_of(g_ref, gamma_ref, beta_ref, co_ref):
    total, mean, inv_std = combine(g_ref, gamma_ref.shape[1])
    put(co_ref, 0, mean)
    put(co_ref, 1, 0.5 * gamma_ref[...] * inv_std)
    put(co_ref, 2, 0.5 * beta_ref[...])
    put(co_ref, 3, inv_std)
    put(co_ref, 4, total)


def silu_of(away, co_ref):
    u = away * at(co_ref, 1) + at(co_ref, 2)
    return u + u * jnp.tanh(u)


def double_slope(away, co_ref):
    u = away * at(co_ref, 1) + at(co_ref, 2)
    t = jnp.tanh(u)
    return (1.0 + t) * (1.0 + u * (1.0 - t))


def coefs_kernel(st_ref, g_ref, gamma_ref, beta_ref, rest_ref, out_ref, token_ref, co_ref):
    mark(token_ref)
    columns_of(g_ref, gamma_ref, beta_ref, co_ref)
    scale = at(co_ref, 1)
    reference = unpacked(st_ref, 0, scale.shape[1])
    shift = (reference - at(co_ref, 0)) * scale + at(co_ref, 2)
    rows = [*split_three(scale), *split_three(shift)]
    rows.append(jnp.zeros((TAIL - len(rows), scale.shape[1]), BF))
    out_ref[...] = jnp.concatenate([r.astype(F32) for r in rows], axis=0).astype(BF)


def with_coefs(rest, stats, norm, tokens):
    nodes, columns = rest.shape
    args = [stats, *norm, rest]
    return pl.pallas_call(
        lambda *refs: coefs_kernel(*refs[: len(args)], *refs[len(args) + len(tokens) :]),
        grid=(1,),
        in_specs=[pl.BlockSpec((1,) + stats.shape[1:], lambda i: (0, 0, 0))]
        + [pl.BlockSpec(v.shape, lambda i, n=v.ndim: (0,) * n) for v in norm]
        + [pl.BlockSpec(memory_space=pl.ANY)] * (1 + len(tokens)),
        out_specs=[pl.BlockSpec((TAIL, columns), lambda i: (nodes // TAIL - 1, 0)), token_spec()],
        out_shape=[jax.ShapeDtypeStruct((nodes, columns), BF), TOKEN],
        scratch_shapes=[pltpu.VMEM((8, columns), F32)],
        input_output_aliases={len(args) - 1: 0},
        compiler_params=params(24),
        cost_estimate=SMALL,
        name="coefs",
    )(*args, *tokens)


def result_kernel(big, lin_ref, val_ref, g_ref, gamma_ref, beta_ref, out_ref, token_ref, co_ref):
    mark(token_ref)

    @pl.when(pl.program_id(0) == 0)
    def _():
        columns_of(g_ref, gamma_ref, beta_ref, co_ref)

    def part(s, inner, rows):
        value = silu_of(lin_ref[rows, :] - at(co_ref, 0), co_ref)
        out_ref[rows, :] = (wide(val_ref[s, inner, :], lin_ref.shape[1]) * value).astype(out_ref.dtype)

    each_part(big, part)


def sums_kernel(big, lin_ref, cot_ref, val_ref, g_ref, gamma_ref, beta_ref, st_ref, co_ref, acc_ref):
    @pl.when(pl.program_id(0) == 0)
    def _():
        columns_of(g_ref, gamma_ref, beta_ref, co_ref)
        acc_ref[...] = jnp.zeros_like(acc_ref)

    def part(s, inner, rows):
        away = lin_ref[rows, :] - at(co_ref, 0)
        valid = wide(val_ref[s, inner, :], lin_ref.shape[1])
        grad = cot_ref[rows, :].astype(F32) * valid * double_slope(away, co_ref)
        acc_ref[0] += fold(grad)
        acc_ref[1] += fold(grad * away)

    each_part(big, part)
    finish_sums(st_ref, co_ref, acc_ref)


def finish_sums(st_ref, co_ref, acc_ref):
    @pl.when(pl.program_id(0) == pl.num_programs(0) - 1)
    def _():
        grad_beta = 0.5 * jnp.sum(acc_ref[0], axis=0, keepdims=True)
        grad_gamma = 0.5 * at(co_ref, 3) * jnp.sum(acc_ref[1], axis=0, keepdims=True)
        spread_rows(st_ref, (grad_beta, grad_gamma))


def turn_kernel(from_cot, big, lin_ref, grad_ref, inv_ref, ht_ref, g_ref, sg_ref, gamma_ref, beta_ref, out_ref, token_ref, co_ref, lg_ref):
    mark(token_ref)

    @pl.when(pl.program_id(0) == 0)
    def _():
        columns_of(g_ref, gamma_ref, beta_ref, co_ref)
        twice = 2.0 / at(co_ref, 4)
        put(co_ref, 5, twice * jnp.sum(unpacked(sg_ref, 0, lin_ref.shape[1]), axis=0, keepdims=True))
        put(co_ref, 6, twice * at(co_ref, 3) * jnp.sum(unpacked(sg_ref, 1, lin_ref.shape[1]), axis=0, keepdims=True))

    columns = lin_ref.shape[1]

    for s in range(big):
        for r in range(SLOT // PART):
            inner = slice(r * PART, (r + 1) * PART)
            rows = slice(s * SLOT + r * PART, s * SLOT + (r + 1) * PART)
            away = lin_ref[rows, :] - at(co_ref, 0)
            if from_cot:
                grad = grad_ref[rows, :].astype(F32) * double_slope(away, co_ref)
            else:
                grad = grad_ref[rows, :]
            weight = wide(inv_ref[s, inner, :], columns)
            lg_ref[s, inner, :] = (weight * (grad - (at(co_ref, 5) + away * at(co_ref, 6)))).astype(BF)
        out_ref[s * SLOT : (s + 1) * SLOT, :] = (dot(ht_ref[s], lg_ref[s]) * at(co_ref, 1)).astype(BF)


def rows_call(kernel, big, arrays, tiles, smalls, out_dtype, scratch, name, tokens=(), limit=24):
    rows = big * SLOT
    nodes, columns = arrays[0].shape
    flat = pl.BlockSpec((rows, columns), lambda i: (i, 0))
    ins = [flat for _ in arrays]
    ins += [pl.BlockSpec((big,) + t.shape[1:], lambda i: (i, 0, 0)) for t in tiles]
    ins += [pl.BlockSpec(s.shape, lambda i, n=s.ndim: (0,) * n) for s in smalls]
    if out_dtype is None:
        out_spec = pl.BlockSpec(copies_shape(columns, 2), lambda i: (0, 0, 0))
        out_shape = jax.ShapeDtypeStruct(copies_shape(columns, 2), F32)
    else:
        out_spec = [flat, token_spec()]
        out_shape = [jax.ShapeDtypeStruct((nodes, columns), out_dtype), TOKEN]
    return launch(
        functools.partial(kernel, big), (nodes // rows,), ins, out_spec, out_shape, [*arrays, *tiles, *smalls], name,
        scratch=[pltpu.VMEM((8, columns), F32)] + scratch, tokens=tokens, limit=limit,
    )


def turn_call(from_cot, big, lin, grad, tiles, norm, sums, name, tokens=()):
    _, ht, inv, _ = tiles
    return rows_call(
        functools.partial(turn_kernel, from_cot), big, [lin, grad], [inv, ht], [norm[0], sums, *norm[1:]], BF,
        [pltpu.VMEM((big, SLOT, lin.shape[1]), BF)], name, tokens, 60,
    )


def backward_kernel(big, last, early_ref, y_ref, w_beyond, *refs):
    total = early_ref[...] + dot_t(y_ref[...], w_beyond[...])
    if last:
        refs[-2][...] = total
        mark(refs[-1])
        return
    lin_ref, g_ref, gamma_ref, beta_ref, out_ref, st_ref, co_ref, acc_ref = refs
    out_ref[...] = total

    @pl.when(pl.program_id(0) == 0)
    def _():
        columns_of(g_ref, gamma_ref, beta_ref, co_ref)
        acc_ref[...] = jnp.zeros_like(acc_ref)

    def part(s, inner, rows):
        away = lin_ref[rows, :] - at(co_ref, 0)
        grad = out_ref[rows, :] * double_slope(away, co_ref)
        out_ref[rows, :] = grad
        acc_ref[0] += fold(grad)
        acc_ref[1] += fold(grad * away)

    each_part(big, part)
    finish_sums(st_ref, co_ref, acc_ref)


def backward(big, early, beyond, piece, lin, norm, name, tokens=()):
    nodes, columns = early.shape
    rows = big * SLOT
    last = norm is None
    flat = pl.BlockSpec((rows, columns), lambda i: (i, 0))
    fixed = lambda s: pl.BlockSpec(s.shape, lambda i, n=s.ndim: (0,) * n)
    ins = [flat, flat, fixed(piece)]
    args = [early, beyond, piece]
    out_specs = [flat]
    out_shape = [jax.ShapeDtypeStruct((nodes, columns), F32)]
    scratch = []
    if last:
        out_specs.append(token_spec())
        out_shape.append(TOKEN)
    else:
        ins += [flat, *map(fixed, norm)]
        args += [lin, *norm]
        out_specs.append(pl.BlockSpec(copies_shape(columns, 2), lambda i: (0, 0, 0)))
        out_shape.append(jax.ShapeDtypeStruct(copies_shape(columns, 2), F32))
        scratch = [pltpu.VMEM((8, columns), F32), pltpu.VMEM((2, 8, columns), F32)]
    return launch(
        functools.partial(backward_kernel, big, last), (nodes // rows,), ins, out_specs, out_shape, args, name,
        scratch=scratch, tokens=tokens,
    )


def weight_kernel(spans, other, meta_ref, *refs):
    sources, h_hbm, outs, (token_ref, buf_ref, h_ref, sem) = refs[:4], refs[4], refs[5:7], refs[7:]
    mark(token_ref)
    for m in range(2):
        for n, span in enumerate(spans):
            rows = pl.ds(*span)
            if m == 0:
                pltpu.make_async_copy(h_hbm.at[rows, :], h_ref.at[rows, :], sem.at[2, n]).start()
            for k in range(2):

                @pl.when((meta_ref[4 + m] ^ other) == k)
                def _():
                    pltpu.make_async_copy(
                        sources[2 * m + k].at[rows, :], buf_ref.at[m, rows, :], sem.at[m, n]
                    ).start()

    for m in range(2):
        total = None
        for n, (start, size) in enumerate(spans):
            rows = pl.ds(start, size)
            if m == 0:
                pltpu.make_async_copy(h_hbm.at[rows, :], h_ref.at[rows, :], sem.at[2, n]).wait()
            pltpu.make_async_copy(sources[2 * m].at[rows, :], buf_ref.at[m, rows, :], sem.at[m, n]).wait()
            x, h = buf_ref[m, start : start + size, :], h_ref[start : start + size, :]
            term = lax.dot_general(x, h, (((0,), (0,)), ((), ())), preferred_element_type=F32)
            total = term if total is None else total + term
        outs[m][...] = total.astype(outs[m].dtype)


def weight_terms(meta, other, pairs, h, name, tokens=()):
    nodes, depth = pairs[0][0].shape
    columns = h.shape[1]
    pieces = 2 if nodes % 32 == 0 else 1
    spans = tuple((n * (nodes // pieces), nodes // pieces) for n in range(pieces))
    whole = pl.BlockSpec((depth, columns), lambda i, meta: (0, 0))
    return launch(
        functools.partial(weight_kernel, spans, other), (1,), [pl.BlockSpec(memory_space=pl.ANY)] * 5,
        [whole, whole, token_spec()],
        [jax.ShapeDtypeStruct((depth, columns), BF)] * 2 + [TOKEN], [*pairs[0], *pairs[1], h], name, prefetch=[meta],
        scratch=[
            pltpu.VMEM((2, nodes, depth), BF), pltpu.VMEM((nodes, columns), BF), pltpu.SemaphoreType.DMA((3, pieces))
        ],
        tokens=tokens, limit=60,
    )


def place_kernel(orders, meta_ref, *refs):
    out_ref, token_ref = refs[-2:]
    mark(token_ref)
    pieces = 1 << (len(orders[0]) - 2)
    size = out_ref.shape[0] // pieces
    for k in range(4):

        @pl.when(pl.program_id(0) == k)
        def _():
            mask = 0
            for b in orders[k // 2][1:-1]:
                mask = 2 * mask + meta_ref[4 + b]
            for n in range(pieces):
                start = pl.multiple_of((mask ^ n) * size, size)
                out_ref[pl.ds(start, size), :] = refs[k][n * size : (n + 1) * size, :].astype(F32)


def place_blocks(meta, blocks, orders, name, limit, tokens):
    depth, columns = blocks[0].shape
    return launch(
        functools.partial(place_kernel, orders), (4,), [pl.BlockSpec((depth, columns), lambda i, meta: (0, 0))] * 4,
        [
            pl.BlockSpec((depth, columns), lambda i, meta: (meta[0] ^ (i // 2 * 2) ^ (i % 2) ^ meta[4 + i // 2], 0)),
            token_spec(),
        ],
        [jax.ShapeDtypeStruct((4 * depth, columns), F32), TOKEN], blocks, name, prefetch=[meta], limit=limit,
        tokens=tokens,
    )


def after(value, *tokens):
    value, tokens = lax.optimization_barrier((value, tokens))
    return value, tokens


def across(value, axis, distance):
    size = lax.axis_size(axis)
    return lax.ppermute(value, axis, [(i, i ^ distance) for i in range(size)])


def slices_kernel(ids_ref, one_ref, two_ref, *refs):
    outs, (token_ref, sem) = refs[:6], refs[6:]
    mark(token_ref)
    depth = outs[0].shape[0]
    copies = []
    for n, out_ref in enumerate(outs):
        start = pl.multiple_of(ids_ref[1 + n % 3] * depth, depth)
        source = (one_ref, two_ref)[n // 3].at[pl.ds(start, depth), :]
        copies.append(pltpu.make_async_copy(source, out_ref, sem.at[n]))
    for copy in copies:
        copy.start()
    for copy in copies:
        copy.wait()


def weight_slices(ids, one, two):
    depth, columns = one.shape[0] // 4, one.shape[1]
    hbm = pl.BlockSpec(memory_space=pltpu.HBM)
    outs = launch(
        slices_kernel, (1,), [hbm, hbm], [hbm] * 6 + [token_spec()],
        [jax.ShapeDtypeStruct((depth, columns), one.dtype)] * 6 + [TOKEN], [one, two], "weight_slices",
        prefetch=[ids], scratch=[pltpu.SemaphoreType.DMA((6,))],
    )
    return outs[:3], outs[3:6], outs[6]


def weight_rows(slices):
    far = across(slices[1], "col", 2)
    other = across(slices[2], "col", 2)
    return [across(slices[0], "col", 1), far, across(other, "col", 1)], (far, other)


def fold_kernel(last, place, meta_ref, keep_ref, got_ref, *refs):
    mark(refs[-1])
    if last:
        refs[0][...] = (keep_ref[...].astype(F32) + got_ref[...].astype(F32)).astype(BF)
        return
    part = refs[0].shape[0]
    bit = meta_ref[4 + place]
    for out_ref, which in zip(refs[:2], (1 - bit, bit)):
        rows = pl.ds(pl.multiple_of(which * part, part), part)
        out_ref[...] = (keep_ref[rows, :].astype(F32) + got_ref[rows, :].astype(F32)).astype(BF)


def join_kernel(meta_ref, keep_ref, got_ref, out_ref, token_ref):
    mark(token_ref)
    part = keep_ref.shape[0]
    out_ref[:part, :] = keep_ref[...]
    out_ref[part:, :] = got_ref[...]


def small_call(kernel, meta, keep, got, rows, name, tokens):
    columns = keep.shape[1]
    whole = lambda r: pl.BlockSpec((r, columns), lambda i, bit: (0, 0))
    return launch(
        kernel, (1,), [whole(keep.shape[0])] * 2, [whole(r) for r in rows] + [token_spec()],
        [jax.ShapeDtypeStruct((r, columns), BF) for r in rows] + [TOKEN], [keep, got], name, prefetch=[meta], tokens=tokens,
    )


class RowSum:
    def __init__(self, axis, meta, terms, name, between=tuple):
        self.axis, self.meta, self.name = axis, meta, name
        self.bits = lax.axis_size(axis).bit_length() - 1
        self.stages = 2 * self.bits - 1
        self.orders = [list(range(self.bits)), list(range(1, self.bits)) + [0]]
        *self.send, self.sent = terms(1, ())
        *self.keep, self.kept = terms(0, (self.sent, *between()))
        self.done = [0, 0]
        self.got = [None, None]
        self.step(())

    def advance(self, n, *tokens):
        s, last = self.done[n], self.bits - 1
        if s == self.stages:
            return tokens
        self.done[n] += 1
        started = ()
        rows = self.keep[n].shape[0]
        call = lambda kernel, sizes: small_call(
            kernel, self.meta, self.keep[n], self.got[n], sizes, f"{self.name}_{n}_{s}", tokens
        )
        if 0 < s < last:
            fold = functools.partial(fold_kernel, False, self.orders[n][s])
            self.send[n], self.keep[n], *started = call(fold, [rows // 2] * 2)
        elif s == last or s == last + 1:
            self.keep[n], *started = call(functools.partial(fold_kernel, True, 0), [rows])
        elif s > last + 1:
            self.keep[n], *started = call(join_kernel, [2 * rows])
        level = s if s <= last else 2 * last - s
        moved = self.send if s < last else self.keep
        self.got[n] = across(moved[n], self.axis, 1 << self.orders[n][level])
        return tuple(started)

    def step(self, tokens):
        return (*self.advance(0, *tokens), *self.advance(1, *tokens))

    def next(self, *tokens):
        return self.step(tokens) if min(self.done) < self.stages else tokens

    def placed(self, limit, tokens=()):
        while min(self.done) < self.stages:
            self.step(())
        blocks = [v for n in range(2) for v in (self.keep[n], self.got[n])]
        return place_blocks(self.meta, blocks, self.orders, f"place_{self.name}", limit, tokens)


def local(
    features,
    neighbours,
    node_valid,
    weight_one,
    gamma_one,
    beta_one,
    weight_two,
    gamma_two,
    beta_two,
    cotangent,
):
    nodes, columns = features.shape
    slots = nodes // SLOT
    big = slots // 2 if slots % 2 == 0 else slots
    lead = max(1, min(big, 5 * slots // 14))
    q = lax.axis_index("col")
    place = lax.axis_index("row")
    bits = [(place >> b) & 1 for b in range(lax.axis_size("row").bit_length() - 1)]
    ids = jnp.stack([q, q ^ 1, q ^ 2, q ^ 3, *bits]).astype(jnp.int32)
    g1, b1, g2, b2 = (v.reshape(1, columns) for v in (gamma_one, beta_one, gamma_two, beta_two))

    far_one = across(features, "col", 2)
    near_one = across(features, "col", 1)
    *tiles, tiles_token = build_tiles(neighbours, node_valid)
    val = tiles[3]
    slices_one, slices_two, slices_token = weight_slices(ids, weight_one, weight_two)
    early, token = half(ids, big, [features, near_one], [weight_block(weight_one, b) for b in (0, 1)], False, "half_one")
    far_one, tokens = after(far_one, token, tiles_token, slices_token)
    beyond_one = across(far_one, "col", 1)
    early, _ = half(ids, big, [far_one], [weight_block(weight_one, 2)], False, "far_half_one", tokens, early)
    lin_one, stats, _, sent, rest = forward(ids, big, lead, early, [beyond_one], weight_one, tiles, "forward_one", tokens, send=True)

    far_lead = across(sent, "col", 2)
    norm_one = (small_gather(stats, "row"), g1, b1)
    rest, token = with_coefs(rest, stats, norm_one, (far_lead,))
    far_rest = across(rest, "col", 2)
    hidden, _ = rows_call(result_kernel, big, [lin_one], [val], norm_one, BF, [], "hidden", (token,))
    near_two = across(hidden, "col", 1)
    early, token = half(
        ids, big, [hidden, near_two], [weight_block(weight_two, b) for b in (0, 1)], False, "half_two"
    )
    far_rest, tokens = after(far_rest, token)
    beyond_two = [across(x, "col", 1) for x in (far_lead, far_rest)]
    early, far_two = far_half(
        ids, big, (far_lead, far_rest), weight_block(weight_two, 2), val, early, "far_half_two", tokens
    )
    lin_two, stats, beyond_two, token = forward(ids, big, lead, early, beyond_two, weight_two, tiles, "forward_two")
    norm_two = (small_gather(stats, "row"), g2, b2)
    slices_two, tokens = after(slices_two, token)
    rows_two, crossing = weight_rows(slices_two)

    sums = rows_call(
        sums_kernel, big, [lin_two, cotangent], [val], norm_two, None, [pltpu.VMEM((2, 8, columns), F32)], "sums_two", tokens
    )
    grads_two = small_gather(sums, "row")
    turned, _ = turn_call(True, big, lin_two, cotangent, tiles, norm_two, grads_two, "turn_two", crossing)
    far, near = across(turned, "col", 2), across(turned, "col", 1)

    def terms_two(other, tokens, h=turned):
        return weight_terms(ids, other, ((hidden, near_two), (far_two, beyond_two)), h, "terms_two", tokens)

    sum_two = RowSum("row", ids, terms_two, "two")
    weights = [weight_block(weight_two, 0), whole_block(rows_two[0])]
    early, token = half(ids, big, [turned, near], weights, True, "half_back_two", (sum_two.kept,))
    far, tokens = after(far, *sum_two.next(*sum_two.next(token)))
    beyond = across(far, "col", 1)
    slices_one, (far,) = after(slices_one, far)
    rows_one, crossing = weight_rows(slices_one)
    early, _ = half(ids, big, [far], [whole_block(rows_two[1])], True, "far_half_back_two", tokens, early)
    grad_one, sums = backward(big, early, beyond, rows_two[2], lin_one, norm_one, "backward_two", tokens)
    tokens = (*crossing, *sum_two.next(sums))
    grads_one = small_gather(sums, "row")

    turned, _ = turn_call(False, big, lin_one, grad_one, tiles, norm_one, grads_one, "turn_one", tokens)
    far, near = across(turned, "col", 2), across(turned, "col", 1)

    def terms_one(other, tokens, h=turned):
        return weight_terms(ids, other, ((features, near_one), (far_one, beyond_one)), h, "terms_one", tokens)

    sum_one = RowSum("row", ids, terms_one, "one", lambda: sum_two.next())
    weights = [weight_block(weight_one, 0), whole_block(rows_one[0])]
    early, token = half(ids, big, [turned, near], weights, True, "half_back_one", sum_one.next())
    output, token = rows_call(result_kernel, big, [lin_two], [val], norm_two, F32, [], "output", (token,))
    started = sum_one.next(token)
    far, tokens = after(far, *started)
    beyond = across(far, "col", 1)
    tokens = (*tokens, *sum_one.next())
    early, _ = half(ids, big, [far], [whole_block(rows_one[1])], True, "far_half_back_one", (*tokens, sum_two.got[1]), early)
    grad_features, token = backward(big, early, beyond, rows_one[2], None, None, "backward_one", tokens)
    while min(sum_one.done) < sum_one.stages - 1:
        sum_one.next()
    tokens = sum_one.next(token)
    grad_weight_two, _ = sum_two.placed(60, tokens)
    grad_weight_one, _ = sum_one.placed(24)

    per = columns // LANES
    sums_one, sums_two = (jnp.sum(g, axis=0)[: 2 * per].reshape(2, columns) for g in (grads_one, grads_two))
    return (
        output,
        grad_features,
        grad_weight_one,
        sums_one[1],
        sums_one[0],
        grad_weight_two,
        sums_two[1],
        sums_two[0],
    )


def solution(mesh):
    placed = (
        P("row", "col"),
        P("row", None),
        P("row"),
        P(None, "col"),
        P("col"),
        P("col"),
        P(None, "col"),
        P("col"),
        P("col"),
        P("row", "col"),
    )
    return jax.shard_map(
        local,
        mesh=mesh,
        in_specs=placed,
        out_specs=(
            P("row", "col"),
            P("row", "col"),
            P(None, "col"),
            P("col"),
            P("col"),
            P(None, "col"),
            P("col"),
            P("col"),
        ),
        check_vma=False,
    )
```

```python
import functools

import jax
import jax.numpy as jnp
from jax import lax
from jax.experimental import pallas as pl
from jax.experimental.pallas import tpu as pltpu
from jax.sharding import PartitionSpec as P

SLOT = 128
NBR = 32
TAIL = 16
PART = 32
LANES = 128
EPSILON = 1e-05
ANY = pl.BlockSpec(memory_space=pl.ANY)
BF = jnp.bfloat16
F32 = jnp.float32


def params(limit):
    return pltpu.CompilerParams(dimension_semantics=("arbitrary",), vmem_limit_bytes=limit << 20)


SMALL = pl.CostEstimate(flops=1000000, bytes_accessed=1000, transcendentals=0)


TOKEN = jax.ShapeDtypeStruct((8, LANES), F32)


def token_spec():
    return pl.BlockSpec((8, LANES), lambda i, *_: (0, 0))


def mark(token_ref):
    token_ref[...] = jnp.zeros_like(token_ref)


def launch(kernel, grid, ins, outs, shapes, args, name, prefetch=(), scratch=(), tokens=(), limit=24):
    count = len(prefetch) + len(args)

    def body(*refs):
        kernel(*refs[:count], *refs[count + len(tokens) :])

    return pl.pallas_call(
        body,
        grid_spec=pltpu.PrefetchScalarGridSpec(
            num_scalar_prefetch=len(prefetch),
            grid=grid,
            in_specs=[*ins, *[pl.BlockSpec(memory_space=pl.ANY)] * len(tokens)],
            out_specs=outs,
            scratch_shapes=list(scratch),
        ),
        out_shape=shapes,
        compiler_params=params(limit),
        cost_estimate=SMALL,
        name=name,
    )(*prefetch, *args, *tokens)


def dot(a, b):
    return jnp.dot(a, b, preferred_element_type=F32)


def dot_t(a, b):
    return lax.dot_general(a, b, (((1,), (1,)), ((), ())), preferred_element_type=F32)


def wide(v, columns):
    return jnp.concatenate([v] * (columns // LANES), axis=1)


def tiles_kernel(nbr_ref, valid_ref, h_ref, ht_ref, inv_ref, val_ref, token_ref):
    mark(token_ref)
    entries = nbr_ref[0]
    rows = lax.broadcasted_iota(jnp.int32, (SLOT, SLOT), 0)
    cols = lax.broadcasted_iota(jnp.int32, (SLOT, SLOT), 1)
    hits = jnp.zeros((SLOT, SLOT), F32)
    degree = jnp.zeros((1, SLOT), F32)
    for k in range(entries.shape[0]):
        one = entries[k : k + 1, :]
        hits += (one == rows).astype(F32)
        degree += (one >= 0).astype(F32)
    eye = (rows == cols).astype(F32)
    joined = hits + eye
    counts = joined + joined * eye
    ht_ref[0] = counts.astype(BF)
    h_ref[0] = wide(counts.T.astype(BF), 2 * SLOT)
    valid = valid_ref[0].astype(F32)
    inv_ref[0] = jnp.broadcast_to(valid / (degree + 1.0), (SLOT, SLOT)).T
    val_ref[0] = jnp.broadcast_to(valid, (SLOT, SLOT)).T


def build_tiles(neighbours, node_valid):
    slots = neighbours.shape[0] // SLOT
    turned = neighbours.reshape(slots, SLOT, NBR).transpose(0, 2, 1)
    square = pl.BlockSpec((1, SLOT, SLOT), lambda i: (i, 0, 0))
    double = pl.BlockSpec((1, SLOT, 2 * SLOT), lambda i: (i, 0, 0))
    return launch(
        tiles_kernel, (slots,),
        [pl.BlockSpec((1, NBR, SLOT), lambda i: (i, 0, 0)), pl.BlockSpec((1, 1, SLOT), lambda i: (i, 0, 0))],
        [double, square, square, square, token_spec()],
        [
            jax.ShapeDtypeStruct((slots, SLOT, w), t)
            for w, t in ((2 * SLOT, BF), (SLOT, BF), (SLOT, F32), (SLOT, F32))
        ]
        + [TOKEN],
        [turned, node_valid.reshape(slots, 1, SLOT)], "tiles",
    )


def combine(g_ref, columns):
    mref, first, second, count = (unpacked(g_ref, k, columns) for k in range(4))
    shift = first / count
    mean_each = mref + shift
    spread_each = second - first * shift
    total = jnp.sum(count, axis=0, keepdims=True)
    mean = jnp.sum(count * mean_each, axis=0, keepdims=True) / total
    away = mean_each - mean
    variance = jnp.sum(spread_each + count * away * away, axis=0, keepdims=True) / total
    return total, mean, lax.rsqrt(variance + EPSILON)


def small_gather(copies, axis):
    return lax.all_to_all(copies, axis, split_axis=0, concat_axis=0, tiled=True)


def copies_shape(columns, count):
    rows = count * columns // LANES
    return (lax.axis_size("row"), rows + -rows % 8, LANES)


def spread_rows(out_ref, rows):
    pieces = [row[:, j : j + LANES] for row in rows for j in range(0, row.shape[1], LANES)]
    if len(pieces) < out_ref.shape[1]:
        pieces.append(jnp.zeros((out_ref.shape[1] - len(pieces), LANES), F32))
    block = jnp.concatenate(pieces, axis=0)

    def one(n, carry):
        out_ref[n] = block
        return carry

    lax.fori_loop(0, out_ref.shape[0], one, 0)


def unpacked(ref, k, columns):
    per = columns // LANES
    return jnp.concatenate([ref[:, k * per + j, :] for j in range(per)], axis=1)


def split(value):
    high = value.astype(BF)
    return high, (value - high.astype(F32)).astype(BF)


def fold(value):
    return jnp.sum(value.reshape(value.shape[0] // 8, 8, value.shape[1]), axis=0)


def at(ref, k):
    return ref[k : k + 1, :]


def put(ref, k, value):
    ref[k : k + 1, :] = value


def half(ids, big, sources, weights, turned, name, tokens=(), early=None):
    nodes, depth = sources[0].shape
    columns = weights[0][0].shape[1]
    rows = big * SLOT
    n = len(sources)
    before = [] if early is None else [early]
    product = dot_t if turned else dot

    def kernel(ids_ref, *refs):
        out_ref, token_ref = refs[-2:]
        mark(token_ref)
        terms = [product(x_ref[...], w_ref[...]) for x_ref, w_ref in zip(refs[:n], refs[n : 2 * n])]
        terms += [e_ref[...] for e_ref in refs[2 * n : -2]]
        out_ref[...] = sum(terms[1:], terms[0])

    flat = pl.BlockSpec((rows, depth), lambda i, ids: (i, 0))
    wide_flat = pl.BlockSpec((rows, columns), lambda i, ids: (i, 0))
    return launch(
        kernel, (nodes // rows,), [flat] * n + [spec for _, spec in weights] + [wide_flat for _ in before],
        [wide_flat, token_spec()], [jax.ShapeDtypeStruct((nodes, columns), F32), TOKEN],
        [*sources, *[w for w, _ in weights], *before], name, prefetch=[ids], tokens=tokens,
    )


def weight_block(weight, b):
    depth = weight.shape[0] // 4
    return weight, pl.BlockSpec((depth, weight.shape[1]), lambda i, ids: (ids[b], 0))


def whole_block(piece):
    return piece, pl.BlockSpec(piece.shape, lambda i, ids: (0, 0))


def each_part(big, body, part=32):
    for s in range(big):
        for r in range(SLOT // part):
            body(s, slice(r * part, (r + 1) * part), slice(s * SLOT + r * part, s * SLOT + (r + 1) * part))


def split_three(value):
    high, rest = split(value)
    middle, low = split(value - high.astype(F32) - rest.astype(F32))
    return high, rest, middle


def coef_rows(ref, base):
    rows = ref[base : base + TAIL, :].astype(F32)
    return tuple(rows[k : k + 1] + rows[k + 1 : k + 2] + rows[k + 2 : k + 3] for k in (0, 3))


def receive(big, lead, i, lead_ref, rest_ref, val_ref, to_ref):
    columns = to_ref.shape[1]
    scale, shift = coef_rows(rest_ref, rest_ref.shape[0] - TAIL)
    for s in range(big):
        rows = slice(s * SLOT, (s + 1) * SLOT)
        if s < lead:

            @pl.when(i == 0)
            def _():
                to_ref[rows, :] = lead_ref[rows, :]

            @pl.when(i > 0)
            def _():
                to_ref[rows, :] = rest_ref[pl.ds(pl.multiple_of((i * big + s - lead) * SLOT, SLOT), SLOT), :]

        else:
            to_ref[rows, :] = rest_ref[pl.ds(pl.multiple_of((i * big + s - lead) * SLOT, SLOT), SLOT), :]

    def part(s, inner, rows):
        u = to_ref[rows, :].astype(F32) * scale + shift
        to_ref[rows, :] = (wide(val_ref[s, inner, :], columns) * (u + u * jnp.tanh(u))).astype(BF)

    each_part(big, part)


def far_kernel(big, lead, ids_ref, lead_ref, rest_ref, val_ref, w_ref, early_ref, out_ref, to_ref):
    receive(big, lead, pl.program_id(0), lead_ref, rest_ref, val_ref, to_ref)
    out_ref[...] = early_ref[...] + dot(to_ref[...], w_ref[...])


def far_half(ids, big, sent, weight, val, early, name, tokens=()):
    nodes, columns = early.shape
    block, spec = weight
    depth = block.shape[1] if spec.block_shape is None else spec.block_shape[0]
    rows = big * SLOT
    flat = pl.BlockSpec((rows, columns), lambda i, ids: (i, 0))
    to = pl.BlockSpec((rows, depth), lambda i, ids: (i, 0))
    return launch(
        functools.partial(far_kernel, big, sent[0].shape[0] // SLOT), (nodes // rows,),
        [
            *[pl.BlockSpec(x.shape, lambda i, ids: (0, 0)) for x in sent],
            pl.BlockSpec((big, SLOT, SLOT), lambda i, ids: (i, 0, 0)), spec, flat,
        ],
        [flat, to], [jax.ShapeDtypeStruct((nodes, columns), F32), jax.ShapeDtypeStruct((nodes, depth), BF)],
        [*sent, val, block, early], name, prefetch=[ids], tokens=tokens,
    )


def forward_kernel(big, lead, send, got, ids_ref, early_ref, *refs):
    if got:
        lead_ref, rest_ref, w_beyond, h_ref, inv_ref, val_ref, lin_ref, st_ref, y_ref, *refs = refs
        receive(big, lead, pl.program_id(0), lead_ref, rest_ref, val_ref, y_ref)
    else:
        y_ref, w_beyond, h_ref, inv_ref, val_ref, lin_ref, st_ref, *refs = refs
    token_ref, *refs = refs
    mark(token_ref)
    if send:
        lead_ref, rest_ref, *refs = refs
    tot_ref, acc_ref, ref_ref = refs
    forward_body(
        big, early_ref, y_ref, w_beyond, h_ref, inv_ref, val_ref, lin_ref, st_ref, tot_ref, acc_ref, ref_ref
    )
    if not send:
        return
    i = pl.program_id(0)
    mref = at(ref_ref, 0)
    for s in range(big):
        value = (lin_ref[s * SLOT : (s + 1) * SLOT, :] - mref).astype(BF)
        later = pl.ds(pl.multiple_of((i * big + s - lead) * SLOT, SLOT), SLOT)
        if s < lead:

            @pl.when(i == 0)
            def _():
                lead_ref[s * SLOT : (s + 1) * SLOT, :] = value

            @pl.when(i > 0)
            def _():
                rest_ref[later, :] = value

        else:
            rest_ref[later, :] = value


def forward_body(big, early_ref, y_ref, w_beyond, h_ref, inv_ref, val_ref, lin_ref, st_ref, tot_ref, acc_ref, ref_ref):
    i = pl.program_id(0)
    columns = lin_ref.shape[1]
    tot_ref[...] = early_ref[...] + dot(y_ref[...], w_beyond[...])

    def mixed(s):
        high, low = split(tot_ref[s * SLOT : (s + 1) * SLOT, :])
        return dot(h_ref[s], jnp.concatenate([high, low], axis=0)) * wide(inv_ref[s], columns)

    @pl.when(i == 0)
    def _():
        acc_ref[...] = jnp.zeros_like(acc_ref)
        v = val_ref[0]
        count = jnp.sum(v, axis=0, keepdims=True)
        put(ref_ref, 0, jnp.sum(mixed(0) * wide(v, columns), axis=0, keepdims=True) / wide(count, columns))

    mref = at(ref_ref, 0)
    for s in range(big):
        lin_ref[s * SLOT : (s + 1) * SLOT, :] = mixed(s)
        for r in range(SLOT // 32):
            v = val_ref[s, r * 32 : (r + 1) * 32, :]
            away = (lin_ref[s * SLOT + r * 32 : s * SLOT + (r + 1) * 32, :] - mref) * wide(v, columns)
            acc_ref[0] += fold(away)
            acc_ref[1] += fold(away * away)
            acc_ref[2, :, :LANES] += fold(v)

    @pl.when(i == pl.num_programs(0) - 1)
    def _():
        first, second = (jnp.sum(acc_ref[k], axis=0, keepdims=True) for k in range(2))
        count = wide(jnp.sum(acc_ref[2, :, :LANES], axis=0, keepdims=True), columns)
        spread_rows(st_ref, (at(ref_ref, 0), first, second, count))


def forward(ids, big, lead, early, beyond, weight, tiles, name, tokens=(), send=False):
    h, _, inv, val = tiles
    nodes, columns = early.shape
    depth = weight.shape[0] // 4
    rows = big * SLOT
    got = len(beyond) == 2
    flat = pl.BlockSpec((rows, columns), lambda i, ids: (i, 0))
    to = pl.BlockSpec((rows, depth), lambda i, ids: (i, 0))
    whole = lambda shape: pl.BlockSpec(shape, lambda i, ids: (0, 0))
    tile = pl.BlockSpec((big, SLOT, SLOT), lambda i, ids: (i, 0, 0))
    double = pl.BlockSpec((big, SLOT, 2 * SLOT), lambda i, ids: (i, 0, 0))
    _, block = weight_block(weight, 3)
    outs = [flat, pl.BlockSpec(copies_shape(columns, 4), lambda i, ids: (0, 0, 0))]
    shapes = [jax.ShapeDtypeStruct((nodes, columns), F32), jax.ShapeDtypeStruct(copies_shape(columns, 4), F32)]
    if got:
        outs.append(to)
        shapes.append(jax.ShapeDtypeStruct((nodes, depth), BF))
    outs.append(token_spec())
    shapes.append(TOKEN)
    if send:
        for r in (lead * SLOT, nodes - lead * SLOT + TAIL):
            outs.append(whole((r, columns)))
            shapes.append(jax.ShapeDtypeStruct((r, columns), BF))
    return launch(
        functools.partial(forward_kernel, big, lead, send, got), (nodes // rows,),
        [flat, *([whole(x.shape) for x in beyond] if got else [to]), block, double, tile, tile],
        outs, shapes, [early, *beyond, weight, h, inv, val], name, prefetch=[ids],
        scratch=[pltpu.VMEM((rows, columns), F32), pltpu.VMEM((3, 8, columns), F32), pltpu.VMEM((8, columns), F32)],
        tokens=tokens,
    )


def columns_of(g_ref, gamma_ref, beta_ref, co_ref):
    total, mean, inv_std = combine(g_ref, gamma_ref.shape[1])
    put(co_ref, 0, mean)
    put(co_ref, 1, 0.5 * gamma_ref[...] * inv_std)
    put(co_ref, 2, 0.5 * beta_ref[...])
    put(co_ref, 3, inv_std)
    put(co_ref, 4, total)


def silu_of(away, co_ref):
    u = away * at(co_ref, 1) + at(co_ref, 2)
    return u + u * jnp.tanh(u)


def double_slope(away, co_ref):
    u = away * at(co_ref, 1) + at(co_ref, 2)
    t = jnp.tanh(u)
    return (1.0 + t) * (1.0 + u * (1.0 - t))


def coefs_kernel(st_ref, g_ref, gamma_ref, beta_ref, rest_ref, out_ref, token_ref, co_ref):
    mark(token_ref)
    columns_of(g_ref, gamma_ref, beta_ref, co_ref)
    scale = at(co_ref, 1)
    reference = unpacked(st_ref, 0, scale.shape[1])
    shift = (reference - at(co_ref, 0)) * scale + at(co_ref, 2)
    rows = [*split_three(scale), *split_three(shift)]
    rows.append(jnp.zeros((TAIL - len(rows), scale.shape[1]), BF))
    out_ref[...] = jnp.concatenate([r.astype(F32) for r in rows], axis=0).astype(BF)


def with_coefs(rest, stats, norm, tokens):
    nodes, columns = rest.shape
    args = [stats, *norm, rest]
    return pl.pallas_call(
        lambda *refs: coefs_kernel(*refs[: len(args)], *refs[len(args) + len(tokens) :]),
        grid=(1,),
        in_specs=[pl.BlockSpec((1,) + stats.shape[1:], lambda i: (0, 0, 0))]
        + [pl.BlockSpec(v.shape, lambda i, n=v.ndim: (0,) * n) for v in norm]
        + [pl.BlockSpec(memory_space=pl.ANY)] * (1 + len(tokens)),
        out_specs=[pl.BlockSpec((TAIL, columns), lambda i: (nodes // TAIL - 1, 0)), token_spec()],
        out_shape=[jax.ShapeDtypeStruct((nodes, columns), BF), TOKEN],
        scratch_shapes=[pltpu.VMEM((8, columns), F32)],
        input_output_aliases={len(args) - 1: 0},
        compiler_params=params(24),
        cost_estimate=SMALL,
        name="coefs",
    )(*args, *tokens)


def result_kernel(big, lin_ref, val_ref, g_ref, gamma_ref, beta_ref, out_ref, token_ref, co_ref):
    mark(token_ref)

    @pl.when(pl.program_id(0) == 0)
    def _():
        columns_of(g_ref, gamma_ref, beta_ref, co_ref)

    def part(s, inner, rows):
        value = silu_of(lin_ref[rows, :] - at(co_ref, 0), co_ref)
        out_ref[rows, :] = (wide(val_ref[s, inner, :], lin_ref.shape[1]) * value).astype(out_ref.dtype)

    each_part(big, part)


def sums_kernel(big, lin_ref, cot_ref, val_ref, g_ref, gamma_ref, beta_ref, st_ref, co_ref, acc_ref):
    @pl.when(pl.program_id(0) == 0)
    def _():
        columns_of(g_ref, gamma_ref, beta_ref, co_ref)
        acc_ref[...] = jnp.zeros_like(acc_ref)

    def part(s, inner, rows):
        away = lin_ref[rows, :] - at(co_ref, 0)
        valid = wide(val_ref[s, inner, :], lin_ref.shape[1])
        grad = cot_ref[rows, :].astype(F32) * valid * double_slope(away, co_ref)
        acc_ref[0] += fold(grad)
        acc_ref[1] += fold(grad * away)

    each_part(big, part)
    finish_sums(st_ref, co_ref, acc_ref)


def finish_sums(st_ref, co_ref, acc_ref):
    @pl.when(pl.program_id(0) == pl.num_programs(0) - 1)
    def _():
        grad_beta = 0.5 * jnp.sum(acc_ref[0], axis=0, keepdims=True)
        grad_gamma = 0.5 * at(co_ref, 3) * jnp.sum(acc_ref[1], axis=0, keepdims=True)
        spread_rows(st_ref, (grad_beta, grad_gamma))


def turn_kernel(from_cot, big, lin_ref, grad_ref, inv_ref, ht_ref, g_ref, sg_ref, gamma_ref, beta_ref, out_ref, token_ref, co_ref, lg_ref):
    mark(token_ref)

    @pl.when(pl.program_id(0) == 0)
    def _():
        columns_of(g_ref, gamma_ref, beta_ref, co_ref)
        twice = 2.0 / at(co_ref, 4)
        put(co_ref, 5, twice * jnp.sum(unpacked(sg_ref, 0, lin_ref.shape[1]), axis=0, keepdims=True))
        put(co_ref, 6, twice * at(co_ref, 3) * jnp.sum(unpacked(sg_ref, 1, lin_ref.shape[1]), axis=0, keepdims=True))

    columns = lin_ref.shape[1]

    for s in range(big):
        for r in range(SLOT // PART):
            inner = slice(r * PART, (r + 1) * PART)
            rows = slice(s * SLOT + r * PART, s * SLOT + (r + 1) * PART)
            away = lin_ref[rows, :] - at(co_ref, 0)
            if from_cot:
                grad = grad_ref[rows, :].astype(F32) * double_slope(away, co_ref)
            else:
                grad = grad_ref[rows, :]
            weight = wide(inv_ref[s, inner, :], columns)
            lg_ref[s, inner, :] = (weight * (grad - (at(co_ref, 5) + away * at(co_ref, 6)))).astype(BF)
        out_ref[s * SLOT : (s + 1) * SLOT, :] = (dot(ht_ref[s], lg_ref[s]) * at(co_ref, 1)).astype(BF)


def rows_call(kernel, big, arrays, tiles, smalls, out_dtype, scratch, name, tokens=(), limit=24):
    rows = big * SLOT
    nodes, columns = arrays[0].shape
    flat = pl.BlockSpec((rows, columns), lambda i: (i, 0))
    ins = [flat for _ in arrays]
    ins += [pl.BlockSpec((big,) + t.shape[1:], lambda i: (i, 0, 0)) for t in tiles]
    ins += [pl.BlockSpec(s.shape, lambda i, n=s.ndim: (0,) * n) for s in smalls]
    if out_dtype is None:
        out_spec = pl.BlockSpec(copies_shape(columns, 2), lambda i: (0, 0, 0))
        out_shape = jax.ShapeDtypeStruct(copies_shape(columns, 2), F32)
    else:
        out_spec = [flat, token_spec()]
        out_shape = [jax.ShapeDtypeStruct((nodes, columns), out_dtype), TOKEN]
    return launch(
        functools.partial(kernel, big), (nodes // rows,), ins, out_spec, out_shape, [*arrays, *tiles, *smalls], name,
        scratch=[pltpu.VMEM((8, columns), F32)] + scratch, tokens=tokens, limit=limit,
    )


def turn_call(from_cot, big, lin, grad, tiles, norm, sums, name, tokens=()):
    _, ht, inv, _ = tiles
    return rows_call(
        functools.partial(turn_kernel, from_cot), big, [lin, grad], [inv, ht], [norm[0], sums, *norm[1:]], BF,
        [pltpu.VMEM((big, SLOT, lin.shape[1]), BF)], name, tokens, 60,
    )


def backward_kernel(big, last, early_ref, y_ref, w_beyond, *refs):
    total = early_ref[...] + dot_t(y_ref[...], w_beyond[...])
    if last:
        refs[-2][...] = total
        mark(refs[-1])
        return
    lin_ref, g_ref, gamma_ref, beta_ref, out_ref, st_ref, co_ref, acc_ref = refs
    out_ref[...] = total

    @pl.when(pl.program_id(0) == 0)
    def _():
        columns_of(g_ref, gamma_ref, beta_ref, co_ref)
        acc_ref[...] = jnp.zeros_like(acc_ref)

    def part(s, inner, rows):
        away = lin_ref[rows, :] - at(co_ref, 0)
        grad = out_ref[rows, :] * double_slope(away, co_ref)
        out_ref[rows, :] = grad
        acc_ref[0] += fold(grad)
        acc_ref[1] += fold(grad * away)

    each_part(big, part)
    finish_sums(st_ref, co_ref, acc_ref)


def backward(big, early, beyond, piece, lin, norm, name, tokens=()):
    nodes, columns = early.shape
    rows = big * SLOT
    last = norm is None
    flat = pl.BlockSpec((rows, columns), lambda i: (i, 0))
    fixed = lambda s: pl.BlockSpec(s.shape, lambda i, n=s.ndim: (0,) * n)
    ins = [flat, flat, fixed(piece)]
    args = [early, beyond, piece]
    out_specs = [flat]
    out_shape = [jax.ShapeDtypeStruct((nodes, columns), F32)]
    scratch = []
    if last:
        out_specs.append(token_spec())
        out_shape.append(TOKEN)
    else:
        ins += [flat, *map(fixed, norm)]
        args += [lin, *norm]
        out_specs.append(pl.BlockSpec(copies_shape(columns, 2), lambda i: (0, 0, 0)))
        out_shape.append(jax.ShapeDtypeStruct(copies_shape(columns, 2), F32))
        scratch = [pltpu.VMEM((8, columns), F32), pltpu.VMEM((2, 8, columns), F32)]
    return launch(
        functools.partial(backward_kernel, big, last), (nodes // rows,), ins, out_specs, out_shape, args, name,
        scratch=scratch, tokens=tokens,
    )


def weight_kernel(spans, other, meta_ref, *refs):
    sources, h_hbm, outs, (token_ref, buf_ref, h_ref, sem) = refs[:4], refs[4], refs[5:7], refs[7:]
    mark(token_ref)
    for m in range(2):
        for n, span in enumerate(spans):
            rows = pl.ds(*span)
            if m == 0:
                pltpu.make_async_copy(h_hbm.at[rows, :], h_ref.at[rows, :], sem.at[2, n]).start()
            for k in range(2):

                @pl.when((meta_ref[4 + m] ^ other) == k)
                def _():
                    pltpu.make_async_copy(
                        sources[2 * m + k].at[rows, :], buf_ref.at[m, rows, :], sem.at[m, n]
                    ).start()

    for m in range(2):
        total = None
        for n, (start, size) in enumerate(spans):
            rows = pl.ds(start, size)
            if m == 0:
                pltpu.make_async_copy(h_hbm.at[rows, :], h_ref.at[rows, :], sem.at[2, n]).wait()
            pltpu.make_async_copy(sources[2 * m].at[rows, :], buf_ref.at[m, rows, :], sem.at[m, n]).wait()
            x, h = buf_ref[m, start : start + size, :], h_ref[start : start + size, :]
            term = lax.dot_general(x, h, (((0,), (0,)), ((), ())), preferred_element_type=F32)
            total = term if total is None else total + term
        outs[m][...] = total.astype(outs[m].dtype)


def weight_terms(meta, other, pairs, h, name, tokens=()):
    nodes, depth = pairs[0][0].shape
    columns = h.shape[1]
    pieces = 2 if nodes % 32 == 0 else 1
    spans = tuple((n * (nodes // pieces), nodes // pieces) for n in range(pieces))
    whole = pl.BlockSpec((depth, columns), lambda i, meta: (0, 0))
    return launch(
        functools.partial(weight_kernel, spans, other), (1,), [pl.BlockSpec(memory_space=pl.ANY)] * 5,
        [whole, whole, token_spec()],
        [jax.ShapeDtypeStruct((depth, columns), BF)] * 2 + [TOKEN], [*pairs[0], *pairs[1], h], name, prefetch=[meta],
        scratch=[
            pltpu.VMEM((2, nodes, depth), BF), pltpu.VMEM((nodes, columns), BF), pltpu.SemaphoreType.DMA((3, pieces))
        ],
        tokens=tokens, limit=60,
    )


def place_kernel(orders, meta_ref, *refs):
    out_ref, token_ref = refs[-2:]
    mark(token_ref)
    pieces = 1 << (len(orders[0]) - 2)
    size = out_ref.shape[0] // pieces
    for k in range(4):

        @pl.when(pl.program_id(0) == k)
        def _():
            mask = 0
            for b in orders[k // 2][1:-1]:
                mask = 2 * mask + meta_ref[4 + b]
            for n in range(pieces):
                start = pl.multiple_of((mask ^ n) * size, size)
                out_ref[pl.ds(start, size), :] = refs[k][n * size : (n + 1) * size, :].astype(F32)


def place_blocks(meta, blocks, orders, name, limit, tokens):
    depth, columns = blocks[0].shape
    return launch(
        functools.partial(place_kernel, orders), (4,), [pl.BlockSpec((depth, columns), lambda i, meta: (0, 0))] * 4,
        [
            pl.BlockSpec((depth, columns), lambda i, meta: (meta[0] ^ (i // 2 * 2) ^ (i % 2) ^ meta[4 + i // 2], 0)),
            token_spec(),
        ],
        [jax.ShapeDtypeStruct((4 * depth, columns), F32), TOKEN], blocks, name, prefetch=[meta], limit=limit,
        tokens=tokens,
    )


def after(value, *tokens):
    value, tokens = lax.optimization_barrier((value, tokens))
    return value, tokens


def across(value, axis, distance):
    size = lax.axis_size(axis)
    return lax.ppermute(value, axis, [(i, i ^ distance) for i in range(size)])


def slices_kernel(ids_ref, one_ref, two_ref, *refs):
    outs, (token_ref, sem) = refs[:6], refs[6:]
    mark(token_ref)
    depth = outs[0].shape[0]
    copies = []
    for n, out_ref in enumerate(outs):
        start = pl.multiple_of(ids_ref[1 + n % 3] * depth, depth)
        source = (one_ref, two_ref)[n // 3].at[pl.ds(start, depth), :]
        copies.append(pltpu.make_async_copy(source, out_ref, sem.at[n]))
    for copy in copies:
        copy.start()
    for copy in copies:
        copy.wait()


def weight_slices(ids, one, two):
    depth, columns = one.shape[0] // 4, one.shape[1]
    hbm = pl.BlockSpec(memory_space=pltpu.HBM)
    outs = launch(
        slices_kernel, (1,), [hbm, hbm], [hbm] * 6 + [token_spec()],
        [jax.ShapeDtypeStruct((depth, columns), one.dtype)] * 6 + [TOKEN], [one, two], "weight_slices",
        prefetch=[ids], scratch=[pltpu.SemaphoreType.DMA((6,))],
    )
    return outs[:3], outs[3:6], outs[6]


def weight_rows(slices):
    far = across(slices[1], "col", 2)
    other = across(slices[2], "col", 2)
    return [across(slices[0], "col", 1), far, across(other, "col", 1)], (far, other)


def fold_kernel(last, place, meta_ref, keep_ref, got_ref, *refs):
    mark(refs[-1])
    if last:
        refs[0][...] = (keep_ref[...].astype(F32) + got_ref[...].astype(F32)).astype(BF)
        return
    part = refs[0].shape[0]
    bit = meta_ref[4 + place]
    for out_ref, which in zip(refs[:2], (1 - bit, bit)):
        rows = pl.ds(pl.multiple_of(which * part, part), part)
        out_ref[...] = (keep_ref[rows, :].astype(F32) + got_ref[rows, :].astype(F32)).astype(BF)


def join_kernel(meta_ref, keep_ref, got_ref, out_ref, token_ref):
    mark(token_ref)
    part = keep_ref.shape[0]
    out_ref[:part, :] = keep_ref[...]
    out_ref[part:, :] = got_ref[...]


def small_call(kernel, meta, keep, got, rows, name, tokens):
    columns = keep.shape[1]
    whole = lambda r: pl.BlockSpec((r, columns), lambda i, bit: (0, 0))
    return launch(
        kernel, (1,), [whole(keep.shape[0])] * 2, [whole(r) for r in rows] + [token_spec()],
        [jax.ShapeDtypeStruct((r, columns), BF) for r in rows] + [TOKEN], [keep, got], name, prefetch=[meta], tokens=tokens,
    )


class RowSum:
    def __init__(self, axis, meta, terms, name, between=tuple):
        self.axis, self.meta, self.name = axis, meta, name
        self.bits = lax.axis_size(axis).bit_length() - 1
        self.stages = 2 * self.bits - 1
        self.orders = [list(range(self.bits)), list(range(1, self.bits)) + [0]]
        *self.send, self.sent = terms(1, ())
        *self.keep, self.kept = terms(0, (self.sent, *between()))
        self.done = [0, 0]
        self.got = [None, None]
        self.step(())

    def advance(self, n, *tokens):
        s, last = self.done[n], self.bits - 1
        if s == self.stages:
            return tokens
        self.done[n] += 1
        started = ()
        rows = self.keep[n].shape[0]
        call = lambda kernel, sizes: small_call(
            kernel, self.meta, self.keep[n], self.got[n], sizes, f"{self.name}_{n}_{s}", tokens
        )
        if 0 < s < last:
            fold = functools.partial(fold_kernel, False, self.orders[n][s])
            self.send[n], self.keep[n], *started = call(fold, [rows // 2] * 2)
        elif s == last or s == last + 1:
            self.keep[n], *started = call(functools.partial(fold_kernel, True, 0), [rows])
        elif s > last + 1:
            self.keep[n], *started = call(join_kernel, [2 * rows])
        level = s if s <= last else 2 * last - s
        moved = self.send if s < last else self.keep
        self.got[n] = across(moved[n], self.axis, 1 << self.orders[n][level])
        return tuple(started)

    def step(self, tokens):
        return (*self.advance(0, *tokens), *self.advance(1, *tokens))

    def next(self, *tokens):
        return self.step(tokens) if min(self.done) < self.stages else tokens

    def placed(self, limit, tokens=()):
        while min(self.done) < self.stages:
            self.step(())
        blocks = [v for n in range(2) for v in (self.keep[n], self.got[n])]
        return place_blocks(self.meta, blocks, self.orders, f"place_{self.name}", limit, tokens)


def local(
    features,
    neighbours,
    node_valid,
    weight_one,
    gamma_one,
    beta_one,
    weight_two,
    gamma_two,
    beta_two,
    cotangent,
):
    nodes, columns = features.shape
    slots = nodes // SLOT
    big = slots // 2 if slots % 2 == 0 else slots
    lead = max(1, min(big, 5 * slots // 14))
    q = lax.axis_index("col")
    place = lax.axis_index("row")
    bits = [(place >> b) & 1 for b in range(lax.axis_size("row").bit_length() - 1)]
    ids = jnp.stack([q, q ^ 1, q ^ 2, q ^ 3, *bits]).astype(jnp.int32)
    g1, b1, g2, b2 = (v.reshape(1, columns) for v in (gamma_one, beta_one, gamma_two, beta_two))

    far_one = across(features, "col", 2)
    near_one = across(features, "col", 1)
    *tiles, tiles_token = build_tiles(neighbours, node_valid)
    val = tiles[3]
    slices_one, slices_two, slices_token = weight_slices(ids, weight_one, weight_two)
    early, token = half(ids, big, [features, near_one], [weight_block(weight_one, b) for b in (0, 1)], False, "half_one")
    far_one, tokens = after(far_one, token, tiles_token, slices_token)
    beyond_one = across(far_one, "col", 1)
    early, _ = half(ids, big, [far_one], [weight_block(weight_one, 2)], False, "far_half_one", tokens, early)
    lin_one, stats, _, sent, rest = forward(ids, big, lead, early, [beyond_one], weight_one, tiles, "forward_one", tokens, send=True)

    far_lead = across(sent, "col", 2)
    norm_one = (small_gather(stats, "row"), g1, b1)
    rest, token = with_coefs(rest, stats, norm_one, (far_lead,))
    far_rest = across(rest, "col", 2)
    hidden, _ = rows_call(result_kernel, big, [lin_one], [val], norm_one, BF, [], "hidden", (token,))
    near_two = across(hidden, "col", 1)
    early, token = half(
        ids, big, [hidden, near_two], [weight_block(weight_two, b) for b in (0, 1)], False, "half_two"
    )
    far_rest, tokens = after(far_rest, token)
    beyond_two = [across(x, "col", 1) for x in (far_lead, far_rest)]
    early, far_two = far_half(
        ids, big, (far_lead, far_rest), weight_block(weight_two, 2), val, early, "far_half_two", tokens
    )
    lin_two, stats, beyond_two, token = forward(ids, big, lead, early, beyond_two, weight_two, tiles, "forward_two")
    norm_two = (small_gather(stats, "row"), g2, b2)
    slices_two, tokens = after(slices_two, token)
    rows_two, crossing = weight_rows(slices_two)

    sums = rows_call(
        sums_kernel, big, [lin_two, cotangent], [val], norm_two, None, [pltpu.VMEM((2, 8, columns), F32)], "sums_two", tokens
    )
    grads_two = small_gather(sums, "row")
    turned, _ = turn_call(True, big, lin_two, cotangent, tiles, norm_two, grads_two, "turn_two", crossing)
    far, near = across(turned, "col", 2), across(turned, "col", 1)

    def terms_two(other, tokens, h=turned):
        return weight_terms(ids, other, ((hidden, near_two), (far_two, beyond_two)), h, "terms_two", tokens)

    sum_two = RowSum("row", ids, terms_two, "two")
    weights = [weight_block(weight_two, 0), whole_block(rows_two[0])]
    early, token = half(ids, big, [turned, near], weights, True, "half_back_two", (sum_two.kept,))
    far, tokens = after(far, *sum_two.next(*sum_two.next(token)))
    beyond = across(far, "col", 1)
    slices_one, (far,) = after(slices_one, far)
    rows_one, crossing = weight_rows(slices_one)
    early, _ = half(ids, big, [far], [whole_block(rows_two[1])], True, "far_half_back_two", tokens, early)
    grad_one, sums = backward(big, early, beyond, rows_two[2], lin_one, norm_one, "backward_two", tokens)
    tokens = (crossing[1], *sum_two.next(sums))
    grads_one = small_gather(sums, "row")

    turned, _ = turn_call(False, big, lin_one, grad_one, tiles, norm_one, grads_one, "turn_one", tokens)
    far, near = across(turned, "col", 2), across(turned, "col", 1)

    def terms_one(other, tokens, h=turned):
        return weight_terms(ids, other, ((features, near_one), (far_one, beyond_one)), h, "terms_one", tokens)

    sum_one = RowSum("row", ids, terms_one, "one", lambda: sum_two.next())
    weights = [weight_block(weight_one, 0), whole_block(rows_one[0])]
    early, token = half(ids, big, [turned, near], weights, True, "half_back_one", sum_one.next())
    output, token = rows_call(result_kernel, big, [lin_two], [val], norm_two, F32, [], "output", (token,))
    started = sum_one.next(token)
    far, tokens = after(far, *started)
    beyond = across(far, "col", 1)
    tokens = (*tokens, *sum_one.next())
    early, _ = half(ids, big, [far], [whole_block(rows_one[1])], True, "far_half_back_one", (*tokens, sum_two.got[1]), early)
    grad_features, token = backward(big, early, beyond, rows_one[2], None, None, "backward_one", tokens)
    while min(sum_one.done) < sum_one.stages - 1:
        sum_one.next()
    tokens = sum_one.next(token)
    grad_weight_two, _ = sum_two.placed(60, tokens)
    grad_weight_one, _ = sum_one.placed(24)

    per = columns // LANES
    sums_one, sums_two = (jnp.sum(g, axis=0)[: 2 * per].reshape(2, columns) for g in (grads_one, grads_two))
    return (
        output,
        grad_features,
        grad_weight_one,
        sums_one[1],
        sums_one[0],
        grad_weight_two,
        sums_two[1],
        sums_two[0],
    )


def solution(mesh):
    placed = (
        P("row", "col"),
        P("row", None),
        P("row"),
        P(None, "col"),
        P("col"),
        P("col"),
        P(None, "col"),
        P("col"),
        P("col"),
        P("row", "col"),
    )
    return jax.shard_map(
        local,
        mesh=mesh,
        in_specs=placed,
        out_specs=(
            P("row", "col"),
            P("row", "col"),
            P(None, "col"),
            P("col"),
            P("col"),
            P(None, "col"),
            P("col"),
            P("col"),
        ),
        check_vma=False,
    )
```
